32 devices in a mesh: ctx: 16 (over z, y, x), head: 2 (over core).
Axes of the slice: x: 2, y: 2, z: 4, core: 2. Of those that a mesh axis runs over, the one named last changes fastest.
Arguments:
- queries: bfloat16 [2048, 32, 128], P('ctx', 'head'), may hold values from -190 to 190
- keys: bfloat16 [2048, 8, 128], P('ctx', 'head'), may hold values from -6.2 to 6.2
- values: bfloat16 [2048, 8, 128], P('ctx', 'head'), may hold values from -16 to 16
- feature_weight: float32 [32, 128, 128], P('head'), may hold values from -0.5 to 0.5
Outputs:
- student: bfloat16 [2048, 32, 128], P('ctx', 'head')
- update: float32 [32, 128, 128], P('head')
The draws below stay inside these ranges and needn't reach their ends.
All inputs are finite; a program needn't handle non-finite values.
Results may differ from the reference program's by a relative error of at most 0.003.
The reference program's roundings to bfloat16 on the way count: a program that leaves them out, or rounds other values in their place, can miss the bound.
Values may be sent and summed in bfloat16 or wider, within the bound.
A program may use at most 64 MiB of HBM per device.

```python
import math
import jax
import jax.numpy as jnp
from jax import lax

HQ = 32
KVH = 8
DH = 128
DF = 64
TOK_DEV = 128
SEQ = 2048


def draw_pair(key):
    query_seed = jax.random.fold_in(key, 101)
    key_seed = jax.random.fold_in(key, 102)
    key_rows = jnp.clip(jax.random.normal(key_seed, (SEQ, KVH, DH), jnp.float32), -6.0, 6.0)
    query_rows = 1.5 * jnp.clip(jax.random.normal(query_seed, (SEQ, HQ, DH), jnp.float32), -6.0, 6.0)
    return (query_rows, key_rows)


def draw_queries(key, part):
    return draw_pair(key)[0].astype(jnp.bfloat16)


def draw_keys(key, part):
    return draw_pair(key)[1].astype(jnp.bfloat16)


def draw_values(key, part):
    noise_seed = jax.random.fold_in(key, 201)
    ladder = jnp.arange(KVH, dtype=jnp.float32) / max(KVH - 1, 1)
    noise = jnp.clip(jax.random.normal(noise_seed, (SEQ, KVH, DH), jnp.float32), -4.0, 4.0)
    head_scale = 1.0 + 2.0 * ladder
    return (noise * head_scale[None, :, None]).astype(jnp.bfloat16)


def shard_levels(rng, shape, split, smallest, high):
    factor_of, own = 1.0, jax.random.fold_in(rng, 6)
    for dim, blocks in split:
        steps = jnp.exp(jax.random.uniform(jax.random.fold_in(own, dim), (blocks,), jnp.float32, smallest / len(split), high / len(split)))
        factor_of = factor_of * jnp.repeat(steps, shape[dim] // blocks).reshape([-1 if axis == dim else 1 for axis in range(len(shape))])
    return factor_of


def bell_draw(own_key, shape, deviation, reach, shards=(), kind=jnp.bfloat16):
    loudness = shard_levels(own_key, shape, shards, -0.22, 0.18) if shards else 1.0
    drawn = jax.random.normal(own_key, shape, jnp.float32) * deviation * loudness
    return jnp.minimum(jnp.maximum(drawn, -reach), reach).astype(kind)


def setup_inputs(seed: int = 0) -> dict:
    key_of = jax.random.split(jax.random.key(seed), 5)
    return {
        "queries": draw_queries(jax.random.fold_in(key_of[4], 71), 0),
        "keys": draw_keys(jax.random.fold_in(key_of[4], 71), 0),
        "values": draw_values(jax.random.fold_in(key_of[4], 71), 0),
        "feature_weight": bell_draw(key_of[3], (HQ, DH, 2 * DF), DH ** -0.5, 0.5, ((0, 2),), jnp.float32),
    }


def feature_map(projection):
    return jnp.concatenate([jax.nn.softmax(projection, axis=-1), jax.nn.softmax(-projection, axis=-1)], axis=-1)

def teacher_head(query, key_rows, value_rows):
    count = query.shape[0]
    scores = jnp.dot(query, key_rows.T, preferred_element_type=jnp.float32) / math.sqrt(DH)
    position = jnp.arange(count, dtype=jnp.int32)
    allowed = position[None, :] <= position[:, None]
    scores = jnp.where(allowed, scores, -1e+30)
    row_max = lax.optimization_barrier(jnp.max(scores, axis=-1, keepdims=True))
    attn_weight = jnp.where(allowed, jnp.exp(scores - row_max), 0.0)
    running_sum = lax.optimization_barrier(jnp.sum(attn_weight, axis=-1, keepdims=True))
    mixed = jnp.dot(attn_weight.astype(jnp.bfloat16), value_rows, preferred_element_type=jnp.float32)
    return mixed / running_sum

def student_head(query, key_rows, value_rows, weight):
    blocks = query.shape[0] // TOK_DEV
    query_blocks = query.reshape(blocks, TOK_DEV, DH).astype(jnp.float32)
    key_blocks = key_rows.reshape(blocks, TOK_DEV, DH)
    value_blocks = value_rows.reshape(blocks, TOK_DEV, DH)
    key_before = jnp.concatenate([jnp.zeros_like(key_blocks[:1]), key_blocks[:-1]], axis=0)
    value_before = jnp.concatenate([jnp.zeros_like(value_blocks[:1]), value_blocks[:-1]], axis=0)
    window_keys = jnp.concatenate([key_before, key_blocks], axis=1).astype(jnp.float32)
    window_values = jnp.concatenate([value_before, value_blocks], axis=1).astype(jnp.float32)
    scores = jnp.einsum('btd,bsd->bts', query_blocks, window_keys) / math.sqrt(DH)
    row_index = jnp.arange(TOK_DEV, dtype=jnp.int32)
    column = jnp.arange(2 * TOK_DEV, dtype=jnp.int32)
    block_ids = jnp.arange(blocks, dtype=jnp.int32)
    earlier = (column[None, None, :] < TOK_DEV) & (block_ids[:, None, None] > 0)
    inside = (column[None, None, :] >= TOK_DEV) & (column[None, None, :] - TOK_DEV <= row_index[None, :, None])
    allowed = earlier | inside
    scores = jnp.where(allowed, scores, -1e+30)
    row_max = lax.optimization_barrier(jnp.max(scores, axis=-1))
    window_weight = jnp.where(allowed, jnp.exp(scores - row_max[..., None]), 0.0)
    window_den = lax.optimization_barrier(jnp.sum(window_weight, axis=-1))
    rounded = lax.optimization_barrier(window_weight.astype(jnp.bfloat16))
    window_num = jnp.einsum('bts,bsd->btd', rounded.astype(jnp.float32), window_values)
    query_feat = feature_map(jnp.dot(query.astype(jnp.float32), weight[:, :DF], precision=lax.Precision.HIGHEST))
    query_feat = query_feat.reshape(blocks, TOK_DEV, 2 * DF)
    key_feat = feature_map(jnp.dot(key_rows.astype(jnp.float32), weight[:, DF:], precision=lax.Precision.HIGHEST))
    key_feat = key_feat.reshape(blocks, TOK_DEV, 2 * DF)
    own_state = jnp.einsum('btf,btd->bfd', key_feat, value_blocks.astype(jnp.float32), precision=lax.Precision.HIGHEST)
    own_norm = lax.optimization_barrier(jnp.sum(key_feat, axis=1))
    run_state = jnp.cumsum(own_state, axis=0)
    run_norm = jnp.cumsum(own_norm, axis=0)
    state = jnp.concatenate([jnp.zeros_like(run_state[:2]), run_state[:-2]], axis=0)
    norm = jnp.concatenate([jnp.zeros_like(run_norm[:2]), run_norm[:-2]], axis=0)
    decay = jnp.exp(-row_max)
    far_num = decay[..., None] * jnp.einsum('btf,bfd->btd', query_feat, state, precision=lax.Precision.HIGHEST)
    far_den = decay * jnp.einsum('btf,bf->bt', query_feat, norm, precision=lax.Precision.HIGHEST)
    mix = (window_num + far_num) / (window_den + far_den)[..., None]
    return mix.reshape(blocks * TOK_DEV, DH)

def reference(queries, keys, values, feature_weight):
    group_size = HQ // KVH

    def per_head(head_id):
        kv_id = head_id // group_size
        query = lax.dynamic_index_in_dim(queries, head_id, 1, keepdims=False)
        key_rows = lax.dynamic_index_in_dim(keys, kv_id, 1, keepdims=False)
        value_rows = lax.dynamic_index_in_dim(values, kv_id, 1, keepdims=False)
        weight = lax.dynamic_index_in_dim(feature_weight, head_id, 0, keepdims=False)
        teacher = teacher_head(query, key_rows, value_rows)

        def student_of(weight_in):
            return student_head(query, key_rows, value_rows, weight_in)
        mix, pull_back = jax.vjp(student_of, weight)
        gradient = pull_back(mix - teacher)[0]
        return (mix.astype(jnp.bfloat16), gradient)
    mixes, gradients = lax.map(per_head, jnp.arange(HQ, dtype=jnp.int32))
    student = jnp.transpose(mixes, (1, 0, 2))
    update = gradients / jnp.sqrt(jnp.mean(gradients * gradients) + 1e-06)
    return (student, update)
```

```python
import functools
import math

import jax
import jax.numpy as jnp
from jax import lax
from jax.experimental import pallas as pl
from jax.experimental.pallas import tpu as pltpu
from jax.sharding import PartitionSpec as P

precise = lax.Precision.HIGHEST
big_negative = -1e30


def shifted(shard, axis, by):
    devices = lax.axis_size(axis)
    pairs = [(i, i + by) for i in range(devices) if 0 <= i + by < devices]
    return lax.ppermute(shard, axis, pairs)


def carried_in(part, axis, combine, identity):
    count = lax.axis_size(axis)
    place = lax.axis_index(axis)
    ahead = count - 1 - place
    gathered = jax.tree.map(lambda a: lax.all_gather(a, axis), part)
    state = jax.tree.map(lambda a, e: jnp.zeros_like(a) + jnp.asarray(e, a.dtype), part, identity)

    def one(step, state):
        source = count - 1 - step
        return combine(
            state, jax.tree.map(lambda a: lax.dynamic_index_in_dim(a, source, 0, False), gathered)
        )

    return lax.fori_loop(0, ahead, one, state)


def feature_map(projection):
    return jnp.concatenate(
        [jax.nn.softmax(projection, axis=-1), jax.nn.softmax(-projection, axis=-1)], axis=-1
    )


def feature_pull(projection, upstream):
    half_len = upstream.shape[-1] // 2
    upper = jax.nn.softmax(projection, axis=-1)
    lower = jax.nn.softmax(-projection, axis=-1)
    grad_upper = upstream[..., :half_len]
    grad_lower = upstream[..., half_len:]
    upper_part = upper * (grad_upper - jnp.sum(upper * grad_upper, axis=-1, keepdims=True))
    lower_part = lower * (grad_lower - jnp.sum(lower * grad_lower, axis=-1, keepdims=True))
    return upper_part - lower_part


def add_pair(earlier, later):
    return (earlier[0] + later[0], earlier[1] + later[1])


def skip_block(carry_in):
    return carry_in


def general_shards(queries, keys, values, feature_weight):
    block_len, head_count, head_width = queries.shape
    kv_count = keys.shape[1]
    group_size = head_count // kv_count
    feature_len = feature_weight.shape[2] // 2
    my_block = lax.axis_index("ctx")
    score_scale = 1.0 / math.sqrt(head_width)
    grouped_q = queries.reshape(block_len, kv_count, group_size, head_width)
    maps_weight = feature_weight.reshape(kv_count, group_size, head_width, 2 * feature_len)
    query_map = maps_weight[..., :feature_len]
    key_map = maps_weight[..., feature_len:]
    query_pos = my_block * block_len + jnp.arange(block_len, dtype=jnp.int32)
    prev_start = (my_block - 1) * block_len
    last_row = my_block * block_len + block_len - 1
    initial = [
        jnp.full((kv_count, group_size, block_len), big_negative, jnp.float32),
        jnp.zeros((kv_count, group_size, block_len), jnp.float32),
        jnp.zeros((kv_count, group_size, block_len, head_width), jnp.float32),
    ]
    initial = initial + [
        jnp.zeros((kv_count, group_size, 2 * feature_len, head_width), jnp.float32),
        jnp.zeros((kv_count, group_size, 2 * feature_len), jnp.float32),
    ]
    initial = tuple(initial)
    piece_keys = lax.all_gather(keys, "ctx", axis=0, tiled=True)
    piece_values = lax.all_gather(values, "ctx", axis=0, tiled=True)
    piece_rows = piece_keys.shape[0]
    step_rows = math.gcd(piece_rows, 512)

    def attend(step_index, running):
        first_row = step_index * step_rows
        block_keys = lax.dynamic_slice_in_dim(piece_keys, step_index * step_rows, step_rows, 0)
        block_values = lax.dynamic_slice_in_dim(piece_values, step_index * step_rows, step_rows, 0)
        key_pos = first_row + jnp.arange(step_rows, dtype=jnp.int32)

        def compute(carry_in):
            row_max, running_sum, accumulated = (carry_in[0], carry_in[1], carry_in[2])
            scores = (
                jnp.einsum(
                    "tkgd,skd->kgts", grouped_q, block_keys, preferred_element_type=jnp.float32
                )
                * score_scale
            )
            allowed = key_pos[None, :] <= query_pos[:, None]
            scores = jnp.where(allowed, scores, big_negative)
            new_max = jnp.maximum(row_max, jnp.max(scores, axis=-1))
            attn_weight = jnp.where(allowed, jnp.exp(scores - new_max[..., None]), 0.0)
            factor = jnp.exp(row_max - new_max)
            running_sum = running_sum * factor + jnp.sum(attn_weight, axis=-1)
            accumulated = accumulated * factor[..., None] + jnp.einsum(
                "kgts,skd->kgtd",
                attn_weight.astype(jnp.bfloat16),
                block_values,
                preferred_element_type=jnp.float32,
            )
            result = [new_max, running_sum, accumulated] + list(carry_in[3:])
            in_state = (key_pos < prev_start).astype(jnp.float32)
            features = feature_map(
                jnp.einsum(
                    "skd,kgdf->kgsf", block_keys.astype(jnp.float32), key_map, precision=precise
                )
            )
            features = features * in_state[None, None, :, None]
            result[-2] = carry_in[-2] + jnp.einsum(
                "kgsf,skd->kgfd", features, block_values.astype(jnp.float32), precision=precise
            )
            result[-1] = carry_in[-1] + jnp.sum(features, axis=2)
            return tuple(result)

        return lax.cond(first_row <= last_row, compute, skip_block, running)

    folded = lax.fori_loop(0, piece_rows // step_rows, attend, initial)
    teacher = folded[2] / folded[1][..., None]
    stacked = jnp.stack([keys, values])
    moved = shifted(stacked, "ctx", 1)
    prev_keys, prev_values = (moved[0], moved[1])
    has_prev = (my_block > 0).astype(jnp.float32)
    window_keys = jnp.concatenate([prev_keys, keys], axis=0)
    window_values = jnp.concatenate([prev_values, values], axis=0)
    column = jnp.arange(2 * block_len, dtype=jnp.int32)
    row_index = jnp.arange(block_len, dtype=jnp.int32)
    allowed = (column[None, :] < block_len) & (my_block > 0) | (column[None, :] >= block_len) & (
        column[None, :] - block_len <= row_index[:, None]
    )
    scores = (
        jnp.einsum("tkgd,skd->kgts", grouped_q, window_keys, preferred_element_type=jnp.float32)
        * score_scale
    )
    scores = jnp.where(allowed, scores, big_negative)
    row_max = jnp.max(scores, axis=-1)
    window_weight = jnp.where(allowed, jnp.exp(scores - row_max[..., None]), 0.0)
    window_den = jnp.sum(window_weight, axis=-1)
    window_num = jnp.einsum(
        "kgts,skd->kgtd",
        window_weight.astype(jnp.bfloat16),
        window_values,
        preferred_element_type=jnp.float32,
    )
    key_proj = jnp.einsum(
        "skd,kgdf->kgsf", prev_keys.astype(jnp.float32), key_map, precision=precise
    )
    state, norm = (folded[-2], folded[-1])
    query_proj = jnp.einsum(
        "tkgd,kgdf->kgtf", grouped_q.astype(jnp.float32), query_map, precision=precise
    )
    query_feats = feature_map(query_proj)
    decay = jnp.exp(-row_max)
    far_num = decay[..., None] * jnp.einsum(
        "kgtf,kgfd->kgtd", query_feats, state, precision=precise
    )
    far_den = decay * jnp.einsum("kgtf,kgf->kgt", query_feats, norm, precision=precise)
    denominator = window_den + far_den
    mix = (window_num + far_num) / denominator[..., None]
    student = jnp.transpose(mix.astype(jnp.bfloat16), (2, 0, 1, 3)).reshape(
        block_len, head_count, head_width
    )
    mismatch = mix - teacher
    grad_num = mismatch / denominator[..., None]
    grad_den = -jnp.sum(mismatch * mix, axis=-1) / denominator
    lifted = decay[..., None] * query_feats
    grad_state = jnp.einsum("kgtf,kgtd->kgfd", lifted, grad_num, precision=precise)
    grad_norm = jnp.einsum("kgtf,kgt->kgf", lifted, grad_den, precision=precise)
    grad_qfeat = decay[..., None] * (
        jnp.einsum("kgfd,kgtd->kgtf", state, grad_num, precision=precise)
        + norm[:, :, None, :] * grad_den[..., None]
    )
    later_state, later_norm = carried_in(
        (grad_state, grad_norm),
        "ctx",
        add_pair,
        (jnp.zeros_like(grad_state), jnp.zeros_like(grad_norm)),
    )
    grad_kfeat = (
        jnp.einsum(
            "kgfd,skd->kgsf", later_state, prev_values.astype(jnp.float32), precision=precise
        )
        + later_norm[:, :, None, :]
    ) * has_prev
    grad_query = jnp.einsum(
        "tkgd,kgtf->kgdf",
        grouped_q.astype(jnp.float32),
        feature_pull(query_proj, grad_qfeat),
        precision=precise,
    )
    grad_key = jnp.einsum(
        "skd,kgsf->kgdf",
        prev_keys.astype(jnp.float32),
        feature_pull(key_proj, grad_kfeat),
        precision=precise,
    )
    gradients = jnp.concatenate([grad_query, grad_key], axis=-1).reshape(
        head_count, head_width, 2 * feature_len
    )
    entry_count = gradients.size * lax.axis_size("head")
    summed = lax.psum(gradients, "ctx")
    squares = lax.psum(jnp.sum(summed * summed), "head")
    update = summed / jnp.sqrt(squares / entry_count + 1e-06)
    return (student, update)


f32, bf16 = jnp.float32, jnp.bfloat16
NN = (((1,), (0,)), ((), ()))
NT = (((1,), (1,)), ((), ()))
TN = (((0,), (0,)), ((), ()))


def mxu(a, b, dims):
    return lax.dot_general(a, b, dims, preferred_element_type=f32)


def split(x, pieces):
    out = []
    for _ in range(pieces):
        piece = x.astype(bf16)
        out.append(piece)
        x = x - piece.astype(f32)
    return out


def cat(parts, axis):
    return jnp.concatenate(parts, axis=axis)


def exact_by_wide(a, b, dims):
    return mxu(cat([a, a], dims[0][0][0]), cat(split(b, 2), dims[0][1][0]), dims)


def wide_by_exact(a, b, dims):
    return mxu(cat(split(a, 2), dims[0][0][0]), cat([b, b], dims[0][1][0]), dims)


def wide_by_wide(a, b, dims):
    a_hi, a_lo = split(a, 2)
    b_hi, b_lo = split(b, 2)
    return mxu(
        cat([a_hi, a_hi, a_lo], dims[0][0][0]), cat([b_hi, b_lo, b_hi], dims[0][1][0]), dims
    )


def half_sum(x, halves):
    return wide_by_exact(x, halves, NN)


def half_softmax(u, is_upper, halves):
    top = jnp.max(jnp.where(is_upper, u, big_negative), axis=-1, keepdims=True)
    low = jnp.max(jnp.where(is_upper, big_negative, u), axis=-1, keepdims=True)
    e = jnp.exp(u - jnp.where(is_upper, top, low))
    return e / half_sum(e, halves)


def remote(src, dst, send_sem, recv_sem, **where):
    return pltpu.make_async_remote_copy(
        src_ref=src,
        dst_ref=dst,
        send_sem=send_sem,
        recv_sem=recv_sem,
        device_id=where,
        device_id_type=pl.DeviceIdType.MESH,
    )


def each(count, body):
    def step(index, carry):
        body(index)
        return carry

    lax.fori_loop(0, count, step, 0)


def head_kernel(
    qt_ref, kvt_ref, w_ref, student_ref, update_ref,
    q_all, kv_all, mix_ref, gat_ref, gat_key_ref, sq_ref, own_ref, sum_ref, pre_ref, pre_norm_ref,
    score_ref, near_ref, kfeat_ref, gstate_ref, gnorm_ref, wq_ref, wk_ref, gq_ref,
    q_send, q_recv, kv_send, kv_recv, kv_relay, local_sem, st_send, st_recv,
    g_send, g_relay, g_recv, sq_send, sq_recv,
):
    blocks, length, width = qt_ref.shape
    planes = kvt_ref.shape[0]
    group = blocks // planes
    me, side = lax.axis_index("ctx"), lax.axis_index("head")
    plane, spot = me // group, me % group
    features = w_ref.shape[1] // 2
    rows = 2 * length
    steps, pairs = blocks // 2, blocks // 4
    middle = pairs - 1
    place = me // 2
    my_pair = jnp.where(place % 2 == 0, place, steps - 1 - place) // 2

    def pair_block(p, u):
        return jnp.where(u < 2, 4 * p + u, blocks - 4 - 4 * p + u)

    gats = (gat_ref, gat_key_ref)
    barrier = pltpu.get_barrier_semaphore()

    def greet(t):
        @pl.when(t != me)
        def _():
            pl.semaphore_signal(
                barrier, inc=1, device_id={"ctx": t}, device_id_type=pl.DeviceIdType.MESH
            )

    each(blocks, greet)
    pl.semaphore_signal(
        barrier, inc=1, device_id={"head": 1 - side}, device_id_type=pl.DeviceIdType.MESH
    )
    pl.semaphore_wait(barrier, blocks)

    def kv_column(g):
        return remote(
            kvt_ref.at[g], kv_all.at[me], kv_send.at[g], kv_recv.at[me], ctx=g * group + spot
        )

    def kv_own(r):
        return remote(
            kvt_ref.at[plane], kv_all.at[me], kv_relay.at[plane, r], kv_recv.at[me],
            ctx=plane * group + r,
        )

    def kv_pass(z, r):
        block = z * group + spot
        return remote(
            kv_all.at[block], kv_all.at[block], kv_relay.at[z, r], kv_recv.at[block],
            ctx=plane * group + r,
        )

    def q_copy(t):
        return remote(qt_ref.at[t], q_all.at[me], q_send.at[t], q_recv.at[me], ctx=t)

    def q_arrival(b):
        return remote(qt_ref.at[b], q_all.at[b], q_send.at[b], q_recv.at[b], ctx=b)

    def kv_arrival(b):
        return remote(
            kv_all.at[b], kv_all.at[b], kv_send.at[0], kv_recv.at[b], ctx=b
        )

    def st_copy(b):
        return remote(mix_ref.at[b], student_ref.at[me], st_send.at[b], st_recv.at[me], ctx=b)

    def st_arrival(b):
        return remote(mix_ref.at[b], student_ref.at[b], st_send.at[b], st_recv.at[b], ctx=b)

    def g_column(part, z):
        piece = gats[part].at[me]
        return remote(
            piece, piece, g_send.at[part, z], g_recv.at[me, part], ctx=z * group + spot
        )

    def g_pass(part, z, r):
        block = z * group + spot
        piece = gats[part].at[block]
        return remote(
            piece, piece, g_relay.at[part, z, r], g_recv.at[block, part], ctx=plane * group + r
        )

    def g_arrival(part, b):
        piece = gats[part].at[b]
        return remote(piece, piece, g_send.at[part, 0], g_recv.at[b, part], ctx=b)

    def planes_but_mine(body):
        def one(z):
            @pl.when(z != plane)
            def _():
                body(z)

        each(planes, one)

    def spots_but_mine(body):
        def one(r):
            @pl.when(r != spot)
            def _():
                body(r)

        each(group, one)

    planes_but_mine(lambda g: kv_column(g).start())
    spots_but_mine(lambda r: kv_own(r).start())
    own_kv = pltpu.make_async_copy(kvt_ref.at[plane], kv_all.at[me], local_sem.at[0])
    own_q = pltpu.make_async_copy(qt_ref.at[me], q_all.at[me], local_sem.at[1])
    own_kv.start()
    own_q.start()
    rate = math.log2(math.e) / math.sqrt(width)
    lane = lax.broadcasted_iota(jnp.int32, (rows, 2 * features), 1)
    is_upper = lane < features
    row_half = lax.broadcasted_iota(jnp.int32, (2 * features, 2 * features), 0) < features
    col_half = lax.broadcasted_iota(jnp.int32, (2 * features, 2 * features), 1) < features
    halves = jnp.where(row_half == col_half, 1.0, 0.0).astype(bf16)
    square = (rows, rows)
    causal = lax.broadcasted_iota(jnp.int32, square, 1) <= lax.broadcasted_iota(jnp.int32, square, 0)
    w = w_ref[...]
    wq, wk = w[:, :features], w[:, features:]
    wq_ref[...] = cat(split(cat([wq, -wq], 1), 3), 0)
    wk_ref[...] = cat(split(cat([wk, -wk], 1), 3), 0)
    gq_ref[...] = jnp.zeros_like(gq_ref)
    own_kv.wait()
    own_q.wait()

    def pass_on(z):
        kv_arrival(z * group + spot).wait_recv()
        spots_but_mine(lambda r: kv_pass(z, r).start())


    def load(part, i):
        if part == 0:
            return q_all[pl.ds(2 * i, 2)].reshape(rows, width)
        return kv_all[pl.ds(2 * i, 2), part - 1].reshape(rows, width)

    def q_arrived(b):
        @pl.when(b != me)
        def _():
            q_arrival(b).wait_recv()

    def kv_arrived(b):
        @pl.when(b % group != spot)
        def _():
            kv_arrival(b).wait_recv()

    def send_student(b):
        @pl.when(b != me)
        def _():
            st_copy(b).start()

        @pl.when(b == me)
        def _():
            student_ref[me] = mix_ref[me]

    def send_grad(part):
        planes_but_mine(lambda z: g_column(part, z).start())
        spots_but_mine(lambda r: g_pass(part, plane, r).start())

    def relay_grad(part):
        def one(z):
            g_arrival(part, z * group + spot).wait_recv()
            spots_but_mine(lambda r: g_pass(part, z, r).start())

        planes_but_mine(one)

    def key_side(pair):
        each(4, lambda u: kv_arrived(4 * pair + u))
        steps_of = (2 * pair, 2 * pair + 1)
        ks, vs = ([load(part, i) for i in steps_of] for part in (1, 2))
        kfs = [
            half_softmax(mxu(cat([k, k, k], 1), wk_ref[...], NN), is_upper, halves) for k in ks
        ]
        for i, kf, v in zip(steps_of, kfs, vs):
            kfeat_ref[i] = kf
            for h in range(2):
                part = kf[h * length:(h + 1) * length]
                own_ref[2 * i + h] = wide_by_exact(part, v[h * length:(h + 1) * length], TN)
                sum_ref[2 * i + h] = jnp.sum(part, axis=0, keepdims=True)

    def push(d):
        t = pair_block((my_pair + pairs - d // 4) % pairs, d % 4)

        @pl.when(t != me)
        def _():
            q_copy(t).start()

    each(blocks, push)

    def relay_first(dz):
        pass_on((plane + dz + 1) % planes)

    each(planes - 1, relay_first)

    def stage(dz):
        each(group // 4, lambda u: key_side((plane + dz) % planes * (group // 4) + u))

    each(planes, stage)
    for b in range(2):
        pre_ref[b] = jnp.zeros_like(pre_ref[b])
        pre_norm_ref[b] = jnp.zeros_like(pre_norm_ref[b])

    def prefix(b):
        pre_ref[b + 2] = pre_ref[b + 1] + own_ref[b]
        pre_norm_ref[b + 2] = pre_norm_ref[b + 1] + sum_ref[b]

    each(blocks - 2, prefix)

    def forward(turn, carry):
        p = (my_pair + turn) % pairs
        a, b = 2 * p, steps - 1 - 2 * p
        each(4, lambda u: q_arrived(pair_block(p, u)))
        tokens = (a, b)
        qs = [load(0, i) for i in tokens]
        vs = [load(2, i) for i in tokens]
        wide_b = b // 2

        def pair_of(part, j):
            return cat([load(part, 2 * j), load(part, 2 * j + 1)], 0)

        def fold(x, combine):
            while x.shape[1] > length:
                half = x.shape[1] // 2
                x = combine(x[:, :half], x[:, half:])
            return x

        s = mxu(qs[0], load(1, a), NT) * rate
        s_a = jnp.where(causal, s, big_negative)
        near_ref[0] = s_a
        s = mxu(qs[1], pair_of(1, wide_b), NT) * rate
        s_b = [s[:, :rows], jnp.where(causal, s[:, rows:], big_negative)]
        near_ref[1], near_ref[2] = s_b
        peaks = [fold(s_a, jnp.maximum), fold(jnp.maximum(*s_b), jnp.maximum)]

        def far_tile(m):
            first = m < p
            return first, jnp.where(first, a, b), jnp.where(first, m, m - p)

        for m in range(middle):
            first, i, j = far_tile(m)
            s = mxu(load(0, i), pair_of(1, j), NT) * rate
            score_ref[m] = s
            top = fold(s, jnp.maximum)
            peaks = [
                jnp.maximum(peaks[0], jnp.where(first, top, big_negative)),
                jnp.maximum(peaks[1], jnp.where(first, big_negative, top)),
            ]
        tops = [jnp.max(x, axis=-1, keepdims=True) for x in peaks]

        weight = jnp.exp2(near_ref[0] - tops[0])
        sums = [fold(weight, jnp.add)]
        accs = [mxu(weight.astype(bf16), vs[0], NN)]
        weight = jnp.exp2(cat([near_ref[1], near_ref[2]], 1) - tops[1])
        sums.append(fold(weight, jnp.add))
        accs.append(mxu(weight.astype(bf16), pair_of(2, wide_b), NN))
        for m in range(middle):
            first, i, j = far_tile(m)
            weight = jnp.exp2(score_ref[m] - jnp.where(first, tops[0], tops[1]))
            part = fold(weight, jnp.add)
            prod = mxu(weight.astype(bf16), pair_of(2, j), NN)
            sums = [sums[0] + jnp.where(first, part, 0.0), sums[1] + jnp.where(first, 0.0, part)]
            accs = [accs[0] + jnp.where(first, prod, 0.0), accs[1] + jnp.where(first, 0.0, prod)]
        teachers = [
            acc / jnp.sum(total, axis=-1, keepdims=True) for acc, total in zip(accs, sums)
        ]

        def halves_of(f):
            return [cat([f(x, 0), f(x, 1)], 0) for x in range(2)]

        def cut(x, half):
            return x[half * length:(half + 1) * length]

        last_far = score_ref[jnp.maximum(p - 1, 0), :length, 3 * length:]
        prevs = [
            cat([jnp.where(p > 0, last_far, big_negative), near_ref[0, length:, :length]], 0),
            cat([near_ref[1, :length, length:], near_ref[2, length:, :length]], 0),
        ]
        owns = [
            cat([near_ref[k, :length, :length], near_ref[k, length:, length:]], 0) for k in (0, 2)
        ]
        win_maxs = [
            jnp.max(jnp.maximum(prev, own), axis=-1, keepdims=True)
            for prev, own in zip(prevs, owns)
        ]
        p_prevs = [jnp.exp2(x - top) for x, top in zip(prevs, win_maxs)]
        p_owns = [jnp.exp2(x - top) for x, top in zip(owns, win_maxs)]
        win_dens = [jnp.sum(x + y, axis=-1, keepdims=True) for x, y in zip(p_prevs, p_owns)]
        p_wins = [cat([x.astype(bf16), y.astype(bf16)], 1) for x, y in zip(p_prevs, p_owns)]
        v_befores = [kv_all[jnp.maximum(2 * i - 1, 0), 1] for i in tokens]
        v_wins = [
            (cat([before, v[:length]], 0), v) for before, v in zip(v_befores, vs)
        ]
        win_nums = halves_of(lambda x, h: mxu(cut(p_wins[x], h), v_wins[x][h], NN))

        qfs = [
            half_softmax(mxu(cat([q, q, q], 1), wq_ref[...], NN), is_upper, halves) for q in qs
        ]
        states = [[pre_ref[2 * i], pre_ref[2 * i + 1]] for i in tokens]
        norms = [
            cat(
                [
                    jnp.broadcast_to(pre_norm_ref[2 * i + h], (length, 2 * features))
                    for h in range(2)
                ],
                0,
            )
            for i in tokens
        ]
        decays = [jnp.exp2(-top) for top in win_maxs]
        fars = halves_of(lambda x, h: wide_by_wide(cut(qfs[x], h), states[x][h], NN))
        dens = [
            win_den + decay * jnp.sum(qf * norm, axis=-1, keepdims=True)
            for win_den, decay, qf, norm in zip(win_dens, decays, qfs, norms)
        ]
        mixes = [
            (num + decay * far) / den
            for num, decay, far, den in zip(win_nums, decays, fars, dens)
        ]
        for i, mix in zip(tokens, mixes):
            mix_ref[pl.ds(2 * i, 2)] = mix.astype(bf16).reshape(2, length, width)
        each(4, lambda u: send_student(pair_block(p, u)))
        mismatches = [mix - teacher for mix, teacher in zip(mixes, teachers)]
        g_nums = [x / den for x, den in zip(mismatches, dens)]
        g_dens = [
            -jnp.sum(x * mix, axis=-1, keepdims=True) / den
            for x, mix, den in zip(mismatches, mixes, dens)
        ]
        lifts = [decay * qf for decay, qf in zip(decays, qfs)]
        pulled_norms = [lift * g_den for lift, g_den in zip(lifts, g_dens)]
        for x, i in enumerate(tokens):
            for h in range(2):
                gstate_ref[2 * i + h] = wide_by_wide(cut(lifts[x], h), cut(g_nums[x], h), TN)
                gnorm_ref[2 * i + h] = jnp.sum(cut(pulled_norms[x], h), axis=0, keepdims=True)
        pulled = halves_of(lambda x, h: wide_by_wide(cut(g_nums[x], h), states[x][h], NT))
        g_qfs = [
            decay * (pull + norm * g_den)
            for decay, pull, norm, g_den in zip(decays, pulled, norms, g_dens)
        ]
        d_qs = [qf * (g - half_sum(qf * g, halves)) for qf, g in zip(qfs, g_qfs)]
        gq_ref[...] += wide_by_exact(d_qs[0], qs[0], TN) + wide_by_exact(d_qs[1], qs[1], TN)
        return carry

    lax.fori_loop(0, pairs, forward, 0)
    gat_ref[me] = (gq_ref[:features] - gq_ref[features:]).astype(bf16)
    send_grad(0)

    for b in range(blocks - 2, 1, -1):
        gstate_ref[b] = gstate_ref[b] + gstate_ref[b + 1]
        gnorm_ref[b] = gnorm_ref[b] + gnorm_ref[b + 1]

    def backward(group_of):
        ks, vs, kfs = ([f(i) for i in group_of] for f in (lambda i: load(1, i), lambda i: load(2, i), lambda i: kfeat_ref[i]))
        g_kfs = [
            cat(
                [
                    exact_by_wide(v[h * length:(h + 1) * length], gstate_ref[2 * i + h + 2], NT)
                    + gnorm_ref[2 * i + h + 2]
                    for h in range(2)
                ],
                0,
            )
            for i, v in zip(group_of, vs)
        ]
        d_ks = [kf * (g - half_sum(kf * g, halves)) for kf, g in zip(kfs, g_kfs)]
        return [wide_by_exact(d_k, k, TN) for d_k, k in zip(d_ks, ks)]

    gk = sum(backward(range(steps // 2)) + backward(range(steps // 2, steps - 1)))
    gat_key_ref[me] = (gk[:features] - gk[features:]).astype(bf16)
    send_grad(1)
    relay_grad(0)
    relay_grad(1)

    def gathered(b):
        @pl.when(b % group != spot)
        def _():
            g_arrival(0, b).wait_recv()
            g_arrival(1, b).wait_recv()

    each(blocks, gathered)
    squares = jnp.zeros((8, width), f32)
    for b in range(blocks):
        piece = cat([gat_ref[b], gat_key_ref[b]], 0).astype(f32)
        piece = piece.reshape(2 * features // 8, 8, width)
        squares = squares + jnp.sum(piece * piece, axis=0)
    sq_ref[0] = squares
    swap = remote(sq_ref.at[0], sq_ref.at[1], sq_send.at[0], sq_recv.at[0], head=1 - side)
    swap.start()

    for b in range(blocks):
        update_ref[b] = cat([gat_ref[b], gat_key_ref[b]], 0).astype(f32).T


    def settle(t):
        @pl.when(t != me)
        def _():
            q_copy(t).wait_send()
            st_copy(t).wait_send()
            st_arrival(t).wait_recv()

    each(blocks, settle)

    def settle_plane(z):
        @pl.when(z != plane)
        def _():
            kv_column(z).wait_send()
            g_column(0, z).wait_send()
            g_column(1, z).wait_send()

        def one(r):
            kv_pass(z, r).wait_send()
            g_pass(0, z, r).wait_send()
            g_pass(1, z, r).wait_send()

        spots_but_mine(one)

    each(planes, settle_plane)
    swap.wait()
    entries = 2 * blocks * width * 2 * features
    total = jnp.sum(sq_ref[0] + sq_ref[1], keepdims=True)
    inverse = 1.0 / jnp.sqrt(total / entries + 1e-06)

    for b in range(blocks):
        update_ref[b] = update_ref[b] * inverse


def whole_head(qt, kvt, w):
    blocks, length, width = qt.shape
    planes = kvt.shape[0]
    group = blocks // planes
    double = w.shape[1]
    rows, steps = 2 * length, blocks // 2
    vmem, dma = pltpu.VMEM, pltpu.SemaphoreType.DMA
    return pl.pallas_call(
        head_kernel,
        out_shape=(
            jax.ShapeDtypeStruct((blocks, length, width), bf16),
            jax.ShapeDtypeStruct((blocks, width, double), f32),
        ),
        in_specs=[pl.BlockSpec(memory_space=vmem)] * 3,
        out_specs=(pl.BlockSpec(memory_space=vmem),) * 2,
        scratch_shapes=[
            vmem((blocks, length, width), bf16),
            vmem((blocks, 2, length, width), bf16),
            vmem((blocks, length, width), bf16),
            vmem((blocks, double // 2, width), bf16),
            vmem((blocks, double // 2, width), bf16),
            vmem((2, 8, width), f32),
            vmem((blocks, double, width), f32),
            vmem((blocks, 1, double), f32),
            vmem((blocks, double, width), f32),
            vmem((blocks, 1, double), f32),
            vmem((blocks // 4 - 1, rows, 2 * rows), f32),
            vmem((3, rows, rows), f32),
            vmem((steps, rows, double), f32),
            vmem((blocks, double, width), f32),
            vmem((blocks, 1, double), f32),
            vmem((3 * width, double), bf16),
            vmem((3 * width, double), bf16),
            vmem((double, width), f32),
            dma((blocks,)),
            dma((blocks,)),
            dma((planes,)),
            dma((blocks,)),
            dma((planes, group)),
            dma((2,)),
            dma((blocks,)),
            dma((blocks,)),
            dma((2, planes)),
            dma((2, planes, group)),
            dma((blocks, 2)),
            dma((1,)),
            dma((1,)),
        ],
        compiler_params=pltpu.CompilerParams(
            vmem_limit_bytes=40 * 2**20, collective_id=0, has_side_effects=True
        ),
    )(qt, kvt, w)


def head_shards(queries, keys, values, feature_weight):
    qt = jnp.transpose(queries, (1, 0, 2))
    kvt = jnp.transpose(jnp.stack([keys, values]), (2, 0, 1, 3))
    w = lax.dynamic_index_in_dim(feature_weight, lax.axis_index("ctx"), 0, False)
    student, update = whole_head(qt, kvt, w)
    return (jnp.transpose(student, (1, 0, 2)), update)


def shards(queries, keys, values, feature_weight):
    count = lax.axis_size("ctx")
    width = queries.shape[2]
    fits = queries.shape[1] == count and lax.axis_size("head") == 2 and count % 4 == 0 and count * queries.shape[0] <= 4096
    fits = fits and queries.shape[1] // keys.shape[1] % 4 == 0 and queries.shape[0] == width and feature_weight.shape[2] == width
    body = head_shards if fits else general_shards
    return body(queries, keys, values, feature_weight)


def solution(mesh):
    return jax.shard_map(
        shards,
        mesh=mesh,
        in_specs=(
            P("ctx", "head", None),
            P("ctx", "head", None),
            P("ctx", "head", None),
            P("head", None, None),
        ),
        out_specs=(P("ctx", "head", None), P("head", None, None)),
        check_vma=False,
    )
```

```python
import functools
import math

import jax
import jax.numpy as jnp
from jax import lax
from jax.experimental import pallas as pl
from jax.experimental.pallas import tpu as pltpu
from jax.sharding import PartitionSpec as P

precise = lax.Precision.HIGHEST
big_negative = -1e30


def shifted(shard, axis, by):
    devices = lax.axis_size(axis)
    pairs = [(i, i + by) for i in range(devices) if 0 <= i + by < devices]
    return lax.ppermute(shard, axis, pairs)


def carried_in(part, axis, combine, identity):
    count = lax.axis_size(axis)
    place = lax.axis_index(axis)
    ahead = count - 1 - place
    gathered = jax.tree.map(lambda a: lax.all_gather(a, axis), part)
    state = jax.tree.map(lambda a, e: jnp.zeros_like(a) + jnp.asarray(e, a.dtype), part, identity)

    def one(step, state):
        source = count - 1 - step
        return combine(
            state, jax.tree.map(lambda a: lax.dynamic_index_in_dim(a, source, 0, False), gathered)
        )

    return lax.fori_loop(0, ahead, one, state)


def feature_map(projection):
    return jnp.concatenate(
        [jax.nn.softmax(projection, axis=-1), jax.nn.softmax(-projection, axis=-1)], axis=-1
    )


def feature_pull(projection, upstream):
    half_len = upstream.shape[-1] // 2
    upper = jax.nn.softmax(projection, axis=-1)
    lower = jax.nn.softmax(-projection, axis=-1)
    grad_upper = upstream[..., :half_len]
    grad_lower = upstream[..., half_len:]
    upper_part = upper * (grad_upper - jnp.sum(upper * grad_upper, axis=-1, keepdims=True))
    lower_part = lower * (grad_lower - jnp.sum(lower * grad_lower, axis=-1, keepdims=True))
    return upper_part - lower_part


def add_pair(earlier, later):
    return (earlier[0] + later[0], earlier[1] + later[1])


def skip_block(carry_in):
    return carry_in


def general_shards(queries, keys, values, feature_weight):
    block_len, head_count, head_width = queries.shape
    kv_count = keys.shape[1]
    group_size = head_count // kv_count
    feature_len = feature_weight.shape[2] // 2
    my_block = lax.axis_index("ctx")
    score_scale = 1.0 / math.sqrt(head_width)
    grouped_q = queries.reshape(block_len, kv_count, group_size, head_width)
    maps_weight = feature_weight.reshape(kv_count, group_size, head_width, 2 * feature_len)
    query_map = maps_weight[..., :feature_len]
    key_map = maps_weight[..., feature_len:]
    query_pos = my_block * block_len + jnp.arange(block_len, dtype=jnp.int32)
    prev_start = (my_block - 1) * block_len
    last_row = my_block * block_len + block_len - 1
    initial = [
        jnp.full((kv_count, group_size, block_len), big_negative, jnp.float32),
        jnp.zeros((kv_count, group_size, block_len), jnp.float32),
        jnp.zeros((kv_count, group_size, block_len, head_width), jnp.float32),
    ]
    initial = initial + [
        jnp.zeros((kv_count, group_size, 2 * feature_len, head_width), jnp.float32),
        jnp.zeros((kv_count, group_size, 2 * feature_len), jnp.float32),
    ]
    initial = tuple(initial)
    piece_keys = lax.all_gather(keys, "ctx", axis=0, tiled=True)
    piece_values = lax.all_gather(values, "ctx", axis=0, tiled=True)
    piece_rows = piece_keys.shape[0]
    step_rows = math.gcd(piece_rows, 512)

    def attend(step_index, running):
        first_row = step_index * step_rows
        block_keys = lax.dynamic_slice_in_dim(piece_keys, step_index * step_rows, step_rows, 0)
        block_values = lax.dynamic_slice_in_dim(piece_values, step_index * step_rows, step_rows, 0)
        key_pos = first_row + jnp.arange(step_rows, dtype=jnp.int32)

        def compute(carry_in):
            row_max, running_sum, accumulated = (carry_in[0], carry_in[1], carry_in[2])
            scores = (
                jnp.einsum(
                    "tkgd,skd->kgts", grouped_q, block_keys, preferred_element_type=jnp.float32
                )
                * score_scale
            )
            allowed = key_pos[None, :] <= query_pos[:, None]
            scores = jnp.where(allowed, scores, big_negative)
            new_max = jnp.maximum(row_max, jnp.max(scores, axis=-1))
            attn_weight = jnp.where(allowed, jnp.exp(scores - new_max[..., None]), 0.0)
            factor = jnp.exp(row_max - new_max)
            running_sum = running_sum * factor + jnp.sum(attn_weight, axis=-1)
            accumulated = accumulated * factor[..., None] + jnp.einsum(
                "kgts,skd->kgtd",
                attn_weight.astype(jnp.bfloat16),
                block_values,
                preferred_element_type=jnp.float32,
            )
            result = [new_max, running_sum, accumulated] + list(carry_in[3:])
            in_state = (key_pos < prev_start).astype(jnp.float32)
            features = feature_map(
                jnp.einsum(
                    "skd,kgdf->kgsf", block_keys.astype(jnp.float32), key_map, precision=precise
                )
            )
            features = features * in_state[None, None, :, None]
            result[-2] = carry_in[-2] + jnp.einsum(
                "kgsf,skd->kgfd", features, block_values.astype(jnp.float32), precision=precise
            )
            result[-1] = carry_in[-1] + jnp.sum(features, axis=2)
            return tuple(result)

        return lax.cond(first_row <= last_row, compute, skip_block, running)

    folded = lax.fori_loop(0, piece_rows // step_rows, attend, initial)
    teacher = folded[2] / folded[1][..., None]
    stacked = jnp.stack([keys, values])
    moved = shifted(stacked, "ctx", 1)
    prev_keys, prev_values = (moved[0], moved[1])
    has_prev = (my_block > 0).astype(jnp.float32)
    window_keys = jnp.concatenate([prev_keys, keys], axis=0)
    window_values = jnp.concatenate([prev_values, values], axis=0)
    column = jnp.arange(2 * block_len, dtype=jnp.int32)
    row_index = jnp.arange(block_len, dtype=jnp.int32)
    allowed = (column[None, :] < block_len) & (my_block > 0) | (column[None, :] >= block_len) & (
        column[None, :] - block_len <= row_index[:, None]
    )
    scores = (
        jnp.einsum("tkgd,skd->kgts", grouped_q, window_keys, preferred_element_type=jnp.float32)
        * score_scale
    )
    scores = jnp.where(allowed, scores, big_negative)
    row_max = jnp.max(scores, axis=-1)
    window_weight = jnp.where(allowed, jnp.exp(scores - row_max[..., None]), 0.0)
    window_den = jnp.sum(window_weight, axis=-1)
    window_num = jnp.einsum(
        "kgts,skd->kgtd",
        window_weight.astype(jnp.bfloat16),
        window_values,
        preferred_element_type=jnp.float32,
    )
    key_proj = jnp.einsum(
        "skd,kgdf->kgsf", prev_keys.astype(jnp.float32), key_map, precision=precise
    )
    state, norm = (folded[-2], folded[-1])
    query_proj = jnp.einsum(
        "tkgd,kgdf->kgtf", grouped_q.astype(jnp.float32), query_map, precision=precise
    )
    query_feats = feature_map(query_proj)
    decay = jnp.exp(-row_max)
    far_num = decay[..., None] * jnp.einsum(
        "kgtf,kgfd->kgtd", query_feats, state, precision=precise
    )
    far_den = decay * jnp.einsum("kgtf,kgf->kgt", query_feats, norm, precision=precise)
    denominator = window_den + far_den
    mix = (window_num + far_num) / denominator[..., None]
    student = jnp.transpose(mix.astype(jnp.bfloat16), (2, 0, 1, 3)).reshape(
        block_len, head_count, head_width
    )
    mismatch = mix - teacher
    grad_num = mismatch / denominator[..., None]
    grad_den = -jnp.sum(mismatch * mix, axis=-1) / denominator
    lifted = decay[..., None] * query_feats
    grad_state = jnp.einsum("kgtf,kgtd->kgfd", lifted, grad_num, precision=precise)
    grad_norm = jnp.einsum("kgtf,kgt->kgf", lifted, grad_den, precision=precise)
    grad_qfeat = decay[..., None] * (
        jnp.einsum("kgfd,kgtd->kgtf", state, grad_num, precision=precise)
        + norm[:, :, None, :] * grad_den[..., None]
    )
    later_state, later_norm = carried_in(
        (grad_state, grad_norm),
        "ctx",
        add_pair,
        (jnp.zeros_like(grad_state), jnp.zeros_like(grad_norm)),
    )
    grad_kfeat = (
        jnp.einsum(
            "kgfd,skd->kgsf", later_state, prev_values.astype(jnp.float32), precision=precise
        )
        + later_norm[:, :, None, :]
    ) * has_prev
    grad_query = jnp.einsum(
        "tkgd,kgtf->kgdf",
        grouped_q.astype(jnp.float32),
        feature_pull(query_proj, grad_qfeat),
        precision=precise,
    )
    grad_key = jnp.einsum(
        "skd,kgsf->kgdf",
        prev_keys.astype(jnp.float32),
        feature_pull(key_proj, grad_kfeat),
        precision=precise,
    )
    gradients = jnp.concatenate([grad_query, grad_key], axis=-1).reshape(
        head_count, head_width, 2 * feature_len
    )
    entry_count = gradients.size * lax.axis_size("head")
    summed = lax.psum(gradients, "ctx")
    squares = lax.psum(jnp.sum(summed * summed), "head")
    update = summed / jnp.sqrt(squares / entry_count + 1e-06)
    return (student, update)


f32, bf16 = jnp.float32, jnp.bfloat16
NN = (((1,), (0,)), ((), ()))
NT = (((1,), (1,)), ((), ()))
TN = (((0,), (0,)), ((), ()))


def mxu(a, b, dims):
    return lax.dot_general(a, b, dims, preferred_element_type=f32)


def split(x, pieces):
    out = []
    for _ in range(pieces):
        piece = x.astype(bf16)
        out.append(piece)
        x = x - piece.astype(f32)
    return out


def cat(parts, axis):
    return jnp.concatenate(parts, axis=axis)


def exact_by_wide(a, b, dims):
    return mxu(cat([a, a], dims[0][0][0]), cat(split(b, 2), dims[0][1][0]), dims)


def wide_by_exact(a, b, dims):
    return mxu(cat(split(a, 2), dims[0][0][0]), cat([b, b], dims[0][1][0]), dims)


def wide_by_wide(a, b, dims):
    a_hi, a_lo = split(a, 2)
    b_hi, b_lo = split(b, 2)
    return mxu(
        cat([a_hi, a_hi, a_lo], dims[0][0][0]), cat([b_hi, b_lo, b_hi], dims[0][1][0]), dims
    )


def half_sum(x, halves):
    return wide_by_exact(x, halves, NN)


def half_softmax(u, is_upper, halves):
    top = jnp.max(jnp.where(is_upper, u, big_negative), axis=-1, keepdims=True)
    low = jnp.max(jnp.where(is_upper, big_negative, u), axis=-1, keepdims=True)
    e = jnp.exp(u - jnp.where(is_upper, top, low))
    return e / half_sum(e, halves)


def remote(src, dst, send_sem, recv_sem, **where):
    return pltpu.make_async_remote_copy(
        src_ref=src,
        dst_ref=dst,
        send_sem=send_sem,
        recv_sem=recv_sem,
        device_id=where,
        device_id_type=pl.DeviceIdType.MESH,
    )


def each(count, body):
    def step(index, carry):
        body(index)
        return carry

    lax.fori_loop(0, count, step, 0)


def head_kernel(
    q_hbm, k_hbm, v_hbm, w_hbm, student_hbm, grad_hbm, scale_hbm,
    q_raw, k_raw, v_raw, w_ref, qt_ref, kvt_ref, q_all, kv_all, st_all, st_turned, mix_ref,
    own_grad, gat_ref, sq_ref, scale_ref, own_ref, sum_ref, pre_ref, pre_norm_ref,
    score_ref, near_ref, kfeat_ref, gstate_ref, gnorm_ref, wq_ref, wk_ref, gq_ref,
    q_send, q_recv, kv_send, kv_recv, kv_cross, kv_sibling, local_sem, st_send, st_recv,
    g_send, g_relay, g_recv, sq_send, sq_recv, fetch_sem, w_send, w_recv, out_sem,
):
    blocks, length, width = qt_ref.shape
    planes = kvt_ref.shape[0]
    group = blocks // planes
    me, side = lax.axis_index("ctx"), lax.axis_index("head")
    plane, spot = me // group, me % group
    row, column = spot // 2, spot % 2
    native = row == side
    mine = plane * group + 2 * column + side
    features = w_ref.shape[1] // 2
    rows = 2 * length
    steps, pairs = blocks // 2, blocks // 4
    middle = pairs - 1

    def pair_block(p, u):
        return jnp.where(u < 2, 4 * p + u, blocks - 4 - 4 * p + u)

    my_pair = jnp.where(row == 0, plane, planes - 1 - plane)
    barrier = pltpu.get_barrier_semaphore()

    def greet(t, h):
        pl.semaphore_signal(
            barrier, inc=1, device_id={"ctx": t, "head": h}, device_id_type=pl.DeviceIdType.MESH
        )

    def greet_side(d):
        t = (me + d) % blocks

        @pl.when(jnp.logical_not(native & (t == me)))
        def _():
            greet(t, row)

    each(blocks, greet_side)
    each(blocks // 2, lambda n: greet((n // 2) * group + 2 * side + n % 2, 1 - row))
    fetches = [
        pltpu.make_async_copy(src, dst, fetch_sem.at[n])
        for n, (src, dst) in enumerate([(k_hbm, k_raw), (v_hbm, v_raw), (q_hbm, q_raw)])
    ]
    for fetch in fetches:
        fetch.start()
    own_w = pltpu.make_async_copy(w_hbm.at[mine], w_ref, local_sem.at[2])

    @pl.when(native)
    def _():
        own_w.start()

    def flip(index, d):
        bit = 1
        while bit <= d:
            if d & bit:
                index = index + bit - 2 * bit * ((index // bit) % 2)
            bit *= 2
        return index

    def w_copy():
        other = plane * group + 2 * column + 1 - side
        return remote(w_hbm.at[other], w_ref, w_send.at[0], w_recv.at[0], ctx=me, head=1 - side)

    def kv_land(g):
        return remote(
            kvt_ref.at[g], kv_all.at[me], kv_send.at[g], kv_recv.at[me],
            ctx=g * group + 2 * side + column, head=row,
        )

    def landed_block(z):
        return z * group + 2 * side + column

    def crossed_block(z):
        return z * group + 2 * side + 1 - column

    def kv_across(z):
        block = landed_block(z)
        return remote(
            kv_all.at[block], kv_all.at[block], kv_cross.at[z], kv_recv.at[block],
            ctx=plane * group + 2 * row + 1 - column, head=side,
        )

    def kv_share(block, n):
        return remote(
            kv_all.at[block], kv_all.at[block], kv_sibling.at[n], kv_recv.at[block],
            ctx=me, head=1 - side,
        )

    def q_copy(j):
        return remote(
            qt_ref.at[j], q_all.at[me], q_send.at[j], q_recv.at[me],
            ctx=(j // group) * group + 2 * side + (j % group) // 2, head=j % 2,
        )

    def q_arrival(b):
        return remote(qt_ref.at[b], q_all.at[b], q_send.at[b], q_recv.at[b], ctx=b, head=row)

    def kv_arrival(b):
        return remote(kv_all.at[b], kv_all.at[b], kv_send.at[0], kv_recv.at[b], ctx=b, head=row)

    def st_copy(b):
        return remote(mix_ref.at[b], st_all.at[mine], st_send.at[b], st_recv.at[mine], ctx=b, head=row)

    def st_arrival(j):
        return remote(mix_ref.at[j], st_all.at[j], st_send.at[j], st_recv.at[j], ctx=j, head=row)

    def g_column(part, z):
        return remote(
            own_grad.at[part], gat_ref.at[part, mine], g_send.at[part, z], g_recv.at[part, mine],
            ctx=z * group + spot, head=row,
        )

    def g_pass(part, j, d):
        piece = gat_ref.at[part, j]
        return remote(
            piece, piece, g_relay.at[part, j, d - 1], g_recv.at[part, j],
            ctx=plane * group + flip(spot, d), head=side,
        )

    def g_arrival(part, j):
        piece = gat_ref.at[part, j]
        return remote(piece, piece, g_send.at[part, 0], g_recv.at[part, j], ctx=j, head=row)

    def unless_own(b, body):
        @pl.when(jnp.logical_not(native & (b == me)))
        def _():
            body()

    rate = math.log2(math.e) / math.sqrt(width)
    lane = lax.broadcasted_iota(jnp.int32, (rows, 2 * features), 1)
    is_upper = lane < features
    row_half = lax.broadcasted_iota(jnp.int32, (2 * features, 2 * features), 0) < features
    col_half = lax.broadcasted_iota(jnp.int32, (2 * features, 2 * features), 1) < features
    halves = jnp.where(row_half == col_half, 1.0, 0.0).astype(bf16)
    square = (rows, rows)
    causal = lax.broadcasted_iota(jnp.int32, square, 1) <= lax.broadcasted_iota(jnp.int32, square, 0)
    for part, (fetch, raw) in enumerate(zip(fetches, (k_raw, v_raw))):
        fetch.wait()
        kvt_ref[:, part] = jnp.transpose(raw[...], (1, 0, 2))
    own_kv = pltpu.make_async_copy(kvt_ref.at[plane], kv_all.at[me], local_sem.at[0])

    @pl.when(native)
    def _():
        own_kv.start()

    pl.semaphore_wait(barrier, jnp.where(native, 3 * blocks // 2 - 1, 3 * blocks // 2))
    for d in range(planes):
        g = flip(plane, d)
        if d == 0:
            @pl.when(jnp.logical_not(native))
            def _():
                kv_land(g).start()
        else:
            kv_land(g).start()

    @pl.when(native)
    def _():
        w_copy().start()

    fetches[2].wait()
    qt_ref[...] = jnp.transpose(q_raw[...], (1, 0, 2))
    own_q = pltpu.make_async_copy(qt_ref.at[mine], q_all.at[me], local_sem.at[1])

    @pl.when(native)
    def _():
        own_q.start()
        own_kv.wait()

    def land(d):
        z = flip(plane, d)
        block = landed_block(z)
        unless_own(block, lambda: kv_arrival(block).wait_recv())
        kv_across(z).start()
        kv_share(block, z).start()

    def cross(d):
        z = flip(plane, d)
        block = crossed_block(z)
        kv_arrival(block).wait_recv()
        kv_share(block, planes + z).start()

    def load(part, i):
        if part == 0:
            return q_all[pl.ds(2 * i, 2)].reshape(rows, width)
        return kv_all[pl.ds(2 * i, 2), part - 1].reshape(rows, width)

    def q_arrived(b):
        unless_own(b, lambda: q_arrival(b).wait_recv())

    def kv_arrived(b):
        @pl.when((b % group) // 2 != side)
        def _():
            kv_arrival(b).wait_recv()

    def send_student(b):
        unless_own(b, lambda: st_copy(b).start())

        @pl.when(native & (b == me))
        def _():
            st_all[mine] = mix_ref[me]

    def send_grad(part):
        for d in range(planes):
            z = flip(plane, d)
            if d == 0:
                @pl.when(native)
                def _():
                    gat_ref[part, mine] = own_grad[part]

                @pl.when(jnp.logical_not(native))
                def _():
                    g_column(part, z).start()
            else:
                g_column(part, z).start()

    def relay_grad(part):
        @pl.when(native)
        def _():
            for z in range(planes):
                for h in range(2):
                    j = flip(plane, z) * group + 2 * column + h

                    @pl.when(j != mine)
                    def _():
                        g_arrival(part, j).wait_recv()

                    for d in range(1, group):
                        g_pass(part, j, d).start()

    def key_side(pair):
        each(4, lambda u: kv_arrived(4 * pair + u))
        steps_of = (2 * pair, 2 * pair + 1)
        ks, vs = ([load(part, i) for i in steps_of] for part in (1, 2))
        kfs = [
            half_softmax(mxu(cat([k, k, k], 1), wk_ref[...], NN), is_upper, halves) for k in ks
        ]
        for i, kf, v in zip(steps_of, kfs, vs):
            kfeat_ref[i] = kf
            for h in range(2):
                part = kf[h * length:(h + 1) * length]
                own_ref[2 * i + h] = wide_by_exact(part, v[h * length:(h + 1) * length], TN)
                sum_ref[2 * i + h] = jnp.sum(part, axis=0, keepdims=True)

    def push(n):
        p = (my_pair + pairs - n // group) % pairs
        j = jnp.where(side == 0, p, planes - 1 - p) * group + n % group

        @pl.when(jnp.logical_not(native & (j == mine)))
        def _():
            q_copy(j).start()

    def plane_keys(z):
        each(group // 4, lambda u: key_side(z * (group // 4) + u))

    def push_turns(first, last):
        each((last - first) * group, lambda n: push(first * group + n))

    land(0)
    land(1)
    cross(0)
    push_turns(0, 1)
    land(2)
    cross(1)
    land(3)
    cross(2)
    cross(3)

    @pl.when(native)
    def _():
        own_w.wait()

    @pl.when(jnp.logical_not(native))
    def _():
        w_copy().wait_recv()

    w = w_ref[...]
    wq, wk = w[:, :features], w[:, features:]
    wq_ref[...] = cat(split(cat([wq, -wq], 1), 3), 0)
    wk_ref[...] = cat(split(cat([wk, -wk], 1), 3), 0)
    gq_ref[...] = jnp.zeros_like(gq_ref)
    push_turns(1, pairs)
    for d in range(planes):
        plane_keys(flip(plane, d))

    @pl.when(native)
    def _():
        own_q.wait()

    for b in range(2):
        pre_ref[b] = jnp.zeros_like(pre_ref[b])
        pre_norm_ref[b] = jnp.zeros_like(pre_norm_ref[b])

    def prefix(b):
        pre_ref[b + 2] = pre_ref[b + 1] + own_ref[b]
        pre_norm_ref[b + 2] = pre_norm_ref[b + 1] + sum_ref[b]

    each(blocks - 2, prefix)

    def forward(turn, carry):
        p = (my_pair + turn) % pairs
        a, b = 2 * p, steps - 1 - 2 * p
        each(4, lambda u: q_arrived(pair_block(p, u)))
        tokens = (a, b)
        qs = [load(0, i) for i in tokens]
        vs = [load(2, i) for i in tokens]
        wide_b = b // 2

        def pair_of(part, j):
            return cat([load(part, 2 * j), load(part, 2 * j + 1)], 0)

        def fold(x, combine):
            while x.shape[1] > length:
                half = x.shape[1] // 2
                x = combine(x[:, :half], x[:, half:])
            return x

        s = mxu(qs[0], load(1, a), NT) * rate
        s_a = jnp.where(causal, s, big_negative)
        near_ref[0] = s_a
        s = mxu(qs[1], pair_of(1, wide_b), NT) * rate
        s_b = [s[:, :rows], jnp.where(causal, s[:, rows:], big_negative)]
        near_ref[1], near_ref[2] = s_b
        peaks = [fold(s_a, jnp.maximum), fold(jnp.maximum(*s_b), jnp.maximum)]

        def far_tile(m):
            first = m < p
            return first, jnp.where(first, a, b), jnp.where(first, m, m - p)

        for m in range(middle):
            first, i, j = far_tile(m)
            s = mxu(load(0, i), pair_of(1, j), NT) * rate
            score_ref[m] = s
            top = fold(s, jnp.maximum)
            peaks = [
                jnp.maximum(peaks[0], jnp.where(first, top, big_negative)),
                jnp.maximum(peaks[1], jnp.where(first, big_negative, top)),
            ]
        tops = [jnp.max(x, axis=-1, keepdims=True) for x in peaks]

        weight = jnp.exp2(near_ref[0] - tops[0])
        sums = [fold(weight, jnp.add)]
        accs = [mxu(weight.astype(bf16), vs[0], NN)]
        weight = jnp.exp2(cat([near_ref[1], near_ref[2]], 1) - tops[1])
        sums.append(fold(weight, jnp.add))
        accs.append(mxu(weight.astype(bf16), pair_of(2, wide_b), NN))
        for m in range(middle):
            first, i, j = far_tile(m)
            weight = jnp.exp2(score_ref[m] - jnp.where(first, tops[0], tops[1]))
            part = fold(weight, jnp.add)
            prod = mxu(weight.astype(bf16), pair_of(2, j), NN)
            sums = [sums[0] + jnp.where(first, part, 0.0), sums[1] + jnp.where(first, 0.0, part)]
            accs = [accs[0] + jnp.where(first, prod, 0.0), accs[1] + jnp.where(first, 0.0, prod)]
        teachers = [
            acc / jnp.sum(total, axis=-1, keepdims=True) for acc, total in zip(accs, sums)
        ]

        def halves_of(f):
            return [cat([f(x, 0), f(x, 1)], 0) for x in range(2)]

        def cut(x, half):
            return x[half * length:(half + 1) * length]

        last_far = score_ref[jnp.maximum(p - 1, 0), :length, 3 * length:]
        prevs = [
            cat([jnp.where(p > 0, last_far, big_negative), near_ref[0, length:, :length]], 0),
            cat([near_ref[1, :length, length:], near_ref[2, length:, :length]], 0),
        ]
        owns = [
            cat([near_ref[k, :length, :length], near_ref[k, length:, length:]], 0) for k in (0, 2)
        ]
        win_maxs = [
            jnp.max(jnp.maximum(prev, own), axis=-1, keepdims=True)
            for prev, own in zip(prevs, owns)
        ]
        p_prevs = [jnp.exp2(x - top) for x, top in zip(prevs, win_maxs)]
        p_owns = [jnp.exp2(x - top) for x, top in zip(owns, win_maxs)]
        win_dens = [jnp.sum(x + y, axis=-1, keepdims=True) for x, y in zip(p_prevs, p_owns)]
        p_wins = [cat([x.astype(bf16), y.astype(bf16)], 1) for x, y in zip(p_prevs, p_owns)]
        v_befores = [kv_all[jnp.maximum(2 * i - 1, 0), 1] for i in tokens]
        v_wins = [
            (cat([before, v[:length]], 0), v) for before, v in zip(v_befores, vs)
        ]
        win_nums = halves_of(lambda x, h: mxu(cut(p_wins[x], h), v_wins[x][h], NN))

        qfs = [
            half_softmax(mxu(cat([q, q, q], 1), wq_ref[...], NN), is_upper, halves) for q in qs
        ]
        states = [[pre_ref[2 * i], pre_ref[2 * i + 1]] for i in tokens]
        norms = [
            cat(
                [
                    jnp.broadcast_to(pre_norm_ref[2 * i + h], (length, 2 * features))
                    for h in range(2)
                ],
                0,
            )
            for i in tokens
        ]
        decays = [jnp.exp2(-top) for top in win_maxs]
        fars = halves_of(lambda x, h: wide_by_wide(cut(qfs[x], h), states[x][h], NN))
        dens = [
            win_den + decay * jnp.sum(qf * norm, axis=-1, keepdims=True)
            for win_den, decay, qf, norm in zip(win_dens, decays, qfs, norms)
        ]
        mixes = [
            (num + decay * far) / den
            for num, decay, far, den in zip(win_nums, decays, fars, dens)
        ]
        for i, mix in zip(tokens, mixes):
            mix_ref[pl.ds(2 * i, 2)] = mix.astype(bf16).reshape(2, length, width)
        each(4, lambda u: send_student(pair_block(p, u)))
        mismatches = [mix - teacher for mix, teacher in zip(mixes, teachers)]
        g_nums = [x / den for x, den in zip(mismatches, dens)]
        g_dens = [
            -jnp.sum(x * mix, axis=-1, keepdims=True) / den
            for x, mix, den in zip(mismatches, mixes, dens)
        ]
        lifts = [decay * qf for decay, qf in zip(decays, qfs)]
        pulled_norms = [lift * g_den for lift, g_den in zip(lifts, g_dens)]
        for x, i in enumerate(tokens):
            for h in range(2):
                gstate_ref[2 * i + h] = wide_by_wide(cut(lifts[x], h), cut(g_nums[x], h), TN)
                gnorm_ref[2 * i + h] = jnp.sum(cut(pulled_norms[x], h), axis=0, keepdims=True)
        pulled = halves_of(lambda x, h: wide_by_wide(cut(g_nums[x], h), states[x][h], NT))
        g_qfs = [
            decay * (pull + norm * g_den)
            for decay, pull, norm, g_den in zip(decays, pulled, norms, g_dens)
        ]
        d_qs = [qf * (g - half_sum(qf * g, halves)) for qf, g in zip(qfs, g_qfs)]
        gq_ref[...] += wide_by_exact(d_qs[0], qs[0], TN) + wide_by_exact(d_qs[1], qs[1], TN)
        return carry

    lax.fori_loop(0, pairs, forward, 0)
    own_grad[0] = (gq_ref[:features] - gq_ref[features:]).astype(bf16)
    send_grad(0)

    for b in range(blocks - 2, 1, -1):
        gstate_ref[b] = gstate_ref[b] + gstate_ref[b + 1]
        gnorm_ref[b] = gnorm_ref[b] + gnorm_ref[b + 1]

    def backward(group_of):
        ks, vs, kfs = ([f(i) for i in group_of] for f in (lambda i: load(1, i), lambda i: load(2, i), lambda i: kfeat_ref[i]))
        g_kfs = [
            cat(
                [
                    exact_by_wide(v[h * length:(h + 1) * length], gstate_ref[2 * i + h + 2], NT)
                    + gnorm_ref[2 * i + h + 2]
                    for h in range(2)
                ],
                0,
            )
            for i, v in zip(group_of, vs)
        ]
        d_ks = [kf * (g - half_sum(kf * g, halves)) for kf, g in zip(kfs, g_kfs)]
        return [wide_by_exact(d_k, k, TN) for d_k, k in zip(d_ks, ks)]

    gk = sum(backward(range(steps // 2)) + backward(range(steps // 2, steps - 1)))
    own_grad[1] = (gk[:features] - gk[features:]).astype(bf16)
    send_grad(1)
    relay_grad(0)
    relay_grad(1)

    def unless_mine(j, body):
        @pl.when(jnp.logical_not(native & (j == mine)))
        def _():
            body()

    each(blocks, lambda j: unless_mine(j, lambda: st_arrival(j).wait_recv()))
    st_turned[...] = jnp.transpose(st_all[...], (1, 0, 2))
    student_out = pltpu.make_async_copy(st_turned, student_hbm, out_sem.at[0])
    student_out.start()

    def gathered(j):
        relayed = native & ((j % group) // 2 == column)

        @pl.when(jnp.logical_not(relayed))
        def _():
            g_arrival(0, j).wait_recv()
            g_arrival(1, j).wait_recv()

    each(blocks, gathered)
    grad_out = pltpu.make_async_copy(gat_ref, grad_hbm, out_sem.at[1])
    grad_out.start()
    squares = jnp.zeros((8, width), f32)
    for j in range(blocks):
        piece = cat([gat_ref[0, j], gat_ref[1, j]], 0).astype(f32)
        piece = piece.reshape(2 * features // 8, 8, width)
        squares = squares + jnp.sum(piece * piece, axis=0)
    sq_ref[0] = squares
    swap = remote(
        sq_ref.at[0], sq_ref.at[1], sq_send.at[0], sq_recv.at[0], ctx=me, head=1 - side
    )
    swap.start()

    def settle(j):
        unless_mine(j, lambda: q_copy(j).wait_send())
        unless_own(j, lambda: st_copy(j).wait_send())

    each(blocks, settle)

    def settle_plane(z):
        @pl.when(jnp.logical_not(native & (z == plane)))
        def _():
            kv_land(z).wait_send()
            g_column(0, z).wait_send()
            g_column(1, z).wait_send()

        kv_across(z).wait_send()
        kv_share(landed_block(z), z).wait_send()
        kv_share(crossed_block(z), planes + z).wait_send()

    each(planes, settle_plane)

    @pl.when(native)
    def _():
        w_copy().wait_send()

        def relayed(n):
            j = (n // 2) * group + 2 * column + n % 2
            for d in range(1, group):
                g_pass(0, j, d).wait_send()
                g_pass(1, j, d).wait_send()

        each(2 * planes, relayed)

    swap.wait()
    entries = 2 * blocks * width * 2 * features
    total = jnp.sum(sq_ref[0] + sq_ref[1], keepdims=True)
    scale_ref[...] = jnp.broadcast_to(1.0 / jnp.sqrt(total / entries + 1e-06), (8, width))
    scale_out = pltpu.make_async_copy(scale_ref, scale_hbm, out_sem.at[2])
    scale_out.start()
    student_out.wait()
    grad_out.wait()
    scale_out.wait()


def finish_kernel(
    student_hbm, grad_hbm, scale_hbm, student_out, update_out,
    st_ref, grad_ref, scale_ref, update_ref, in_sem, out_sem,
):
    parts, blocks, features, width = grad_ref.shape
    chunks = in_sem.shape[0] - 2
    each_len = blocks // chunks
    fetches = [
        pltpu.make_async_copy(
            grad_hbm.at[:, pl.ds(n * each_len, each_len)],
            grad_ref.at[:, pl.ds(n * each_len, each_len)], in_sem.at[n],
        )
        for n in range(chunks)
    ]
    scale_in = pltpu.make_async_copy(scale_hbm, scale_ref, in_sem.at[chunks])
    student_in = pltpu.make_async_copy(student_hbm, st_ref, in_sem.at[chunks + 1])
    scale_in.start()
    for fetch in fetches:
        fetch.start()
    student_in.start()
    scale_in.wait()
    scale = scale_ref[:1]
    stores = []
    for n, fetch in enumerate(fetches):
        fetch.wait()
        for j in range(n * each_len, (n + 1) * each_len):
            piece = cat([grad_ref[0, j], grad_ref[1, j]], 0).astype(f32)
            update_ref[j] = piece.T * scale
        stores.append(
            pltpu.make_async_copy(
                update_ref.at[pl.ds(n * each_len, each_len)],
                update_out.at[pl.ds(n * each_len, each_len)], out_sem.at[n],
            )
        )
        stores[-1].start()
    student_in.wait()
    stores.append(pltpu.make_async_copy(st_ref, student_out, out_sem.at[chunks]))
    stores[-1].start()
    for store in stores:
        store.wait()


def whole_head(queries, keys, values, w):
    length, blocks, width = queries.shape
    planes = keys.shape[1]
    group = blocks // planes
    double = w.shape[2]
    half = double // 2
    rows, steps = 2 * length, blocks // 2
    vmem, dma = pltpu.VMEM, pltpu.SemaphoreType.DMA
    hbm = pl.BlockSpec(memory_space=pltpu.MemorySpace.HBM)
    limit = 67_043_328
    student, grads, scale = pl.pallas_call(
        head_kernel,
        out_shape=(
            jax.ShapeDtypeStruct((length, blocks, width), bf16),
            jax.ShapeDtypeStruct((2, blocks, half, width), bf16),
            jax.ShapeDtypeStruct((8, width), f32),
        ),
        in_specs=[hbm] * 4,
        out_specs=(hbm,) * 3,
        scratch_shapes=[
            vmem((length, blocks, width), bf16),
            vmem((length, planes, width), bf16),
            vmem((length, planes, width), bf16),
            vmem((width, double), f32),
            vmem((blocks, length, width), bf16),
            vmem((planes, 2, length, width), bf16),
            vmem((blocks, length, width), bf16),
            vmem((blocks, 2, length, width), bf16),
            vmem((blocks, length, width), bf16),
            vmem((length, blocks, width), bf16),
            vmem((blocks, length, width), bf16),
            vmem((2, half, width), bf16),
            vmem((2, blocks, half, width), bf16),
            vmem((2, 8, width), f32),
            vmem((8, width), f32),
            vmem((blocks, double, width), f32),
            vmem((blocks, 1, double), f32),
            vmem((blocks, double, width), f32),
            vmem((blocks, 1, double), f32),
            vmem((blocks // 4 - 1, rows, 2 * rows), f32),
            vmem((3, rows, rows), f32),
            vmem((steps, rows, double), f32),
            vmem((blocks, double, width), f32),
            vmem((blocks, 1, double), f32),
            vmem((3 * width, double), bf16),
            vmem((3 * width, double), bf16),
            vmem((double, width), f32),
            dma((blocks,)),
            dma((blocks,)),
            dma((planes,)),
            dma((blocks,)),
            dma((planes,)),
            dma((2 * planes,)),
            dma((3,)),
            dma((blocks,)),
            dma((blocks,)),
            dma((2, planes)),
            dma((2, blocks, group - 1)),
            dma((2, blocks)),
            dma((1,)),
            dma((1,)),
            dma((3,)),
            dma((1,)),
            dma((1,)),
            dma((3,)),
        ],
        compiler_params=pltpu.CompilerParams(
            vmem_limit_bytes=limit, collective_id=0, has_side_effects=True
        ),
    )(queries, keys, values, w)
    chunks = 4
    return pl.pallas_call(
        finish_kernel,
        out_shape=(
            jax.ShapeDtypeStruct((length, blocks, width), bf16),
            jax.ShapeDtypeStruct((blocks, width, double), f32),
        ),
        in_specs=[hbm] * 3,
        out_specs=(hbm,) * 2,
        scratch_shapes=[
            vmem((length, blocks, width), bf16),
            vmem((2, blocks, half, width), bf16),
            vmem((8, width), f32),
            vmem((blocks, width, double), f32),
            dma((chunks + 2,)),
            dma((chunks + 1,)),
        ],
        compiler_params=pltpu.CompilerParams(vmem_limit_bytes=limit),
    )(student, grads, scale)


def head_shards(queries, keys, values, feature_weight):
    return whole_head(queries, keys, values, feature_weight)


def shards(queries, keys, values, feature_weight):
    count = lax.axis_size("ctx")
    width = queries.shape[2]
    fits = queries.shape[1] == count and count == 4 * keys.shape[1] and lax.axis_size("head") == 2 and count % 4 == 0 and keys.shape[1] == 4 and count * queries.shape[0] <= 4096
    fits = fits and queries.shape[1] // keys.shape[1] % 4 == 0 and queries.shape[0] == width and feature_weight.shape[2] == width
    body = head_shards if fits else general_shards
    return body(queries, keys, values, feature_weight)


def solution(mesh):
    return jax.shard_map(
        shards,
        mesh=mesh,
        in_specs=(
            P("ctx", "head", None),
            P("ctx", "head", None),
            P("ctx", "head", None),
            P("head", None, None),
        ),
        out_specs=(P("ctx", "head", None), P("head", None, None)),
        check_vma=False,
    )
```

```python
import functools
import math

import jax
import jax.numpy as jnp
from jax import lax
from jax.experimental import pallas as pl
from jax.experimental.pallas import tpu as pltpu
from jax.sharding import PartitionSpec as P

precise = lax.Precision.HIGHEST
big_negative = -1e30


def shifted(shard, axis, by):
    devices = lax.axis_size(axis)
    pairs = [(i, i + by) for i in range(devices) if 0 <= i + by < devices]
    return lax.ppermute(shard, axis, pairs)


def carried_in(part, axis, combine, identity):
    count = lax.axis_size(axis)
    place = lax.axis_index(axis)
    ahead = count - 1 - place
    gathered = jax.tree.map(lambda a: lax.all_gather(a, axis), part)
    state = jax.tree.map(lambda a, e: jnp.zeros_like(a) + jnp.asarray(e, a.dtype), part, identity)

    def one(step, state):
        source = count - 1 - step
        return combine(
            state, jax.tree.map(lambda a: lax.dynamic_index_in_dim(a, source, 0, False), gathered)
        )

    return lax.fori_loop(0, ahead, one, state)


def feature_map(projection):
    return jnp.concatenate(
        [jax.nn.softmax(projection, axis=-1), jax.nn.softmax(-projection, axis=-1)], axis=-1
    )


def feature_pull(projection, upstream):
    half_len = upstream.shape[-1] // 2
    upper = jax.nn.softmax(projection, axis=-1)
    lower = jax.nn.softmax(-projection, axis=-1)
    grad_upper = upstream[..., :half_len]
    grad_lower = upstream[..., half_len:]
    upper_part = upper * (grad_upper - jnp.sum(upper * grad_upper, axis=-1, keepdims=True))
    lower_part = lower * (grad_lower - jnp.sum(lower * grad_lower, axis=-1, keepdims=True))
    return upper_part - lower_part


def add_pair(earlier, later):
    return (earlier[0] + later[0], earlier[1] + later[1])


def skip_block(carry_in):
    return carry_in


def general_shards(queries, keys, values, feature_weight):
    block_len, head_count, head_width = queries.shape
    kv_count = keys.shape[1]
    group_size = head_count // kv_count
    feature_len = feature_weight.shape[2] // 2
    my_block = lax.axis_index("ctx")
    score_scale = 1.0 / math.sqrt(head_width)
    grouped_q = queries.reshape(block_len, kv_count, group_size, head_width)
    maps_weight = feature_weight.reshape(kv_count, group_size, head_width, 2 * feature_len)
    query_map = maps_weight[..., :feature_len]
    key_map = maps_weight[..., feature_len:]
    query_pos = my_block * block_len + jnp.arange(block_len, dtype=jnp.int32)
    prev_start = (my_block - 1) * block_len
    last_row = my_block * block_len + block_len - 1
    initial = [
        jnp.full((kv_count, group_size, block_len), big_negative, jnp.float32),
        jnp.zeros((kv_count, group_size, block_len), jnp.float32),
        jnp.zeros((kv_count, group_size, block_len, head_width), jnp.float32),
    ]
    initial = initial + [
        jnp.zeros((kv_count, group_size, 2 * feature_len, head_width), jnp.float32),
        jnp.zeros((kv_count, group_size, 2 * feature_len), jnp.float32),
    ]
    initial = tuple(initial)
    piece_keys = lax.all_gather(keys, "ctx", axis=0, tiled=True)
    piece_values = lax.all_gather(values, "ctx", axis=0, tiled=True)
    piece_rows = piece_keys.shape[0]
    step_rows = math.gcd(piece_rows, 512)

    def attend(step_index, running):
        first_row = step_index * step_rows
        block_keys = lax.dynamic_slice_in_dim(piece_keys, step_index * step_rows, step_rows, 0)
        block_values = lax.dynamic_slice_in_dim(piece_values, step_index * step_rows, step_rows, 0)
        key_pos = first_row + jnp.arange(step_rows, dtype=jnp.int32)

        def compute(carry_in):
            row_max, running_sum, accumulated = (carry_in[0], carry_in[1], carry_in[2])
            scores = (
                jnp.einsum(
                    "tkgd,skd->kgts", grouped_q, block_keys, preferred_element_type=jnp.float32
                )
                * score_scale
            )
            allowed = key_pos[None, :] <= query_pos[:, None]
            scores = jnp.where(allowed, scores, big_negative)
            new_max = jnp.maximum(row_max, jnp.max(scores, axis=-1))
            attn_weight = jnp.where(allowed, jnp.exp(scores - new_max[..., None]), 0.0)
            factor = jnp.exp(row_max - new_max)
            running_sum = running_sum * factor + jnp.sum(attn_weight, axis=-1)
            accumulated = accumulated * factor[..., None] + jnp.einsum(
                "kgts,skd->kgtd",
                attn_weight.astype(jnp.bfloat16),
                block_values,
                preferred_element_type=jnp.float32,
            )
            result = [new_max, running_sum, accumulated] + list(carry_in[3:])
            in_state = (key_pos < prev_start).astype(jnp.float32)
            features = feature_map(
                jnp.einsum(
                    "skd,kgdf->kgsf", block_keys.astype(jnp.float32), key_map, precision=precise
                )
            )
            features = features * in_state[None, None, :, None]
            result[-2] = carry_in[-2] + jnp.einsum(
                "kgsf,skd->kgfd", features, block_values.astype(jnp.float32), precision=precise
            )
            result[-1] = carry_in[-1] + jnp.sum(features, axis=2)
            return tuple(result)

        return lax.cond(first_row <= last_row, compute, skip_block, running)

    folded = lax.fori_loop(0, piece_rows // step_rows, attend, initial)
    teacher = folded[2] / folded[1][..., None]
    stacked = jnp.stack([keys, values])
    moved = shifted(stacked, "ctx", 1)
    prev_keys, prev_values = (moved[0], moved[1])
    has_prev = (my_block > 0).astype(jnp.float32)
    window_keys = jnp.concatenate([prev_keys, keys], axis=0)
    window_values = jnp.concatenate([prev_values, values], axis=0)
    column = jnp.arange(2 * block_len, dtype=jnp.int32)
    row_index = jnp.arange(block_len, dtype=jnp.int32)
    allowed = (column[None, :] < block_len) & (my_block > 0) | (column[None, :] >= block_len) & (
        column[None, :] - block_len <= row_index[:, None]
    )
    scores = (
        jnp.einsum("tkgd,skd->kgts", grouped_q, window_keys, preferred_element_type=jnp.float32)
        * score_scale
    )
    scores = jnp.where(allowed, scores, big_negative)
    row_max = jnp.max(scores, axis=-1)
    window_weight = jnp.where(allowed, jnp.exp(scores - row_max[..., None]), 0.0)
    window_den = jnp.sum(window_weight, axis=-1)
    window_num = jnp.einsum(
        "kgts,skd->kgtd",
        window_weight.astype(jnp.bfloat16),
        window_values,
        preferred_element_type=jnp.float32,
    )
    key_proj = jnp.einsum(
        "skd,kgdf->kgsf", prev_keys.astype(jnp.float32), key_map, precision=precise
    )
    state, norm = (folded[-2], folded[-1])
    query_proj = jnp.einsum(
        "tkgd,kgdf->kgtf", grouped_q.astype(jnp.float32), query_map, precision=precise
    )
    query_feats = feature_map(query_proj)
    decay = jnp.exp(-row_max)
    far_num = decay[..., None] * jnp.einsum(
        "kgtf,kgfd->kgtd", query_feats, state, precision=precise
    )
    far_den = decay * jnp.einsum("kgtf,kgf->kgt", query_feats, norm, precision=precise)
    denominator = window_den + far_den
    mix = (window_num + far_num) / denominator[..., None]
    student = jnp.transpose(mix.astype(jnp.bfloat16), (2, 0, 1, 3)).reshape(
        block_len, head_count, head_width
    )
    mismatch = mix - teacher
    grad_num = mismatch / denominator[..., None]
    grad_den = -jnp.sum(mismatch * mix, axis=-1) / denominator
    lifted = decay[..., None] * query_feats
    grad_state = jnp.einsum("kgtf,kgtd->kgfd", lifted, grad_num, precision=precise)
    grad_norm = jnp.einsum("kgtf,kgt->kgf", lifted, grad_den, precision=precise)
    grad_qfeat = decay[..., None] * (
        jnp.einsum("kgfd,kgtd->kgtf", state, grad_num, precision=precise)
        + norm[:, :, None, :] * grad_den[..., None]
    )
    later_state, later_norm = carried_in(
        (grad_state, grad_norm),
        "ctx",
        add_pair,
        (jnp.zeros_like(grad_state), jnp.zeros_like(grad_norm)),
    )
    grad_kfeat = (
        jnp.einsum(
            "kgfd,skd->kgsf", later_state, prev_values.astype(jnp.float32), precision=precise
        )
        + later_norm[:, :, None, :]
    ) * has_prev
    grad_query = jnp.einsum(
        "tkgd,kgtf->kgdf",
        grouped_q.astype(jnp.float32),
        feature_pull(query_proj, grad_qfeat),
        precision=precise,
    )
    grad_key = jnp.einsum(
        "skd,kgsf->kgdf",
        prev_keys.astype(jnp.float32),
        feature_pull(key_proj, grad_kfeat),
        precision=precise,
    )
    gradients = jnp.concatenate([grad_query, grad_key], axis=-1).reshape(
        head_count, head_width, 2 * feature_len
    )
    entry_count = gradients.size * lax.axis_size("head")
    summed = lax.psum(gradients, "ctx")
    squares = lax.psum(jnp.sum(summed * summed), "head")
    update = summed / jnp.sqrt(squares / entry_count + 1e-06)
    return (student, update)


f32, bf16 = jnp.float32, jnp.bfloat16
NN = (((1,), (0,)), ((), ()))
NT = (((1,), (1,)), ((), ()))
TN = (((0,), (0,)), ((), ()))


def mxu(a, b, dims):
    return lax.dot_general(a, b, dims, preferred_element_type=f32)


def split(x, pieces):
    out = []
    for _ in range(pieces):
        piece = x.astype(bf16)
        out.append(piece)
        x = x - piece.astype(f32)
    return out


def cat(parts, axis):
    return jnp.concatenate(parts, axis=axis)


def exact_by_wide(a, b, dims):
    return mxu(cat([a, a], dims[0][0][0]), cat(split(b, 2), dims[0][1][0]), dims)


def wide_by_exact(a, b, dims):
    return mxu(cat(split(a, 2), dims[0][0][0]), cat([b, b], dims[0][1][0]), dims)


def wide_by_wide(a, b, dims):
    a_hi, a_lo = split(a, 2)
    b_hi, b_lo = split(b, 2)
    return mxu(
        cat([a_hi, a_hi, a_lo], dims[0][0][0]), cat([b_hi, b_lo, b_hi], dims[0][1][0]), dims
    )


def half_sum(x, halves):
    return wide_by_exact(x, halves, NN)


def half_softmax(u, is_upper, halves):
    top = jnp.max(jnp.where(is_upper, u, big_negative), axis=-1, keepdims=True)
    low = jnp.max(jnp.where(is_upper, big_negative, u), axis=-1, keepdims=True)
    e = jnp.exp(u - jnp.where(is_upper, top, low))
    return e / half_sum(e, halves)


def remote(src, dst, send_sem, recv_sem, **where):
    return pltpu.make_async_remote_copy(
        src_ref=src,
        dst_ref=dst,
        send_sem=send_sem,
        recv_sem=recv_sem,
        device_id=where,
        device_id_type=pl.DeviceIdType.MESH,
    )


def each(count, body):
    def step(index, carry):
        body(index)
        return carry

    lax.fori_loop(0, count, step, 0)


def head_kernel(
    q_hbm, k_hbm, v_hbm, w_hbm, student_hbm, grad_hbm, scale_hbm,
    q_raw, k_raw, v_raw, w_ref, qt_ref, kvt_ref, q_all, kv_all, st_all, st_turned, mix_ref,
    own_grad, gat_ref, sq_ref, scale_ref, own_ref, sum_ref, pre_ref, pre_norm_ref,
    score_ref, near_ref, kfeat_ref, gstate_ref, gnorm_ref, wq_ref, wk_ref, gq_ref,
    q_send, q_recv, kv_send, kv_recv, kv_cross, kv_sibling, local_sem, st_send, st_recv,
    g_send, g_relay, g_recv, sq_send, sq_recv, fetch_sem, w_send, w_recv, out_sem,
):
    blocks, length, width = qt_ref.shape
    planes = kvt_ref.shape[0]
    group = blocks // planes
    me, side = lax.axis_index("ctx"), lax.axis_index("head")
    plane, spot = me // group, me % group
    row, column = spot // 2, spot % 2
    native = row == side
    mine = plane * group + 2 * column + side
    features = w_ref.shape[1] // 2
    rows = 2 * length
    steps, pairs = blocks // 2, blocks // 4
    middle = pairs - 1

    def pair_block(p, u):
        return jnp.where(u < 2, 4 * p + u, blocks - 4 - 4 * p + u)

    my_pair = jnp.where(row == 0, plane, planes - 1 - plane)
    barrier = pltpu.get_barrier_semaphore()

    def greet(t, h):
        pl.semaphore_signal(
            barrier, inc=1, device_id={"ctx": t, "head": h}, device_id_type=pl.DeviceIdType.MESH
        )

    def greet_side(d):
        t = (me + d) % blocks

        @pl.when(jnp.logical_not(native & (t == me)))
        def _():
            greet(t, row)

    each(blocks, greet_side)
    each(blocks // 2, lambda n: greet((n // 2) * group + 2 * side + n % 2, 1 - row))
    fetches = [
        pltpu.make_async_copy(src, dst, fetch_sem.at[n])
        for n, (src, dst) in enumerate([(k_hbm, k_raw), (v_hbm, v_raw), (q_hbm, q_raw)])
    ]
    for fetch in fetches:
        fetch.start()
    own_w = pltpu.make_async_copy(w_hbm.at[mine], w_ref, local_sem.at[2])

    @pl.when(native)
    def _():
        own_w.start()

    def flip(index, d):
        bit = 1
        while bit <= d:
            if d & bit:
                index = index + bit - 2 * bit * ((index // bit) % 2)
            bit *= 2
        return index

    def w_copy():
        other = plane * group + 2 * column + 1 - side
        return remote(w_hbm.at[other], w_ref, w_send.at[0], w_recv.at[0], ctx=me, head=1 - side)

    def kv_land(g):
        return remote(
            kvt_ref.at[g], kv_all.at[me], kv_send.at[g], kv_recv.at[me],
            ctx=g * group + 2 * side + column, head=row,
        )

    def landed_block(z):
        return z * group + 2 * side + column

    def crossed_block(z):
        return z * group + 2 * side + 1 - column

    def kv_across(z):
        block = landed_block(z)
        return remote(
            kv_all.at[block], kv_all.at[block], kv_cross.at[z], kv_recv.at[block],
            ctx=plane * group + 2 * row + 1 - column, head=side,
        )

    def kv_share(block, n):
        return remote(
            kv_all.at[block], kv_all.at[block], kv_sibling.at[n], kv_recv.at[block],
            ctx=me, head=1 - side,
        )

    def q_copy(j):
        return remote(
            qt_ref.at[j], q_all.at[me], q_send.at[j], q_recv.at[me],
            ctx=(j // group) * group + 2 * side + (j % group) // 2, head=j % 2,
        )

    def q_arrival(b):
        return remote(qt_ref.at[b], q_all.at[b], q_send.at[b], q_recv.at[b], ctx=b, head=row)

    def kv_arrival(b):
        return remote(kv_all.at[b], kv_all.at[b], kv_send.at[0], kv_recv.at[b], ctx=b, head=row)

    def st_copy(b):
        return remote(mix_ref.at[b], st_all.at[mine], st_send.at[b], st_recv.at[mine], ctx=b, head=row)

    def st_arrival(j):
        return remote(mix_ref.at[j], st_all.at[j], st_send.at[j], st_recv.at[j], ctx=j, head=row)

    def g_column(part, z):
        return remote(
            own_grad.at[part], gat_ref.at[part, mine], g_send.at[part, z], g_recv.at[part, mine],
            ctx=z * group + spot, head=row,
        )

    def g_pass(part, j, d):
        piece = gat_ref.at[part, j]
        return remote(
            piece, piece, g_relay.at[part, j, d - 1], g_recv.at[part, j],
            ctx=plane * group + flip(spot, d), head=side,
        )

    def g_arrival(part, j):
        piece = gat_ref.at[part, j]
        return remote(piece, piece, g_send.at[part, 0], g_recv.at[part, j], ctx=j, head=row)

    def unless_own(b, body):
        @pl.when(jnp.logical_not(native & (b == me)))
        def _():
            body()

    rate = math.log2(math.e) / math.sqrt(width)
    lane = lax.broadcasted_iota(jnp.int32, (rows, 2 * features), 1)
    is_upper = lane < features
    row_half = lax.broadcasted_iota(jnp.int32, (2 * features, 2 * features), 0) < features
    col_half = lax.broadcasted_iota(jnp.int32, (2 * features, 2 * features), 1) < features
    halves = jnp.where(row_half == col_half, 1.0, 0.0).astype(bf16)
    square = (rows, rows)
    causal = lax.broadcasted_iota(jnp.int32, square, 1) <= lax.broadcasted_iota(jnp.int32, square, 0)
    for part, (fetch, raw) in enumerate(zip(fetches, (k_raw, v_raw))):
        fetch.wait()
        kvt_ref[:, part] = jnp.transpose(raw[...], (1, 0, 2))
    own_kv = pltpu.make_async_copy(kvt_ref.at[plane], kv_all.at[me], local_sem.at[0])

    @pl.when(native)
    def _():
        own_kv.start()

    pl.semaphore_wait(barrier, jnp.where(native, 3 * blocks // 2 - 1, 3 * blocks // 2))
    for d in range(planes):
        g = flip(plane, d)
        if d == 0:
            @pl.when(jnp.logical_not(native))
            def _():
                kv_land(g).start()
        else:
            kv_land(g).start()

    @pl.when(native)
    def _():
        w_copy().start()

    fetches[2].wait()
    qt_ref[...] = jnp.transpose(q_raw[...], (1, 0, 2))
    own_q = pltpu.make_async_copy(qt_ref.at[mine], q_all.at[me], local_sem.at[1])

    @pl.when(native)
    def _():
        own_q.start()
        own_kv.wait()

    def land(d):
        z = flip(plane, d)
        block = landed_block(z)
        unless_own(block, lambda: kv_arrival(block).wait_recv())
        kv_across(z).start()
        kv_share(block, z).start()

    def cross(d):
        z = flip(plane, d)
        block = crossed_block(z)
        kv_arrival(block).wait_recv()
        kv_share(block, planes + z).start()

    def load(part, i):
        if part == 0:
            return q_all[pl.ds(2 * i, 2)].reshape(rows, width)
        return kv_all[pl.ds(2 * i, 2), part - 1].reshape(rows, width)

    def q_arrived(b):
        unless_own(b, lambda: q_arrival(b).wait_recv())

    def kv_arrived(b):
        @pl.when((b % group) // 2 != side)
        def _():
            kv_arrival(b).wait_recv()

    def send_student(b):
        unless_own(b, lambda: st_copy(b).start())

        @pl.when(native & (b == me))
        def _():
            st_all[mine] = mix_ref[me]

    def send_grad(part):
        for d in range(planes):
            z = flip(plane, d)
            if d == 0:
                @pl.when(native)
                def _():
                    gat_ref[part, mine] = own_grad[part]

                @pl.when(jnp.logical_not(native))
                def _():
                    g_column(part, z).start()
            else:
                g_column(part, z).start()

    def relay_grad(part):
        @pl.when(native)
        def _():
            for z in range(planes):
                for h in range(2):
                    j = flip(plane, z) * group + 2 * column + h

                    @pl.when(j != mine)
                    def _():
                        g_arrival(part, j).wait_recv()

                    for d in range(1, group):
                        g_pass(part, j, d).start()

    def key_side(pair):
        each(4, lambda u: kv_arrived(4 * pair + u))
        steps_of = (2 * pair, 2 * pair + 1)
        ks, vs = ([load(part, i) for i in steps_of] for part in (1, 2))
        kfs = [
            half_softmax(mxu(cat([k, k, k], 1), wk_ref[...], NN), is_upper, halves) for k in ks
        ]
        for i, kf, v in zip(steps_of, kfs, vs):
            kfeat_ref[i] = kf
            for h in range(2):
                part = kf[h * length:(h + 1) * length]
                own_ref[2 * i + h] = wide_by_exact(part, v[h * length:(h + 1) * length], TN)
                sum_ref[2 * i + h] = jnp.sum(part, axis=0, keepdims=True)

    def push(n):
        p = (my_pair + pairs - n // group) % pairs
        j = jnp.where(side == 0, p, planes - 1 - p) * group + n % group

        @pl.when(jnp.logical_not(native & (j == mine)))
        def _():
            q_copy(j).start()

    def plane_keys(z):
        each(group // 4, lambda u: key_side(z * (group // 4) + u))

    def push_turns(first, last):
        each((last - first) * group, lambda n: push(first * group + n))

    push_turns(0, 1)
    land(0)
    @pl.when(native)
    def _():
        own_w.wait()

    @pl.when(jnp.logical_not(native))
    def _():
        w_copy().wait_recv()

    w = w_ref[...]
    wq, wk = w[:, :features], w[:, features:]
    wq_ref[...] = cat(split(cat([wq, -wq], 1), 3), 0)
    wk_ref[...] = cat(split(cat([wk, -wk], 1), 3), 0)
    gq_ref[...] = jnp.zeros_like(gq_ref)
    land(1)
    cross(0)
    land(2)
    cross(1)
    land(3)
    push_turns(1, 2)
    plane_keys(flip(plane, 0))
    cross(2)
    plane_keys(flip(plane, 1))
    cross(3)
    push_turns(2, pairs)
    plane_keys(flip(plane, 2))
    plane_keys(flip(plane, 3))

    @pl.when(native)
    def _():
        own_q.wait()

    for b in range(2):
        pre_ref[b] = jnp.zeros_like(pre_ref[b])
        pre_norm_ref[b] = jnp.zeros_like(pre_norm_ref[b])

    def prefix(b):
        pre_ref[b + 2] = pre_ref[b + 1] + own_ref[b]
        pre_norm_ref[b + 2] = pre_norm_ref[b + 1] + sum_ref[b]

    each(blocks - 2, prefix)

    def forward(turn, carry):
        p = (my_pair + turn) % pairs
        a, b = 2 * p, steps - 1 - 2 * p
        each(4, lambda u: q_arrived(pair_block(p, u)))
        tokens = (a, b)
        qs = [load(0, i) for i in tokens]
        vs = [load(2, i) for i in tokens]
        wide_b = b // 2

        def pair_of(part, j):
            return cat([load(part, 2 * j), load(part, 2 * j + 1)], 0)

        def fold(x, combine):
            while x.shape[1] > length:
                half = x.shape[1] // 2
                x = combine(x[:, :half], x[:, half:])
            return x

        s = mxu(qs[0], load(1, a), NT) * rate
        s_a = jnp.where(causal, s, big_negative)
        near_ref[0] = s_a
        s = mxu(qs[1], pair_of(1, wide_b), NT) * rate
        s_b = [s[:, :rows], jnp.where(causal, s[:, rows:], big_negative)]
        near_ref[1], near_ref[2] = s_b
        peaks = [fold(s_a, jnp.maximum), fold(jnp.maximum(*s_b), jnp.maximum)]

        def far_tile(m):
            first = m < p
            return first, jnp.where(first, a, b), jnp.where(first, m, m - p)

        for m in range(middle):
            first, i, j = far_tile(m)
            s = mxu(load(0, i), pair_of(1, j), NT) * rate
            score_ref[m] = s
            top = fold(s, jnp.maximum)
            peaks = [
                jnp.maximum(peaks[0], jnp.where(first, top, big_negative)),
                jnp.maximum(peaks[1], jnp.where(first, big_negative, top)),
            ]
        tops = [jnp.max(x, axis=-1, keepdims=True) for x in peaks]

        weight = jnp.exp2(near_ref[0] - tops[0])
        sums = [fold(weight, jnp.add)]
        accs = [mxu(weight.astype(bf16), vs[0], NN)]
        weight = jnp.exp2(cat([near_ref[1], near_ref[2]], 1) - tops[1])
        sums.append(fold(weight, jnp.add))
        accs.append(mxu(weight.astype(bf16), pair_of(2, wide_b), NN))
        for m in range(middle):
            first, i, j = far_tile(m)
            weight = jnp.exp2(score_ref[m] - jnp.where(first, tops[0], tops[1]))
            part = fold(weight, jnp.add)
            prod = mxu(weight.astype(bf16), pair_of(2, j), NN)
            sums = [sums[0] + jnp.where(first, part, 0.0), sums[1] + jnp.where(first, 0.0, part)]
            accs = [accs[0] + jnp.where(first, prod, 0.0), accs[1] + jnp.where(first, 0.0, prod)]
        teachers = [
            acc / jnp.sum(total, axis=-1, keepdims=True) for acc, total in zip(accs, sums)
        ]

        def halves_of(f):
            return [cat([f(x, 0), f(x, 1)], 0) for x in range(2)]

        def cut(x, half):
            return x[half * length:(half + 1) * length]

        last_far = score_ref[jnp.maximum(p - 1, 0), :length, 3 * length:]
        prevs = [
            cat([jnp.where(p > 0, last_far, big_negative), near_ref[0, length:, :length]], 0),
            cat([near_ref[1, :length, length:], near_ref[2, length:, :length]], 0),
        ]
        owns = [
            cat([near_ref[k, :length, :length], near_ref[k, length:, length:]], 0) for k in (0, 2)
        ]
        win_maxs = [
            jnp.max(jnp.maximum(prev, own), axis=-1, keepdims=True)
            for prev, own in zip(prevs, owns)
        ]
        p_prevs = [jnp.exp2(x - top) for x, top in zip(prevs, win_maxs)]
        p_owns = [jnp.exp2(x - top) for x, top in zip(owns, win_maxs)]
        win_dens = [jnp.sum(x + y, axis=-1, keepdims=True) for x, y in zip(p_prevs, p_owns)]
        p_wins = [cat([x.astype(bf16), y.astype(bf16)], 1) for x, y in zip(p_prevs, p_owns)]
        v_befores = [kv_all[jnp.maximum(2 * i - 1, 0), 1] for i in tokens]
        v_wins = [
            (cat([before, v[:length]], 0), v) for before, v in zip(v_befores, vs)
        ]
        win_nums = halves_of(lambda x, h: mxu(cut(p_wins[x], h), v_wins[x][h], NN))

        qfs = [
            half_softmax(mxu(cat([q, q, q], 1), wq_ref[...], NN), is_upper, halves) for q in qs
        ]
        states = [[pre_ref[2 * i], pre_ref[2 * i + 1]] for i in tokens]
        norms = [
            cat(
                [
                    jnp.broadcast_to(pre_norm_ref[2 * i + h], (length, 2 * features))
                    for h in range(2)
                ],
                0,
            )
            for i in tokens
        ]
        decays = [jnp.exp2(-top) for top in win_maxs]
        fars = halves_of(lambda x, h: wide_by_wide(cut(qfs[x], h), states[x][h], NN))
        dens = [
            win_den + decay * jnp.sum(qf * norm, axis=-1, keepdims=True)
            for win_den, decay, qf, norm in zip(win_dens, decays, qfs, norms)
        ]
        mixes = [
            (num + decay * far) / den
            for num, decay, far, den in zip(win_nums, decays, fars, dens)
        ]
        for i, mix in zip(tokens, mixes):
            mix_ref[pl.ds(2 * i, 2)] = mix.astype(bf16).reshape(2, length, width)
        @pl.when(turn < pairs - 1)
        def _():
            each(4, lambda u: send_student(pair_block(p, u)))

        mismatches = [mix - teacher for mix, teacher in zip(mixes, teachers)]
        g_nums = [x / den for x, den in zip(mismatches, dens)]
        g_dens = [
            -jnp.sum(x * mix, axis=-1, keepdims=True) / den
            for x, mix, den in zip(mismatches, mixes, dens)
        ]
        lifts = [decay * qf for decay, qf in zip(decays, qfs)]
        pulled_norms = [lift * g_den for lift, g_den in zip(lifts, g_dens)]
        for x, i in enumerate(tokens):
            for h in range(2):
                gstate_ref[2 * i + h] = wide_by_wide(cut(lifts[x], h), cut(g_nums[x], h), TN)
                gnorm_ref[2 * i + h] = jnp.sum(cut(pulled_norms[x], h), axis=0, keepdims=True)
        pulled = halves_of(lambda x, h: wide_by_wide(cut(g_nums[x], h), states[x][h], NT))
        g_qfs = [
            decay * (pull + norm * g_den)
            for decay, pull, norm, g_den in zip(decays, pulled, norms, g_dens)
        ]
        d_qs = [qf * (g - half_sum(qf * g, halves)) for qf, g in zip(qfs, g_qfs)]
        gq_ref[...] += wide_by_exact(d_qs[0], qs[0], TN) + wide_by_exact(d_qs[1], qs[1], TN)
        return carry

    lax.fori_loop(0, pairs, forward, 0)
    own_grad[0] = (gq_ref[:features] - gq_ref[features:]).astype(bf16)
    send_grad(0)

    for b in range(blocks - 2, 1, -1):
        gstate_ref[b] = gstate_ref[b] + gstate_ref[b + 1]
        gnorm_ref[b] = gnorm_ref[b] + gnorm_ref[b + 1]

    def backward(group_of):
        ks, vs, kfs = ([f(i) for i in group_of] for f in (lambda i: load(1, i), lambda i: load(2, i), lambda i: kfeat_ref[i]))
        g_kfs = [
            cat(
                [
                    exact_by_wide(v[h * length:(h + 1) * length], gstate_ref[2 * i + h + 2], NT)
                    + gnorm_ref[2 * i + h + 2]
                    for h in range(2)
                ],
                0,
            )
            for i, v in zip(group_of, vs)
        ]
        d_ks = [kf * (g - half_sum(kf * g, halves)) for kf, g in zip(kfs, g_kfs)]
        return [wide_by_exact(d_k, k, TN) for d_k, k in zip(d_ks, ks)]

    gk = sum(backward(range(steps // 2)) + backward(range(steps // 2, steps - 1)))
    own_grad[1] = (gk[:features] - gk[features:]).astype(bf16)
    send_grad(1)
    each(4, lambda u: send_student(pair_block((my_pair + pairs - 1) % pairs, u)))
    relay_grad(0)
    relay_grad(1)

    def unless_mine(j, body):
        @pl.when(jnp.logical_not(native & (j == mine)))
        def _():
            body()

    each(blocks, lambda j: unless_mine(j, lambda: st_arrival(j).wait_recv()))
    st_turned[...] = jnp.transpose(st_all[...], (1, 0, 2))
    student_out = pltpu.make_async_copy(st_turned, student_hbm, out_sem.at[0])
    student_out.start()

    def gathered(j):
        relayed = native & ((j % group) // 2 == column)

        @pl.when(jnp.logical_not(relayed))
        def _():
            g_arrival(0, j).wait_recv()
            g_arrival(1, j).wait_recv()

    each(blocks, gathered)
    grad_out = pltpu.make_async_copy(gat_ref, grad_hbm, out_sem.at[1])
    grad_out.start()
    squares = jnp.zeros((8, width), f32)
    for j in range(blocks):
        piece = cat([gat_ref[0, j], gat_ref[1, j]], 0).astype(f32)
        piece = piece.reshape(2 * features // 8, 8, width)
        squares = squares + jnp.sum(piece * piece, axis=0)
    sq_ref[0] = squares
    swap = remote(
        sq_ref.at[0], sq_ref.at[1], sq_send.at[0], sq_recv.at[0], ctx=me, head=1 - side
    )
    swap.start()

    def settle(j):
        unless_mine(j, lambda: q_copy(j).wait_send())
        unless_own(j, lambda: st_copy(j).wait_send())

    each(blocks, settle)

    def settle_plane(z):
        @pl.when(jnp.logical_not(native & (z == plane)))
        def _():
            kv_land(z).wait_send()
            g_column(0, z).wait_send()
            g_column(1, z).wait_send()

        kv_across(z).wait_send()
        kv_share(landed_block(z), z).wait_send()
        kv_share(crossed_block(z), planes + z).wait_send()

    each(planes, settle_plane)

    @pl.when(native)
    def _():
        w_copy().wait_send()

        def relayed(n):
            j = (n // 2) * group + 2 * column + n % 2
            for d in range(1, group):
                g_pass(0, j, d).wait_send()
                g_pass(1, j, d).wait_send()

        each(2 * planes, relayed)

    swap.wait()
    entries = 2 * blocks * width * 2 * features
    total = jnp.sum(sq_ref[0] + sq_ref[1], keepdims=True)
    scale_ref[...] = jnp.broadcast_to(1.0 / jnp.sqrt(total / entries + 1e-06), (8, width))
    scale_out = pltpu.make_async_copy(scale_ref, scale_hbm, out_sem.at[2])
    scale_out.start()
    student_out.wait()
    grad_out.wait()
    scale_out.wait()


def finish_kernel(
    student_hbm, grad_hbm, scale_hbm, student_out, update_out,
    st_ref, grad_ref, scale_ref, update_ref, in_sem, out_sem,
):
    parts, blocks, features, width = grad_ref.shape
    chunks = in_sem.shape[0] - 2
    each_len = blocks // chunks
    fetches = [
        pltpu.make_async_copy(
            grad_hbm.at[:, pl.ds(n * each_len, each_len)],
            grad_ref.at[:, pl.ds(n * each_len, each_len)], in_sem.at[n],
        )
        for n in range(chunks)
    ]
    scale_in = pltpu.make_async_copy(scale_hbm, scale_ref, in_sem.at[chunks])
    student_in = pltpu.make_async_copy(student_hbm, st_ref, in_sem.at[chunks + 1])
    scale_in.start()
    for fetch in fetches:
        fetch.start()
    student_in.start()
    scale_in.wait()
    scale = scale_ref[:1]
    stores = []
    for n, fetch in enumerate(fetches):
        fetch.wait()
        for j in range(n * each_len, (n + 1) * each_len):
            piece = cat([grad_ref[0, j], grad_ref[1, j]], 0).astype(f32)
            update_ref[j] = piece.T * scale
        stores.append(
            pltpu.make_async_copy(
                update_ref.at[pl.ds(n * each_len, each_len)],
                update_out.at[pl.ds(n * each_len, each_len)], out_sem.at[n],
            )
        )
        stores[-1].start()
    student_in.wait()
    stores.append(pltpu.make_async_copy(st_ref, student_out, out_sem.at[chunks]))
    stores[-1].start()
    for store in stores:
        store.wait()


def whole_head(queries, keys, values, w):
    length, blocks, width = queries.shape
    planes = keys.shape[1]
    group = blocks // planes
    double = w.shape[2]
    half = double // 2
    rows, steps = 2 * length, blocks // 2
    vmem, dma = pltpu.VMEM, pltpu.SemaphoreType.DMA
    hbm = pl.BlockSpec(memory_space=pltpu.MemorySpace.HBM)
    limit = 67_043_328
    student, grads, scale = pl.pallas_call(
        head_kernel,
        out_shape=(
            jax.ShapeDtypeStruct((length, blocks, width), bf16),
            jax.ShapeDtypeStruct((2, blocks, half, width), bf16),
            jax.ShapeDtypeStruct((8, width), f32),
        ),
        in_specs=[hbm] * 4,
        out_specs=(hbm,) * 3,
        scratch_shapes=[
            vmem((length, blocks, width), bf16),
            vmem((length, planes, width), bf16),
            vmem((length, planes, width), bf16),
            vmem((width, double), f32),
            vmem((blocks, length, width), bf16),
            vmem((planes, 2, length, width), bf16),
            vmem((blocks, length, width), bf16),
            vmem((blocks, 2, length, width), bf16),
            vmem((blocks, length, width), bf16),
            vmem((length, blocks, width), bf16),
            vmem((blocks, length, width), bf16),
            vmem((2, half, width), bf16),
            vmem((2, blocks, half, width), bf16),
            vmem((2, 8, width), f32),
            vmem((8, width), f32),
            vmem((blocks, double, width), f32),
            vmem((blocks, 1, double), f32),
            vmem((blocks, double, width), f32),
            vmem((blocks, 1, double), f32),
            vmem((blocks // 4 - 1, rows, 2 * rows), f32),
            vmem((3, rows, rows), f32),
            vmem((steps, rows, double), f32),
            vmem((blocks, double, width), f32),
            vmem((blocks, 1, double), f32),
            vmem((3 * width, double), bf16),
            vmem((3 * width, double), bf16),
            vmem((double, width), f32),
            dma((blocks,)),
            dma((blocks,)),
            dma((planes,)),
            dma((blocks,)),
            dma((planes,)),
            dma((2 * planes,)),
            dma((3,)),
            dma((blocks,)),
            dma((blocks,)),
            dma((2, planes)),
            dma((2, blocks, group - 1)),
            dma((2, blocks)),
            dma((1,)),
            dma((1,)),
            dma((3,)),
            dma((1,)),
            dma((1,)),
            dma((3,)),
        ],
        compiler_params=pltpu.CompilerParams(
            vmem_limit_bytes=limit, collective_id=0, has_side_effects=True
        ),
    )(queries, keys, values, w)
    chunks = 4
    return pl.pallas_call(
        finish_kernel,
        out_shape=(
            jax.ShapeDtypeStruct((length, blocks, width), bf16),
            jax.ShapeDtypeStruct((blocks, width, double), f32),
        ),
        in_specs=[hbm] * 3,
        out_specs=(hbm,) * 2,
        scratch_shapes=[
            vmem((length, blocks, width), bf16),
            vmem((2, blocks, half, width), bf16),
            vmem((8, width), f32),
            vmem((blocks, width, double), f32),
            dma((chunks + 2,)),
            dma((chunks + 1,)),
        ],
        compiler_params=pltpu.CompilerParams(vmem_limit_bytes=limit),
    )(student, grads, scale)


def head_shards(queries, keys, values, feature_weight):
    return whole_head(queries, keys, values, feature_weight)


def shards(queries, keys, values, feature_weight):
    count = lax.axis_size("ctx")
    width = queries.shape[2]
    fits = queries.shape[1] == count and count == 4 * keys.shape[1] and lax.axis_size("head") == 2 and count % 4 == 0 and keys.shape[1] == 4 and count * queries.shape[0] <= 4096
    fits = fits and queries.shape[1] // keys.shape[1] % 4 == 0 and queries.shape[0] == width and feature_weight.shape[2] == width
    body = head_shards if fits else general_shards
    return body(queries, keys, values, feature_weight)


def solution(mesh):
    return jax.shard_map(
        shards,
        mesh=mesh,
        in_specs=(
            P("ctx", "head", None),
            P("ctx", "head", None),
            P("ctx", "head", None),
            P("head", None, None),
        ),
        out_specs=(P("ctx", "head", None), P("head", None, None)),
        check_vma=False,
    )
```

```python
import functools
import math

import jax
import jax.numpy as jnp
from jax import lax
from jax.experimental import pallas as pl
from jax.experimental.pallas import tpu as pltpu
from jax.sharding import PartitionSpec as P

precise = lax.Precision.HIGHEST
big_negative = -1e30


def shifted(shard, axis, by):
    devices = lax.axis_size(axis)
    pairs = [(i, i + by) for i in range(devices) if 0 <= i + by < devices]
    return lax.ppermute(shard, axis, pairs)


def carried_in(part, axis, combine, identity):
    count = lax.axis_size(axis)
    place = lax.axis_index(axis)
    ahead = count - 1 - place
    gathered = jax.tree.map(lambda a: lax.all_gather(a, axis), part)
    state = jax.tree.map(lambda a, e: jnp.zeros_like(a) + jnp.asarray(e, a.dtype), part, identity)

    def one(step, state):
        source = count - 1 - step
        return combine(
            state, jax.tree.map(lambda a: lax.dynamic_index_in_dim(a, source, 0, False), gathered)
        )

    return lax.fori_loop(0, ahead, one, state)


def feature_map(projection):
    return jnp.concatenate(
        [jax.nn.softmax(projection, axis=-1), jax.nn.softmax(-projection, axis=-1)], axis=-1
    )


def feature_pull(projection, upstream):
    half_len = upstream.shape[-1] // 2
    upper = jax.nn.softmax(projection, axis=-1)
    lower = jax.nn.softmax(-projection, axis=-1)
    grad_upper = upstream[..., :half_len]
    grad_lower = upstream[..., half_len:]
    upper_part = upper * (grad_upper - jnp.sum(upper * grad_upper, axis=-1, keepdims=True))
    lower_part = lower * (grad_lower - jnp.sum(lower * grad_lower, axis=-1, keepdims=True))
    return upper_part - lower_part


def add_pair(earlier, later):
    return (earlier[0] + later[0], earlier[1] + later[1])


def skip_block(carry_in):
    return carry_in


def general_shards(queries, keys, values, feature_weight):
    block_len, head_count, head_width = queries.shape
    kv_count = keys.shape[1]
    group_size = head_count // kv_count
    feature_len = feature_weight.shape[2] // 2
    my_block = lax.axis_index("ctx")
    score_scale = 1.0 / math.sqrt(head_width)
    grouped_q = queries.reshape(block_len, kv_count, group_size, head_width)
    maps_weight = feature_weight.reshape(kv_count, group_size, head_width, 2 * feature_len)
    query_map = maps_weight[..., :feature_len]
    key_map = maps_weight[..., feature_len:]
    query_pos = my_block * block_len + jnp.arange(block_len, dtype=jnp.int32)
    prev_start = (my_block - 1) * block_len
    last_row = my_block * block_len + block_len - 1
    initial = [
        jnp.full((kv_count, group_size, block_len), big_negative, jnp.float32),
        jnp.zeros((kv_count, group_size, block_len), jnp.float32),
        jnp.zeros((kv_count, group_size, block_len, head_width), jnp.float32),
    ]
    initial = initial + [
        jnp.zeros((kv_count, group_size, 2 * feature_len, head_width), jnp.float32),
        jnp.zeros((kv_count, group_size, 2 * feature_len), jnp.float32),
    ]
    initial = tuple(initial)
    piece_keys = lax.all_gather(keys, "ctx", axis=0, tiled=True)
    piece_values = lax.all_gather(values, "ctx", axis=0, tiled=True)
    piece_rows = piece_keys.shape[0]
    step_rows = math.gcd(piece_rows, 512)

    def attend(step_index, running):
        first_row = step_index * step_rows
        block_keys = lax.dynamic_slice_in_dim(piece_keys, step_index * step_rows, step_rows, 0)
        block_values = lax.dynamic_slice_in_dim(piece_values, step_index * step_rows, step_rows, 0)
        key_pos = first_row + jnp.arange(step_rows, dtype=jnp.int32)

        def compute(carry_in):
            row_max, running_sum, accumulated = (carry_in[0], carry_in[1], carry_in[2])
            scores = (
                jnp.einsum(
                    "tkgd,skd->kgts", grouped_q, block_keys, preferred_element_type=jnp.float32
                )
                * score_scale
            )
            allowed = key_pos[None, :] <= query_pos[:, None]
            scores = jnp.where(allowed, scores, big_negative)
            new_max = jnp.maximum(row_max, jnp.max(scores, axis=-1))
            attn_weight = jnp.where(allowed, jnp.exp(scores - new_max[..., None]), 0.0)
            factor = jnp.exp(row_max - new_max)
            running_sum = running_sum * factor + jnp.sum(attn_weight, axis=-1)
            accumulated = accumulated * factor[..., None] + jnp.einsum(
                "kgts,skd->kgtd",
                attn_weight.astype(jnp.bfloat16),
                block_values,
                preferred_element_type=jnp.float32,
            )
            result = [new_max, running_sum, accumulated] + list(carry_in[3:])
            in_state = (key_pos < prev_start).astype(jnp.float32)
            features = feature_map(
                jnp.einsum(
                    "skd,kgdf->kgsf", block_keys.astype(jnp.float32), key_map, precision=precise
                )
            )
            features = features * in_state[None, None, :, None]
            result[-2] = carry_in[-2] + jnp.einsum(
                "kgsf,skd->kgfd", features, block_values.astype(jnp.float32), precision=precise
            )
            result[-1] = carry_in[-1] + jnp.sum(features, axis=2)
            return tuple(result)

        return lax.cond(first_row <= last_row, compute, skip_block, running)

    folded = lax.fori_loop(0, piece_rows // step_rows, attend, initial)
    teacher = folded[2] / folded[1][..., None]
    stacked = jnp.stack([keys, values])
    moved = shifted(stacked, "ctx", 1)
    prev_keys, prev_values = (moved[0], moved[1])
    has_prev = (my_block > 0).astype(jnp.float32)
    window_keys = jnp.concatenate([prev_keys, keys], axis=0)
    window_values = jnp.concatenate([prev_values, values], axis=0)
    column = jnp.arange(2 * block_len, dtype=jnp.int32)
    row_index = jnp.arange(block_len, dtype=jnp.int32)
    allowed = (column[None, :] < block_len) & (my_block > 0) | (column[None, :] >= block_len) & (
        column[None, :] - block_len <= row_index[:, None]
    )
    scores = (
        jnp.einsum("tkgd,skd->kgts", grouped_q, window_keys, preferred_element_type=jnp.float32)
        * score_scale
    )
    scores = jnp.where(allowed, scores, big_negative)
    row_max = jnp.max(scores, axis=-1)
    window_weight = jnp.where(allowed, jnp.exp(scores - row_max[..., None]), 0.0)
    window_den = jnp.sum(window_weight, axis=-1)
    window_num = jnp.einsum(
        "kgts,skd->kgtd",
        window_weight.astype(jnp.bfloat16),
        window_values,
        preferred_element_type=jnp.float32,
    )
    key_proj = jnp.einsum(
        "skd,kgdf->kgsf", prev_keys.astype(jnp.float32), key_map, precision=precise
    )
    state, norm = (folded[-2], folded[-1])
    query_proj = jnp.einsum(
        "tkgd,kgdf->kgtf", grouped_q.astype(jnp.float32), query_map, precision=precise
    )
    query_feats = feature_map(query_proj)
    decay = jnp.exp(-row_max)
    far_num = decay[..., None] * jnp.einsum(
        "kgtf,kgfd->kgtd", query_feats, state, precision=precise
    )
    far_den = decay * jnp.einsum("kgtf,kgf->kgt", query_feats, norm, precision=precise)
    denominator = window_den + far_den
    mix = (window_num + far_num) / denominator[..., None]
    student = jnp.transpose(mix.astype(jnp.bfloat16), (2, 0, 1, 3)).reshape(
        block_len, head_count, head_width
    )
    mismatch = mix - teacher
    grad_num = mismatch / denominator[..., None]
    grad_den = -jnp.sum(mismatch * mix, axis=-1) / denominator
    lifted = decay[..., None] * query_feats
    grad_state = jnp.einsum("kgtf,kgtd->kgfd", lifted, grad_num, precision=precise)
    grad_norm = jnp.einsum("kgtf,kgt->kgf", lifted, grad_den, precision=precise)
    grad_qfeat = decay[..., None] * (
        jnp.einsum("kgfd,kgtd->kgtf", state, grad_num, precision=precise)
        + norm[:, :, None, :] * grad_den[..., None]
    )
    later_state, later_norm = carried_in(
        (grad_state, grad_norm),
        "ctx",
        add_pair,
        (jnp.zeros_like(grad_state), jnp.zeros_like(grad_norm)),
    )
    grad_kfeat = (
        jnp.einsum(
            "kgfd,skd->kgsf", later_state, prev_values.astype(jnp.float32), precision=precise
        )
        + later_norm[:, :, None, :]
    ) * has_prev
    grad_query = jnp.einsum(
        "tkgd,kgtf->kgdf",
        grouped_q.astype(jnp.float32),
        feature_pull(query_proj, grad_qfeat),
        precision=precise,
    )
    grad_key = jnp.einsum(
        "skd,kgsf->kgdf",
        prev_keys.astype(jnp.float32),
        feature_pull(key_proj, grad_kfeat),
        precision=precise,
    )
    gradients = jnp.concatenate([grad_query, grad_key], axis=-1).reshape(
        head_count, head_width, 2 * feature_len
    )
    entry_count = gradients.size * lax.axis_size("head")
    summed = lax.psum(gradients, "ctx")
    squares = lax.psum(jnp.sum(summed * summed), "head")
    update = summed / jnp.sqrt(squares / entry_count + 1e-06)
    return (student, update)


f32, bf16 = jnp.float32, jnp.bfloat16
NN = (((1,), (0,)), ((), ()))
NT = (((1,), (1,)), ((), ()))
TN = (((0,), (0,)), ((), ()))


def mxu(a, b, dims):
    return lax.dot_general(a, b, dims, preferred_element_type=f32)


def split(x, pieces):
    out = []
    for _ in range(pieces):
        piece = x.astype(bf16)
        out.append(piece)
        x = x - piece.astype(f32)
    return out


def cat(parts, axis):
    return jnp.concatenate(parts, axis=axis)


def exact_by_wide(a, b, dims):
    return mxu(cat([a, a], dims[0][0][0]), cat(split(b, 2), dims[0][1][0]), dims)


def wide_by_exact(a, b, dims):
    return mxu(cat(split(a, 2), dims[0][0][0]), cat([b, b], dims[0][1][0]), dims)


def wide_by_wide(a, b, dims):
    a_hi, a_lo = split(a, 2)
    b_hi, b_lo = split(b, 2)
    return mxu(
        cat([a_hi, a_hi, a_lo], dims[0][0][0]), cat([b_hi, b_lo, b_hi], dims[0][1][0]), dims
    )


def half_sum(x, halves):
    return wide_by_exact(x, halves, NN)


def half_softmax(u, is_upper, halves):
    top = jnp.max(jnp.where(is_upper, u, big_negative), axis=-1, keepdims=True)
    low = jnp.max(jnp.where(is_upper, big_negative, u), axis=-1, keepdims=True)
    e = jnp.exp(u - jnp.where(is_upper, top, low))
    return e / half_sum(e, halves)


def remote(src, dst, send_sem, recv_sem, **where):
    return pltpu.make_async_remote_copy(
        src_ref=src,
        dst_ref=dst,
        send_sem=send_sem,
        recv_sem=recv_sem,
        device_id=where,
        device_id_type=pl.DeviceIdType.MESH,
    )


def each(count, body):
    def step(index, carry):
        body(index)
        return carry

    lax.fori_loop(0, count, step, 0)


def head_kernel(
    q_hbm, k_hbm, v_hbm, w_hbm, student_hbm, grad_hbm, scale_hbm,
    q_raw, k_raw, v_raw, w_ref, qt_ref, kvt_ref, q_all, kv_all, st_all, st_turned, mix_ref,
    own_grad, gat_ref, sq_own, sq_all, sq_ref, scale_ref, own_ref, sum_ref, pre_ref, pre_norm_ref,
    score_ref, near_ref, kfeat_ref, gstate_ref, gnorm_ref, wq_ref, wk_ref, gq_ref,
    q_sem, kv_send, kv_recv, local_sem, st_sem, g_send, g_recv, g_final, sq_sem, fetch_sem,
    w_send, w_recv, out_sem, swap_sem,
):
    blocks, length, width = qt_ref.shape
    planes = kvt_ref.shape[0]
    group = blocks // planes
    me, side = lax.axis_index("ctx"), lax.axis_index("head")
    plane, spot = me // group, me % group
    row, column = spot // 2, spot % 2
    native = row == side
    mine = plane * group + 2 * column + side
    features = w_ref.shape[1] // 2
    rows = 2 * length
    steps, pairs = blocks // 2, blocks // 4
    middle = pairs - 1

    def pair_block(p, u):
        return jnp.where(u < 2, 4 * p + u, blocks - 4 - 4 * p + u)

    my_pair = jnp.where(row == 0, plane, planes - 1 - plane)
    barrier = pltpu.get_barrier_semaphore()

    def greet(t, h):
        pl.semaphore_signal(
            barrier, inc=1, device_id={"ctx": t, "head": h}, device_id_type=pl.DeviceIdType.MESH
        )

    def greet_side(d):
        t = (me + d) % blocks

        @pl.when(jnp.logical_not(native & (t == me)))
        def _():
            greet(t, row)

    fetches = [
        pltpu.make_async_copy(src, dst, fetch_sem.at[n])
        for n, (src, dst) in enumerate([(k_hbm, k_raw), (v_hbm, v_raw), (q_hbm, q_raw)])
    ]
    for fetch in fetches:
        fetch.start()
    each(blocks, greet_side)
    each(blocks // 2, lambda n: greet((n // 2) * group + 2 * side + n % 2, 1 - row))
    own_w = pltpu.make_async_copy(w_hbm.at[mine], w_ref, local_sem.at[2])

    @pl.when(native)
    def _():
        own_w.start()

    def flip(index, d):
        bit = 1
        while bit <= d:
            if d & bit:
                index = index + bit - 2 * bit * ((index // bit) % 2)
            bit *= 2
        return index

    def w_copy():
        other = plane * group + 2 * column + 1 - side
        return remote(w_hbm.at[other], w_ref, w_send.at[0], w_recv.at[0], ctx=me, head=1 - side)

    def kv_land(g):
        return remote(
            kvt_ref.at[g], kv_all.at[me], kv_send.at[0], kv_recv.at[plane],
            ctx=g * group + 2 * side + column, head=row,
        )

    def landed_block(z):
        return z * group + 2 * side + column

    def crossed_block(z):
        return z * group + 2 * side + 1 - column

    def kv_across(z):
        block = landed_block(z)
        return remote(
            kv_all.at[block], kv_all.at[block], kv_send.at[1], kv_recv.at[planes + z],
            ctx=plane * group + 2 * row + 1 - column, head=side,
        )

    def kv_share(block, z):
        return remote(
            kv_all.at[block], kv_all.at[block], kv_send.at[2], kv_recv.at[2 * planes + z],
            ctx=me, head=1 - side,
        )

    def q_copy(j):
        return remote(
            qt_ref.at[j], q_all.at[me], q_sem.at[pairs], q_sem.at[my_pair],
            ctx=(j // group) * group + 2 * side + (j % group) // 2, head=j % 2,
        )

    def bulk(ref, send_sem, recv_sem):
        return remote(ref, ref, send_sem, recv_sem, ctx=me, head=1 - side)

    def kv_arrival(first, count, n):
        return bulk(kv_all.at[pl.ds(first, count)], kv_send.at[0], kv_recv.at[n])

    def st_copy(b):
        return remote(mix_ref.at[b], st_all.at[mine], st_sem.at[0], st_sem.at[1], ctx=b, head=row)

    def g_column(part, z):
        return remote(
            own_grad.at[part], gat_ref.at[part, mine], g_send.at[0], g_recv.at[part, 2 * plane + side],
            ctx=z * group + spot, head=row,
        )

    def g_pass(part, j, d):
        piece = gat_ref.at[part, j]
        return remote(
            piece, piece, g_send.at[d], g_final.at[0],
            ctx=plane * group + flip(spot, d), head=side,
        )

    def g_landing(part, j, n):
        return bulk(gat_ref.at[part, j], g_send.at[0], g_recv.at[part, n])

    def sq_copy(t):
        return remote(
            sq_own, sq_all.at[mine], sq_sem.at[0], sq_sem.at[1], ctx=t, head=row
        )

    def unless_own(b, body):
        @pl.when(jnp.logical_not(native & (b == me)))
        def _():
            body()

    rate = math.log2(math.e) / math.sqrt(width)
    lane = lax.broadcasted_iota(jnp.int32, (rows, 2 * features), 1)
    is_upper = lane < features
    row_half = lax.broadcasted_iota(jnp.int32, (2 * features, 2 * features), 0) < features
    col_half = lax.broadcasted_iota(jnp.int32, (2 * features, 2 * features), 1) < features
    halves = jnp.where(row_half == col_half, 1.0, 0.0).astype(bf16)
    square = (rows, rows)
    causal = lax.broadcasted_iota(jnp.int32, square, 1) <= lax.broadcasted_iota(jnp.int32, square, 0)
    for part, (fetch, raw) in enumerate(zip(fetches, (k_raw, v_raw))):
        fetch.wait()
        kvt_ref[:, part] = jnp.transpose(raw[...], (1, 0, 2))
    own_kv = pltpu.make_async_copy(kvt_ref.at[plane], kv_all.at[me], local_sem.at[0])

    @pl.when(native)
    def _():
        own_kv.start()

    pl.semaphore_wait(barrier, jnp.where(native, 3 * blocks // 2 - 1, 3 * blocks // 2))
    for d in range(planes):
        g = flip(plane, d)
        if d == 0:
            @pl.when(jnp.logical_not(native))
            def _():
                kv_land(g).start()
        else:
            kv_land(g).start()

    @pl.when(native)
    def _():
        w_copy().start()

    fetches[2].wait()
    qt_ref[...] = jnp.transpose(q_raw[...], (1, 0, 2))
    own_q = pltpu.make_async_copy(qt_ref.at[mine], q_all.at[me], local_sem.at[1])

    @pl.when(native)
    def _():
        own_q.start()
        own_kv.wait()

    def land(d):
        z = flip(plane, d)
        block = landed_block(z)
        unless_own(block, lambda: kv_arrival(block, 1, z).wait_recv())
        kv_across(z).start()
        kv_share(block, z).start()

    def cross(d):
        z = flip(plane, d)
        block = crossed_block(z)
        kv_arrival(block, 1, planes + z).wait_recv()
        kv_share(block, z).start()

    def load(part, i):
        if part == 0:
            return q_all[pl.ds(2 * i, 2)].reshape(rows, width)
        return kv_all[pl.ds(2 * i, 2), part - 1].reshape(rows, width)

    def either(less, body):
        for flag, count in ((native, less), (jnp.logical_not(native), 0)):
            @pl.when(flag)
            def _():
                body(count)

    def q_arrived(p):
        here = native & (p == my_pair)
        for flag, count in ((here, 3), (jnp.logical_not(here), 4)):
            @pl.when(flag)
            def _():
                bulk(q_all.at[pl.ds(0, count)], q_sem.at[pairs], q_sem.at[p]).wait_recv()

    def send_student(b):
        unless_own(b, lambda: st_copy(b).start())

        @pl.when(native & (b == me))
        def _():
            st_all[mine] = mix_ref[me]

    def send_grad(part):
        for d in range(planes):
            z = flip(plane, d)
            if d == 0:
                @pl.when(native)
                def _():
                    gat_ref[part, mine] = own_grad[part]

                @pl.when(jnp.logical_not(native))
                def _():
                    g_column(part, z).start()
            else:
                g_column(part, z).start()

    def relay_grad(part):
        @pl.when(native)
        def _():
            for z in range(planes):
                for h in range(2):
                    j = flip(plane, z) * group + 2 * column + h

                    @pl.when(j != mine)
                    def _():
                        g_landing(part, j, 2 * flip(plane, z) + h).wait_recv()

                    for d in range(1, group):
                        g_pass(part, j, d).start()

    def key_side(pair):
        kv_arrival(group * pair, 2, 2 * planes + pair).wait_recv()
        steps_of = (2 * pair, 2 * pair + 1)
        ks, vs = ([load(part, i) for i in steps_of] for part in (1, 2))
        kfs = [
            half_softmax(mxu(cat([k, k, k], 1), wk_ref[...], NN), is_upper, halves) for k in ks
        ]
        for i, kf, v in zip(steps_of, kfs, vs):
            kfeat_ref[i] = kf
            for h in range(2):
                part = kf[h * length:(h + 1) * length]
                own_ref[2 * i + h] = wide_by_exact(part, v[h * length:(h + 1) * length], TN)
                sum_ref[2 * i + h] = jnp.sum(part, axis=0, keepdims=True)

    def push(n):
        p = (my_pair + pairs - n // group) % pairs
        j = jnp.where(side == 0, p, planes - 1 - p) * group + n % group

        @pl.when(jnp.logical_not(native & (j == mine)))
        def _():
            q_copy(j).start()

    def plane_keys(z):
        each(group // 4, lambda u: key_side(z * (group // 4) + u))

    def push_turns(first, last):
        each((last - first) * group, lambda n: push(first * group + n))

    land(0)
    @pl.when(native)
    def _():
        own_w.wait()

    @pl.when(jnp.logical_not(native))
    def _():
        w_copy().wait_recv()

    w = w_ref[...]
    wq, wk = w[:, :features], w[:, features:]
    wq_ref[...] = cat(split(cat([wq, -wq], 1), 3), 0)
    wk_ref[...] = cat(split(cat([wk, -wk], 1), 3), 0)
    gq_ref[...] = jnp.zeros_like(gq_ref)
    land(1)
    push_turns(0, 1)
    cross(0)
    land(2)
    cross(1)
    land(3)
    push_turns(1, 2)
    plane_keys(flip(plane, 0))
    cross(2)
    plane_keys(flip(plane, 1))
    cross(3)
    push_turns(2, pairs)
    plane_keys(flip(plane, 2))
    plane_keys(flip(plane, 3))

    @pl.when(native)
    def _():
        own_q.wait()

    for b in range(2):
        pre_ref[b] = jnp.zeros_like(pre_ref[b])
        pre_norm_ref[b] = jnp.zeros_like(pre_norm_ref[b])

    def prefix(b):
        pre_ref[b + 2] = pre_ref[b + 1] + own_ref[b]
        pre_norm_ref[b + 2] = pre_norm_ref[b + 1] + sum_ref[b]

    each(blocks - 2, prefix)

    def forward(turn, carry):
        p = (my_pair + turn) % pairs
        a, b = 2 * p, steps - 1 - 2 * p
        q_arrived(p)
        tokens = (a, b)
        qs = [load(0, i) for i in tokens]
        vs = [load(2, i) for i in tokens]
        wide_b = b // 2

        def pair_of(part, j):
            return cat([load(part, 2 * j), load(part, 2 * j + 1)], 0)

        def fold(x, combine):
            while x.shape[1] > length:
                half = x.shape[1] // 2
                x = combine(x[:, :half], x[:, half:])
            return x

        s = mxu(qs[0], load(1, a), NT) * rate
        s_a = jnp.where(causal, s, big_negative)
        near_ref[0] = s_a
        s = mxu(qs[1], pair_of(1, wide_b), NT) * rate
        s_b = [s[:, :rows], jnp.where(causal, s[:, rows:], big_negative)]
        near_ref[1], near_ref[2] = s_b
        peaks = [fold(s_a, jnp.maximum), fold(jnp.maximum(*s_b), jnp.maximum)]

        def far_tile(m):
            first = m < p
            return first, jnp.where(first, a, b), jnp.where(first, m, m - p)

        for m in range(middle):
            first, i, j = far_tile(m)
            s = mxu(load(0, i), pair_of(1, j), NT) * rate
            score_ref[m] = s
            top = fold(s, jnp.maximum)
            peaks = [
                jnp.maximum(peaks[0], jnp.where(first, top, big_negative)),
                jnp.maximum(peaks[1], jnp.where(first, big_negative, top)),
            ]
        tops = [jnp.max(x, axis=-1, keepdims=True) for x in peaks]

        weight = jnp.exp2(near_ref[0] - tops[0])
        sums = [fold(weight, jnp.add)]
        accs = [mxu(weight.astype(bf16), vs[0], NN)]
        weight = jnp.exp2(cat([near_ref[1], near_ref[2]], 1) - tops[1])
        sums.append(fold(weight, jnp.add))
        accs.append(mxu(weight.astype(bf16), pair_of(2, wide_b), NN))
        for m in range(middle):
            first, i, j = far_tile(m)
            weight = jnp.exp2(score_ref[m] - jnp.where(first, tops[0], tops[1]))
            part = fold(weight, jnp.add)
            prod = mxu(weight.astype(bf16), pair_of(2, j), NN)
            sums = [sums[0] + jnp.where(first, part, 0.0), sums[1] + jnp.where(first, 0.0, part)]
            accs = [accs[0] + jnp.where(first, prod, 0.0), accs[1] + jnp.where(first, 0.0, prod)]
        teachers = [
            acc / jnp.sum(total, axis=-1, keepdims=True) for acc, total in zip(accs, sums)
        ]

        def halves_of(f):
            return [cat([f(x, 0), f(x, 1)], 0) for x in range(2)]

        def cut(x, half):
            return x[half * length:(half + 1) * length]

        last_far = score_ref[jnp.maximum(p - 1, 0), :length, 3 * length:]
        prevs = [
            cat([jnp.where(p > 0, last_far, big_negative), near_ref[0, length:, :length]], 0),
            cat([near_ref[1, :length, length:], near_ref[2, length:, :length]], 0),
        ]
        owns = [
            cat([near_ref[k, :length, :length], near_ref[k, length:, length:]], 0) for k in (0, 2)
        ]
        win_maxs = [
            jnp.max(jnp.maximum(prev, own), axis=-1, keepdims=True)
            for prev, own in zip(prevs, owns)
        ]
        p_prevs = [jnp.exp2(x - top) for x, top in zip(prevs, win_maxs)]
        p_owns = [jnp.exp2(x - top) for x, top in zip(owns, win_maxs)]
        win_dens = [jnp.sum(x + y, axis=-1, keepdims=True) for x, y in zip(p_prevs, p_owns)]
        p_wins = [cat([x.astype(bf16), y.astype(bf16)], 1) for x, y in zip(p_prevs, p_owns)]
        v_befores = [kv_all[jnp.maximum(2 * i - 1, 0), 1] for i in tokens]
        v_wins = [
            (cat([before, v[:length]], 0), v) for before, v in zip(v_befores, vs)
        ]
        win_nums = halves_of(lambda x, h: mxu(cut(p_wins[x], h), v_wins[x][h], NN))

        qfs = [
            half_softmax(mxu(cat([q, q, q], 1), wq_ref[...], NN), is_upper, halves) for q in qs
        ]
        states = [[pre_ref[2 * i], pre_ref[2 * i + 1]] for i in tokens]
        norms = [
            cat(
                [
                    jnp.broadcast_to(pre_norm_ref[2 * i + h], (length, 2 * features))
                    for h in range(2)
                ],
                0,
            )
            for i in tokens
        ]
        decays = [jnp.exp2(-top) for top in win_maxs]
        fars = halves_of(lambda x, h: wide_by_wide(cut(qfs[x], h), states[x][h], NN))
        dens = [
            win_den + decay * jnp.sum(qf * norm, axis=-1, keepdims=True)
            for win_den, decay, qf, norm in zip(win_dens, decays, qfs, norms)
        ]
        mixes = [
            (num + decay * far) / den
            for num, decay, far, den in zip(win_nums, decays, fars, dens)
        ]
        for i, mix in zip(tokens, mixes):
            mix_ref[pl.ds(2 * i, 2)] = mix.astype(bf16).reshape(2, length, width)
        @pl.when(turn < pairs - 1)
        def _():
            each(4, lambda u: send_student(pair_block(p, u)))

        mismatches = [mix - teacher for mix, teacher in zip(mixes, teachers)]
        g_nums = [x / den for x, den in zip(mismatches, dens)]
        g_dens = [
            -jnp.sum(x * mix, axis=-1, keepdims=True) / den
            for x, mix, den in zip(mismatches, mixes, dens)
        ]
        lifts = [decay * qf for decay, qf in zip(decays, qfs)]
        pulled_norms = [lift * g_den for lift, g_den in zip(lifts, g_dens)]
        for x, i in enumerate(tokens):
            for h in range(2):
                gstate_ref[2 * i + h] = wide_by_wide(cut(lifts[x], h), cut(g_nums[x], h), TN)
                gnorm_ref[2 * i + h] = jnp.sum(cut(pulled_norms[x], h), axis=0, keepdims=True)
        pulled = halves_of(lambda x, h: wide_by_wide(cut(g_nums[x], h), states[x][h], NT))
        g_qfs = [
            decay * (pull + norm * g_den)
            for decay, pull, norm, g_den in zip(decays, pulled, norms, g_dens)
        ]
        d_qs = [qf * (g - half_sum(qf * g, halves)) for qf, g in zip(qfs, g_qfs)]
        gq_ref[...] += wide_by_exact(d_qs[0], qs[0], TN) + wide_by_exact(d_qs[1], qs[1], TN)
        return carry

    lax.fori_loop(0, pairs, forward, 0)
    own_grad[0] = (gq_ref[:features] - gq_ref[features:]).astype(bf16)
    send_grad(0)

    for b in range(blocks - 2, 1, -1):
        gstate_ref[b] = gstate_ref[b] + gstate_ref[b + 1]
        gnorm_ref[b] = gnorm_ref[b] + gnorm_ref[b + 1]

    def backward(group_of):
        ks, vs, kfs = ([f(i) for i in group_of] for f in (lambda i: load(1, i), lambda i: load(2, i), lambda i: kfeat_ref[i]))
        g_kfs = [
            cat(
                [
                    exact_by_wide(v[h * length:(h + 1) * length], gstate_ref[2 * i + h + 2], NT)
                    + gnorm_ref[2 * i + h + 2]
                    for h in range(2)
                ],
                0,
            )
            for i, v in zip(group_of, vs)
        ]
        d_ks = [kf * (g - half_sum(kf * g, halves)) for kf, g in zip(kfs, g_kfs)]
        return [wide_by_exact(d_k, k, TN) for d_k, k in zip(d_ks, ks)]

    gk = sum(backward(range(steps // 2)) + backward(range(steps // 2, steps - 1)))
    own_grad[1] = (gk[:features] - gk[features:]).astype(bf16)
    send_grad(1)
    square = own_grad[...].astype(f32).reshape(2 * features, width)
    sq_own[...] = jnp.sum(square * square, axis=0, keepdims=True)
    each(blocks, lambda n: unless_own((me + n) % blocks, lambda: sq_copy((me + n) % blocks).start()))

    @pl.when(native)
    def _():
        sq_all[mine] = sq_own[...]

    each(4, lambda u: send_student(pair_block((my_pair + pairs - 1) % pairs, u)))
    relay_grad(0)
    relay_grad(1)

    either(1, lambda n: bulk(st_all.at[pl.ds(0, blocks - n)], st_sem.at[0], st_sem.at[1]).wait_recv())
    st_turned[...] = jnp.transpose(st_all[...], (1, 0, 2))
    student_out = pltpu.make_async_copy(st_turned, student_hbm, out_sem.at[0])
    student_out.start()

    either(1, lambda n: bulk(sq_all.at[pl.ds(0, blocks - n)], sq_sem.at[0], sq_sem.at[1]).wait_recv())
    sq_ref[0] = jnp.sum(sq_all[...], axis=0)
    swap = remote(
        sq_ref.at[0], sq_ref.at[1], swap_sem.at[0], swap_sem.at[1], ctx=me, head=1 - side
    )
    swap.start()

    either(1, lambda n: bulk(qt_ref.at[pl.ds(0, blocks - n)], q_sem.at[pairs], q_sem.at[0]).wait_send())
    either(1, lambda n: bulk(mix_ref.at[pl.ds(0, blocks - n)], st_sem.at[0], st_sem.at[1]).wait_send())
    either(1, lambda n: bulk(sq_all.at[pl.ds(0, blocks - n)], sq_sem.at[0], sq_sem.at[1]).wait_send())
    either(1, lambda n: bulk(kvt_ref.at[pl.ds(0, planes - n)], kv_send.at[0], kv_recv.at[0]).wait_send())
    bulk(kv_all.at[pl.ds(0, planes)], kv_send.at[1], kv_recv.at[0]).wait_send()
    bulk(kv_all.at[pl.ds(0, 2 * planes)], kv_send.at[2], kv_recv.at[0]).wait_send()
    either(2, lambda n: bulk(gat_ref.at[0, pl.ds(0, 2 * planes - n)], g_send.at[0], g_final.at[0]).wait_send())

    @pl.when(native)
    def _():
        w_copy().wait_send()

    swap.wait()
    entries = 2 * blocks * width * 2 * features
    total = jnp.sum(sq_ref[0] + sq_ref[1], keepdims=True)
    scale_ref[...] = jnp.broadcast_to(1.0 / jnp.sqrt(total / entries + 1e-06), (8, width))
    scale_out = pltpu.make_async_copy(scale_ref, scale_hbm, out_sem.at[2])
    scale_out.start()

    @pl.when(native)
    def _():
        bulk(gat_ref.at[0], g_send.at[0], g_final.at[0]).wait_recv()

    @pl.when(jnp.logical_not(native))
    def _():
        bulk(gat_ref, g_send.at[0], g_final.at[0]).wait_recv()

    grad_out = pltpu.make_async_copy(gat_ref, grad_hbm, out_sem.at[1])
    grad_out.start()

    @pl.when(native)
    def _():
        for d in range(1, group):
            bulk(gat_ref.at[0], g_send.at[d], g_final.at[0]).wait_send()

    student_out.wait()
    scale_out.wait()
    grad_out.wait()


def finish_kernel(
    student_hbm, grad_hbm, scale_hbm, student_out, update_out,
    st_ref, grad_ref, scale_ref, update_ref, in_sem, out_sem,
):
    parts, blocks, features, width = grad_ref.shape
    chunks = in_sem.shape[0] - 2
    each_len = blocks // chunks
    fetches = [
        pltpu.make_async_copy(
            grad_hbm.at[:, pl.ds(n * each_len, each_len)],
            grad_ref.at[:, pl.ds(n * each_len, each_len)], in_sem.at[n],
        )
        for n in range(chunks)
    ]
    scale_in = pltpu.make_async_copy(scale_hbm, scale_ref, in_sem.at[chunks])
    student_in = pltpu.make_async_copy(student_hbm, st_ref, in_sem.at[chunks + 1])
    scale_in.start()
    for fetch in fetches:
        fetch.start()
    student_in.start()
    scale_in.wait()
    scale = scale_ref[:1]
    stores = []
    for n, fetch in enumerate(fetches):
        fetch.wait()
        for j in range(n * each_len, (n + 1) * each_len):
            piece = cat([grad_ref[0, j], grad_ref[1, j]], 0).astype(f32)
            update_ref[j] = piece.T * scale
        stores.append(
            pltpu.make_async_copy(
                update_ref.at[pl.ds(n * each_len, each_len)],
                update_out.at[pl.ds(n * each_len, each_len)], out_sem.at[n],
            )
        )
        stores[-1].start()
    student_in.wait()
    stores.append(pltpu.make_async_copy(st_ref, student_out, out_sem.at[chunks]))
    stores[-1].start()
    for store in stores:
        store.wait()


def whole_head(queries, keys, values, w):
    length, blocks, width = queries.shape
    planes = keys.shape[1]
    group = blocks // planes
    double = w.shape[2]
    half = double // 2
    rows, steps = 2 * length, blocks // 2
    vmem, dma = pltpu.VMEM, pltpu.SemaphoreType.DMA
    hbm = pl.BlockSpec(memory_space=pltpu.MemorySpace.HBM)
    limit = 67_043_328
    student, grads, scale = pl.pallas_call(
        head_kernel,
        out_shape=(
            jax.ShapeDtypeStruct((length, blocks, width), bf16),
            jax.ShapeDtypeStruct((2, blocks, half, width), bf16),
            jax.ShapeDtypeStruct((8, width), f32),
        ),
        in_specs=[hbm] * 4,
        out_specs=(hbm,) * 3,
        scratch_shapes=[
            vmem((length, blocks, width), bf16),
            vmem((length, planes, width), bf16),
            vmem((length, planes, width), bf16),
            vmem((width, double), f32),
            vmem((blocks, length, width), bf16),
            vmem((planes, 2, length, width), bf16),
            vmem((blocks, length, width), bf16),
            vmem((blocks, 2, length, width), bf16),
            vmem((blocks, length, width), bf16),
            vmem((length, blocks, width), bf16),
            vmem((blocks, length, width), bf16),
            vmem((2, half, width), bf16),
            vmem((2, blocks, half, width), bf16),
            vmem((1, width), f32),
            vmem((blocks, 1, width), f32),
            vmem((2, 1, width), f32),
            vmem((8, width), f32),
            vmem((blocks, double, width), f32),
            vmem((blocks, 1, double), f32),
            vmem((blocks, double, width), f32),
            vmem((blocks, 1, double), f32),
            vmem((blocks // 4 - 1, rows, 2 * rows), f32),
            vmem((3, rows, rows), f32),
            vmem((steps, rows, double), f32),
            vmem((blocks, double, width), f32),
            vmem((blocks, 1, double), f32),
            vmem((3 * width, double), bf16),
            vmem((3 * width, double), bf16),
            vmem((double, width), f32),
            dma((blocks // 4 + 1,)),
            dma((3,)),
            dma((3 * planes,)),
            dma((3,)),
            dma((2,)),
            dma((group,)),
            dma((2, 2 * planes)),
            dma((1,)),
            dma((2,)),
            dma((3,)),
            dma((1,)),
            dma((1,)),
            dma((3,)),
            dma((2,)),
        ],
        compiler_params=pltpu.CompilerParams(
            vmem_limit_bytes=limit, collective_id=0, has_side_effects=True
        ),
    )(queries, keys, values, w)
    chunks = 4
    return pl.pallas_call(
        finish_kernel,
        out_shape=(
            jax.ShapeDtypeStruct((length, blocks, width), bf16),
            jax.ShapeDtypeStruct((blocks, width, double), f32),
        ),
        in_specs=[hbm] * 3,
        out_specs=(hbm,) * 2,
        scratch_shapes=[
            vmem((length, blocks, width), bf16),
            vmem((2, blocks, half, width), bf16),
            vmem((8, width), f32),
            vmem((blocks, width, double), f32),
            dma((chunks + 2,)),
            dma((chunks + 1,)),
        ],
        compiler_params=pltpu.CompilerParams(vmem_limit_bytes=limit),
    )(student, grads, scale)


def head_shards(queries, keys, values, feature_weight):
    return whole_head(queries, keys, values, feature_weight)


def shards(queries, keys, values, feature_weight):
    count = lax.axis_size("ctx")
    width = queries.shape[2]
    fits = queries.shape[1] == count and count == 4 * keys.shape[1] and lax.axis_size("head") == 2 and count % 4 == 0 and keys.shape[1] == 4 and count * queries.shape[0] <= 4096
    fits = fits and queries.shape[1] // keys.shape[1] % 4 == 0 and queries.shape[0] == width and feature_weight.shape[2] == width
    body = head_shards if fits else general_shards
    return body(queries, keys, values, feature_weight)


def solution(mesh):
    return jax.shard_map(
        shards,
        mesh=mesh,
        in_specs=(
            P("ctx", "head", None),
            P("ctx", "head", None),
            P("ctx", "head", None),
            P("head", None, None),
        ),
        out_specs=(P("ctx", "head", None), P("head", None, None)),
        check_vma=False,
    )
```

```python
import functools
import math

import jax
import jax.numpy as jnp
from jax import lax
from jax.experimental import pallas as pl
from jax.experimental.pallas import tpu as pltpu
from jax.sharding import PartitionSpec as P

precise = lax.Precision.HIGHEST
big_negative = -1e30


def shifted(shard, axis, by):
    devices = lax.axis_size(axis)
    pairs = [(i, i + by) for i in range(devices) if 0 <= i + by < devices]
    return lax.ppermute(shard, axis, pairs)


def carried_in(part, axis, combine, identity):
    count = lax.axis_size(axis)
    place = lax.axis_index(axis)
    ahead = count - 1 - place
    gathered = jax.tree.map(lambda a: lax.all_gather(a, axis), part)
    state = jax.tree.map(lambda a, e: jnp.zeros_like(a) + jnp.asarray(e, a.dtype), part, identity)

    def one(step, state):
        source = count - 1 - step
        return combine(
            state, jax.tree.map(lambda a: lax.dynamic_index_in_dim(a, source, 0, False), gathered)
        )

    return lax.fori_loop(0, ahead, one, state)


def feature_map(projection):
    return jnp.concatenate(
        [jax.nn.softmax(projection, axis=-1), jax.nn.softmax(-projection, axis=-1)], axis=-1
    )


def feature_pull(projection, upstream):
    half_len = upstream.shape[-1] // 2
    upper = jax.nn.softmax(projection, axis=-1)
    lower = jax.nn.softmax(-projection, axis=-1)
    grad_upper = upstream[..., :half_len]
    grad_lower = upstream[..., half_len:]
    upper_part = upper * (grad_upper - jnp.sum(upper * grad_upper, axis=-1, keepdims=True))
    lower_part = lower * (grad_lower - jnp.sum(lower * grad_lower, axis=-1, keepdims=True))
    return upper_part - lower_part


def add_pair(earlier, later):
    return (earlier[0] + later[0], earlier[1] + later[1])


def skip_block(carry_in):
    return carry_in


def general_shards(queries, keys, values, feature_weight):
    block_len, head_count, head_width = queries.shape
    kv_count = keys.shape[1]
    group_size = head_count // kv_count
    feature_len = feature_weight.shape[2] // 2
    my_block = lax.axis_index("ctx")
    score_scale = 1.0 / math.sqrt(head_width)
    grouped_q = queries.reshape(block_len, kv_count, group_size, head_width)
    maps_weight = feature_weight.reshape(kv_count, group_size, head_width, 2 * feature_len)
    query_map = maps_weight[..., :feature_len]
    key_map = maps_weight[..., feature_len:]
    query_pos = my_block * block_len + jnp.arange(block_len, dtype=jnp.int32)
    prev_start = (my_block - 1) * block_len
    last_row = my_block * block_len + block_len - 1
    initial = [
        jnp.full((kv_count, group_size, block_len), big_negative, jnp.float32),
        jnp.zeros((kv_count, group_size, block_len), jnp.float32),
        jnp.zeros((kv_count, group_size, block_len, head_width), jnp.float32),
    ]
    initial = initial + [
        jnp.zeros((kv_count, group_size, 2 * feature_len, head_width), jnp.float32),
        jnp.zeros((kv_count, group_size, 2 * feature_len), jnp.float32),
    ]
    initial = tuple(initial)
    piece_keys = lax.all_gather(keys, "ctx", axis=0, tiled=True)
    piece_values = lax.all_gather(values, "ctx", axis=0, tiled=True)
    piece_rows = piece_keys.shape[0]
    step_rows = math.gcd(piece_rows, 512)

    def attend(step_index, running):
        first_row = step_index * step_rows
        block_keys = lax.dynamic_slice_in_dim(piece_keys, step_index * step_rows, step_rows, 0)
        block_values = lax.dynamic_slice_in_dim(piece_values, step_index * step_rows, step_rows, 0)
        key_pos = first_row + jnp.arange(step_rows, dtype=jnp.int32)

        def compute(carry_in):
            row_max, running_sum, accumulated = (carry_in[0], carry_in[1], carry_in[2])
            scores = (
                jnp.einsum(
                    "tkgd,skd->kgts", grouped_q, block_keys, preferred_element_type=jnp.float32
                )
                * score_scale
            )
            allowed = key_pos[None, :] <= query_pos[:, None]
            scores = jnp.where(allowed, scores, big_negative)
            new_max = jnp.maximum(row_max, jnp.max(scores, axis=-1))
            attn_weight = jnp.where(allowed, jnp.exp(scores - new_max[..., None]), 0.0)
            factor = jnp.exp(row_max - new_max)
            running_sum = running_sum * factor + jnp.sum(attn_weight, axis=-1)
            accumulated = accumulated * factor[..., None] + jnp.einsum(
                "kgts,skd->kgtd",
                attn_weight.astype(jnp.bfloat16),
                block_values,
                preferred_element_type=jnp.float32,
            )
            result = [new_max, running_sum, accumulated] + list(carry_in[3:])
            in_state = (key_pos < prev_start).astype(jnp.float32)
            features = feature_map(
                jnp.einsum(
                    "skd,kgdf->kgsf", block_keys.astype(jnp.float32), key_map, precision=precise
                )
            )
            features = features * in_state[None, None, :, None]
            result[-2] = carry_in[-2] + jnp.einsum(
                "kgsf,skd->kgfd", features, block_values.astype(jnp.float32), precision=precise
            )
            result[-1] = carry_in[-1] + jnp.sum(features, axis=2)
            return tuple(result)

        return lax.cond(first_row <= last_row, compute, skip_block, running)

    folded = lax.fori_loop(0, piece_rows // step_rows, attend, initial)
    teacher = folded[2] / folded[1][..., None]
    stacked = jnp.stack([keys, values])
    moved = shifted(stacked, "ctx", 1)
    prev_keys, prev_values = (moved[0], moved[1])
    has_prev = (my_block > 0).astype(jnp.float32)
    window_keys = jnp.concatenate([prev_keys, keys], axis=0)
    window_values = jnp.concatenate([prev_values, values], axis=0)
    column = jnp.arange(2 * block_len, dtype=jnp.int32)
    row_index = jnp.arange(block_len, dtype=jnp.int32)
    allowed = (column[None, :] < block_len) & (my_block > 0) | (column[None, :] >= block_len) & (
        column[None, :] - block_len <= row_index[:, None]
    )
    scores = (
        jnp.einsum("tkgd,skd->kgts", grouped_q, window_keys, preferred_element_type=jnp.float32)
        * score_scale
    )
    scores = jnp.where(allowed, scores, big_negative)
    row_max = jnp.max(scores, axis=-1)
    window_weight = jnp.where(allowed, jnp.exp(scores - row_max[..., None]), 0.0)
    window_den = jnp.sum(window_weight, axis=-1)
    window_num = jnp.einsum(
        "kgts,skd->kgtd",
        window_weight.astype(jnp.bfloat16),
        window_values,
        preferred_element_type=jnp.float32,
    )
    key_proj = jnp.einsum(
        "skd,kgdf->kgsf", prev_keys.astype(jnp.float32), key_map, precision=precise
    )
    state, norm = (folded[-2], folded[-1])
    query_proj = jnp.einsum(
        "tkgd,kgdf->kgtf", grouped_q.astype(jnp.float32), query_map, precision=precise
    )
    query_feats = feature_map(query_proj)
    decay = jnp.exp(-row_max)
    far_num = decay[..., None] * jnp.einsum(
        "kgtf,kgfd->kgtd", query_feats, state, precision=precise
    )
    far_den = decay * jnp.einsum("kgtf,kgf->kgt", query_feats, norm, precision=precise)
    denominator = window_den + far_den
    mix = (window_num + far_num) / denominator[..., None]
    student = jnp.transpose(mix.astype(jnp.bfloat16), (2, 0, 1, 3)).reshape(
        block_len, head_count, head_width
    )
    mismatch = mix - teacher
    grad_num = mismatch / denominator[..., None]
    grad_den = -jnp.sum(mismatch * mix, axis=-1) / denominator
    lifted = decay[..., None] * query_feats
    grad_state = jnp.einsum("kgtf,kgtd->kgfd", lifted, grad_num, precision=precise)
    grad_norm = jnp.einsum("kgtf,kgt->kgf", lifted, grad_den, precision=precise)
    grad_qfeat = decay[..., None] * (
        jnp.einsum("kgfd,kgtd->kgtf", state, grad_num, precision=precise)
        + norm[:, :, None, :] * grad_den[..., None]
    )
    later_state, later_norm = carried_in(
        (grad_state, grad_norm),
        "ctx",
        add_pair,
        (jnp.zeros_like(grad_state), jnp.zeros_like(grad_norm)),
    )
    grad_kfeat = (
        jnp.einsum(
            "kgfd,skd->kgsf", later_state, prev_values.astype(jnp.float32), precision=precise
        )
        + later_norm[:, :, None, :]
    ) * has_prev
    grad_query = jnp.einsum(
        "tkgd,kgtf->kgdf",
        grouped_q.astype(jnp.float32),
        feature_pull(query_proj, grad_qfeat),
        precision=precise,
    )
    grad_key = jnp.einsum(
        "skd,kgsf->kgdf",
        prev_keys.astype(jnp.float32),
        feature_pull(key_proj, grad_kfeat),
        precision=precise,
    )
    gradients = jnp.concatenate([grad_query, grad_key], axis=-1).reshape(
        head_count, head_width, 2 * feature_len
    )
    entry_count = gradients.size * lax.axis_size("head")
    summed = lax.psum(gradients, "ctx")
    squares = lax.psum(jnp.sum(summed * summed), "head")
    update = summed / jnp.sqrt(squares / entry_count + 1e-06)
    return (student, update)


f32, bf16 = jnp.float32, jnp.bfloat16
NN = (((1,), (0,)), ((), ()))
NT = (((1,), (1,)), ((), ()))
TN = (((0,), (0,)), ((), ()))


def mxu(a, b, dims):
    return lax.dot_general(a, b, dims, preferred_element_type=f32)


def split(x, pieces):
    out = []
    for _ in range(pieces):
        piece = x.astype(bf16)
        out.append(piece)
        x = x - piece.astype(f32)
    return out


def cat(parts, axis):
    return jnp.concatenate(parts, axis=axis)


def exact_by_wide(a, b, dims):
    return mxu(cat([a, a], dims[0][0][0]), cat(split(b, 2), dims[0][1][0]), dims)


def wide_by_exact(a, b, dims):
    return mxu(cat(split(a, 2), dims[0][0][0]), cat([b, b], dims[0][1][0]), dims)


def wide_by_rounded(a, b, dims):
    return wide_by_exact(a, b.astype(bf16), dims)


def half_sum(x, halves):
    return wide_by_exact(x, halves, NN)


def half_softmax(u, is_upper, halves):
    top = jnp.max(jnp.where(is_upper, u, big_negative), axis=-1, keepdims=True)
    low = jnp.max(jnp.where(is_upper, big_negative, u), axis=-1, keepdims=True)
    e = jnp.exp(u - jnp.where(is_upper, top, low))
    return e / half_sum(e, halves)


def remote(src, dst, send_sem, recv_sem, **where):
    return pltpu.make_async_remote_copy(
        src_ref=src,
        dst_ref=dst,
        send_sem=send_sem,
        recv_sem=recv_sem,
        device_id=where,
        device_id_type=pl.DeviceIdType.MESH,
    )


def each(count, body):
    def step(index, carry):
        body(index)
        return carry

    lax.fori_loop(0, count, step, 0)


def head_kernel(
    q_hbm, k_hbm, v_hbm, w_hbm, student_hbm, grad_hbm, scale_hbm,
    q_raw, k_raw, v_raw, w_ref, qt_ref, kvt_ref, q_all, kv_all, st_all, st_turned, mix_ref,
    own_grad, gat_ref, sq_own, sq_all, sq_ref, scale_ref, own_ref, sum_ref, pre_ref, pre_norm_ref,
    score_ref, near_ref, kfeat_ref, gstate_ref, gnorm_ref, wq_ref, wk_ref, gq_ref,
    q_sem, kv_send, kv_recv, local_sem, st_sem, g_send, g_recv, g_hop, g_final, sq_sem, fetch_sem,
    w_send, w_recv, out_sem, swap_sem,
):
    blocks, length, width = qt_ref.shape
    planes = kvt_ref.shape[0]
    group = blocks // planes
    me, side = lax.axis_index("ctx"), lax.axis_index("head")
    plane, spot = me // group, me % group
    row, column = spot // 2, spot % 2
    native = row == side
    mine = plane * group + 2 * column + side
    features = w_ref.shape[1] // 2
    rows = 2 * length
    steps, pairs = blocks // 2, blocks // 4
    middle = pairs - 1

    def pair_block(p, u):
        return jnp.where(u < 2, 4 * p + u, blocks - 4 - 4 * p + u)

    my_pair = jnp.where(row == 0, plane, planes - 1 - plane)
    barrier = pltpu.get_barrier_semaphore()

    def greet(t, h):
        pl.semaphore_signal(
            barrier, inc=1, device_id={"ctx": t, "head": h}, device_id_type=pl.DeviceIdType.MESH
        )

    def greet_side(d):
        t = (me + d) % blocks

        @pl.when(jnp.logical_not(native & (t == me)))
        def _():
            greet(t, row)

    fetches = [
        pltpu.make_async_copy(src, dst, fetch_sem.at[n])
        for n, (src, dst) in enumerate([(k_hbm, k_raw), (v_hbm, v_raw), (q_hbm, q_raw)])
    ]
    for fetch in fetches:
        fetch.start()
    each(blocks, greet_side)
    each(blocks // 2, lambda n: greet((n // 2) * group + 2 * side + n % 2, 1 - row))
    own_w = pltpu.make_async_copy(w_hbm.at[mine], w_ref, local_sem.at[2])

    @pl.when(native)
    def _():
        own_w.start()

    def flip(index, d):
        bit = 1
        while bit <= d:
            if d & bit:
                index = index + bit - 2 * bit * ((index // bit) % 2)
            bit *= 2
        return index

    def w_copy():
        other = plane * group + 2 * column + 1 - side
        return remote(w_hbm.at[other], w_ref, w_send.at[0], w_recv.at[0], ctx=me, head=1 - side)

    def kv_land(g):
        return remote(
            kvt_ref.at[g], kv_all.at[me], kv_send.at[0], kv_recv.at[plane],
            ctx=g * group + 2 * side + column, head=row,
        )

    def landed_block(z):
        return z * group + 2 * side + column

    def crossed_block(z):
        return z * group + 2 * side + 1 - column

    def kv_across(z):
        block = landed_block(z)
        return remote(
            kv_all.at[block], kv_all.at[block], kv_send.at[1], kv_recv.at[planes + z],
            ctx=plane * group + 2 * row + 1 - column, head=side,
        )

    def kv_share(block, z):
        return remote(
            kv_all.at[block], kv_all.at[block], kv_send.at[2], kv_recv.at[2 * planes + z],
            ctx=me, head=1 - side,
        )

    def q_copy(j):
        return remote(
            qt_ref.at[j], q_all.at[me], q_sem.at[pairs], q_sem.at[my_pair],
            ctx=(j // group) * group + 2 * side + (j % group) // 2, head=j % 2,
        )

    def bulk(ref, send_sem, recv_sem):
        return remote(ref, ref, send_sem, recv_sem, ctx=me, head=1 - side)

    def kv_arrival(first, count, n):
        return bulk(kv_all.at[pl.ds(first, count)], kv_send.at[0], kv_recv.at[n])

    def st_copy(b):
        return remote(mix_ref.at[b], st_all.at[mine], st_sem.at[0], st_sem.at[1], ctx=b, head=row)

    def g_column(part, z):
        return remote(
            own_grad.at[part], gat_ref.at[part, mine], g_send.at[0], g_recv.at[part, 2 * plane + side],
            ctx=z * group + spot, head=row,
        )

    def g_pass(part, z, h, d):
        piece = gat_ref.at[part, z * group + 2 * column + h]
        arrival = g_hop.at[part, z] if (d == 1) == (h == 0) else g_final.at[0]
        return remote(
            piece, piece, g_send.at[d], arrival, ctx=plane * group + flip(spot, d), head=side
        )

    def g_forward(part, z):
        j = z * group + jnp.where(native, 2 - 2 * column, 2 * column + 1)
        piece = gat_ref.at[part, j]
        target = jnp.where(native, flip(spot, 2), flip(spot, 1))
        return remote(
            piece, piece, g_send.at[3], g_final.at[0], ctx=plane * group + target, head=side
        )

    def g_landing(part, j, n):
        return bulk(gat_ref.at[part, j], g_send.at[0], g_recv.at[part, n])

    def sq_copy(t):
        return remote(
            sq_own, sq_all.at[mine], sq_sem.at[0], sq_sem.at[1], ctx=t, head=row
        )

    def unless_own(b, body):
        @pl.when(jnp.logical_not(native & (b == me)))
        def _():
            body()

    rate = math.log2(math.e) / math.sqrt(width)
    lane = lax.broadcasted_iota(jnp.int32, (rows, 2 * features), 1)
    is_upper = lane < features
    row_half = lax.broadcasted_iota(jnp.int32, (2 * features, 2 * features), 0) < features
    col_half = lax.broadcasted_iota(jnp.int32, (2 * features, 2 * features), 1) < features
    halves = jnp.where(row_half == col_half, 1.0, 0.0).astype(bf16)
    square = (rows, rows)
    causal = lax.broadcasted_iota(jnp.int32, square, 1) <= lax.broadcasted_iota(jnp.int32, square, 0)
    for part, (fetch, raw) in enumerate(zip(fetches, (k_raw, v_raw))):
        fetch.wait()
        kvt_ref[:, part] = jnp.transpose(raw[...], (1, 0, 2))
    own_kv = pltpu.make_async_copy(kvt_ref.at[plane], kv_all.at[me], local_sem.at[0])

    @pl.when(native)
    def _():
        own_kv.start()

    pl.semaphore_wait(barrier, jnp.where(native, 3 * blocks // 2 - 1, 3 * blocks // 2))
    for d in range(planes):
        g = flip(plane, d)
        if d == 0:
            @pl.when(jnp.logical_not(native))
            def _():
                kv_land(g).start()
        else:
            kv_land(g).start()

    @pl.when(native)
    def _():
        w_copy().start()

    fetches[2].wait()
    qt_ref[...] = jnp.transpose(q_raw[...], (1, 0, 2))
    own_q = pltpu.make_async_copy(qt_ref.at[mine], q_all.at[me], local_sem.at[1])

    @pl.when(native)
    def _():
        own_q.start()
        own_kv.wait()

    def land(d):
        z = flip(plane, d)
        block = landed_block(z)
        unless_own(block, lambda: kv_arrival(block, 1, z).wait_recv())
        kv_across(z).start()
        kv_share(block, z).start()

    def cross(d):
        z = flip(plane, d)
        block = crossed_block(z)
        kv_arrival(block, 1, planes + z).wait_recv()
        kv_share(block, z).start()

    def load(part, i):
        if part == 0:
            return q_all[pl.ds(2 * i, 2)].reshape(rows, width)
        return kv_all[pl.ds(2 * i, 2), part - 1].reshape(rows, width)

    def either(less, body):
        for flag, count in ((native, less), (jnp.logical_not(native), 0)):
            @pl.when(flag)
            def _():
                body(count)

    def q_arrived(p):
        here = native & (p == my_pair)
        for flag, count in ((here, 3), (jnp.logical_not(here), 4)):
            @pl.when(flag)
            def _():
                bulk(q_all.at[pl.ds(0, count)], q_sem.at[pairs], q_sem.at[p]).wait_recv()

    def send_student(b):
        unless_own(b, lambda: st_copy(b).start())

        @pl.when(native & (b == me))
        def _():
            st_all[mine] = mix_ref[me]

    def send_grad(part):
        for d in range(planes):
            z = flip(plane, d)
            if d == 0:
                @pl.when(native)
                def _():
                    gat_ref[part, mine] = own_grad[part]

                @pl.when(jnp.logical_not(native))
                def _():
                    g_column(part, z).start()
            else:
                g_column(part, z).start()

    def relay_grad(part):
        @pl.when(native)
        def _():
            for z in range(planes):
                for h in range(2):
                    j = flip(plane, z) * group + 2 * column + h

                    @pl.when(j != mine)
                    def _():
                        g_landing(part, j, 2 * flip(plane, z) + h).wait_recv()

                    for d in range(1, group - 1):
                        g_pass(part, flip(plane, z), h, d).start()

    def hop_grad(part):
        for d in range(planes):
            z = flip(plane, d)
            bulk(gat_ref.at[part, z], g_send.at[0], g_hop.at[part, z]).wait_recv()
            g_forward(part, z).start()

    def key_side(pair):
        kv_arrival(group * pair, 2, 2 * planes + pair).wait_recv()
        steps_of = (2 * pair, 2 * pair + 1)
        ks, vs = ([load(part, i) for i in steps_of] for part in (1, 2))
        kfs = [
            half_softmax(mxu(cat([k, k, k], 1), wk_ref[...], NN), is_upper, halves) for k in ks
        ]
        for i, kf, v in zip(steps_of, kfs, vs):
            kfeat_ref[i] = kf
            for h in range(2):
                part = kf[h * length:(h + 1) * length]
                own_ref[2 * i + h] = wide_by_exact(part, v[h * length:(h + 1) * length], TN)
                sum_ref[2 * i + h] = jnp.sum(part, axis=0, keepdims=True)

    def push(n):
        p = (my_pair + pairs - n // group) % pairs
        j = jnp.where(side == 0, p, planes - 1 - p) * group + n % group

        @pl.when(jnp.logical_not(native & (j == mine)))
        def _():
            q_copy(j).start()

    def plane_keys(z):
        each(group // 4, lambda u: key_side(z * (group // 4) + u))

    def push_turns(first, last):
        each((last - first) * group, lambda n: push(first * group + n))

    land(0)
    @pl.when(native)
    def _():
        own_w.wait()

    @pl.when(jnp.logical_not(native))
    def _():
        w_copy().wait_recv()

    w = w_ref[...]
    wq, wk = w[:, :features], w[:, features:]
    wq_ref[...] = cat(split(cat([wq, -wq], 1), 3), 0)
    wk_ref[...] = cat(split(cat([wk, -wk], 1), 3), 0)
    gq_ref[...] = jnp.zeros_like(gq_ref)
    land(1)
    push_turns(0, 1)
    cross(0)
    land(2)
    cross(1)
    land(3)
    push_turns(1, 2)
    plane_keys(flip(plane, 0))
    cross(2)
    plane_keys(flip(plane, 1))
    cross(3)
    push_turns(2, pairs)
    plane_keys(flip(plane, 2))
    plane_keys(flip(plane, 3))

    @pl.when(native)
    def _():
        own_q.wait()

    for b in range(2):
        pre_ref[b] = jnp.zeros_like(pre_ref[b])
        pre_norm_ref[b] = jnp.zeros_like(pre_norm_ref[b])

    def prefix(b):
        pre_ref[b + 2] = pre_ref[b + 1] + own_ref[b]
        pre_norm_ref[b + 2] = pre_norm_ref[b + 1] + sum_ref[b]

    each(blocks - 2, prefix)

    def forward(turn, carry):
        p = (my_pair + turn) % pairs
        a, b = 2 * p, steps - 1 - 2 * p
        q_arrived(p)
        tokens = (a, b)
        qs = [load(0, i) for i in tokens]
        vs = [load(2, i) for i in tokens]
        wide_b = b // 2

        def pair_of(part, j):
            return cat([load(part, 2 * j), load(part, 2 * j + 1)], 0)

        def fold(x, combine):
            while x.shape[1] > length:
                half = x.shape[1] // 2
                x = combine(x[:, :half], x[:, half:])
            return x

        s = mxu(qs[0], load(1, a), NT) * rate
        s_a = jnp.where(causal, s, big_negative)
        near_ref[0] = s_a
        s = mxu(qs[1], pair_of(1, wide_b), NT) * rate
        s_b = [s[:, :rows], jnp.where(causal, s[:, rows:], big_negative)]
        near_ref[1], near_ref[2] = s_b
        peaks = [fold(s_a, jnp.maximum), fold(jnp.maximum(*s_b), jnp.maximum)]

        def far_tile(m):
            first = m < p
            return first, jnp.where(first, a, b), jnp.where(first, m, m - p)

        for m in range(middle):
            first, i, j = far_tile(m)
            s = mxu(load(0, i), pair_of(1, j), NT) * rate
            score_ref[m] = s
            top = fold(s, jnp.maximum)
            peaks = [
                jnp.maximum(peaks[0], jnp.where(first, top, big_negative)),
                jnp.maximum(peaks[1], jnp.where(first, big_negative, top)),
            ]
        tops = [jnp.max(x, axis=-1, keepdims=True) for x in peaks]

        weight = jnp.exp2(near_ref[0] - tops[0])
        sums = [fold(weight, jnp.add)]
        accs = [mxu(weight.astype(bf16), vs[0], NN)]
        weight = jnp.exp2(cat([near_ref[1], near_ref[2]], 1) - tops[1])
        sums.append(fold(weight, jnp.add))
        accs.append(mxu(weight.astype(bf16), pair_of(2, wide_b), NN))
        for m in range(middle):
            first, i, j = far_tile(m)
            weight = jnp.exp2(score_ref[m] - jnp.where(first, tops[0], tops[1]))
            part = fold(weight, jnp.add)
            prod = mxu(weight.astype(bf16), pair_of(2, j), NN)
            sums = [sums[0] + jnp.where(first, part, 0.0), sums[1] + jnp.where(first, 0.0, part)]
            accs = [accs[0] + jnp.where(first, prod, 0.0), accs[1] + jnp.where(first, 0.0, prod)]
        teachers = [
            acc / jnp.sum(total, axis=-1, keepdims=True) for acc, total in zip(accs, sums)
        ]

        def halves_of(f):
            return [cat([f(x, 0), f(x, 1)], 0) for x in range(2)]

        def cut(x, half):
            return x[half * length:(half + 1) * length]

        last_far = score_ref[jnp.maximum(p - 1, 0), :length, 3 * length:]
        prevs = [
            cat([jnp.where(p > 0, last_far, big_negative), near_ref[0, length:, :length]], 0),
            cat([near_ref[1, :length, length:], near_ref[2, length:, :length]], 0),
        ]
        owns = [
            cat([near_ref[k, :length, :length], near_ref[k, length:, length:]], 0) for k in (0, 2)
        ]
        win_maxs = [
            jnp.max(jnp.maximum(prev, own), axis=-1, keepdims=True)
            for prev, own in zip(prevs, owns)
        ]
        p_prevs = [jnp.exp2(x - top) for x, top in zip(prevs, win_maxs)]
        p_owns = [jnp.exp2(x - top) for x, top in zip(owns, win_maxs)]
        win_dens = [jnp.sum(x + y, axis=-1, keepdims=True) for x, y in zip(p_prevs, p_owns)]
        p_wins = [cat([x.astype(bf16), y.astype(bf16)], 1) for x, y in zip(p_prevs, p_owns)]
        v_befores = [kv_all[jnp.maximum(2 * i - 1, 0), 1] for i in tokens]
        v_wins = [
            (cat([before, v[:length]], 0), v) for before, v in zip(v_befores, vs)
        ]
        win_nums = halves_of(lambda x, h: mxu(cut(p_wins[x], h), v_wins[x][h], NN))

        qfs = [
            half_softmax(mxu(cat([q, q, q], 1), wq_ref[...], NN), is_upper, halves) for q in qs
        ]
        states = [[pre_ref[2 * i], pre_ref[2 * i + 1]] for i in tokens]
        norms = [
            cat(
                [
                    jnp.broadcast_to(pre_norm_ref[2 * i + h], (length, 2 * features))
                    for h in range(2)
                ],
                0,
            )
            for i in tokens
        ]
        decays = [jnp.exp2(-top) for top in win_maxs]
        fars = halves_of(lambda x, h: wide_by_rounded(cut(qfs[x], h), states[x][h], NN))
        dens = [
            win_den + decay * jnp.sum(qf * norm, axis=-1, keepdims=True)
            for win_den, decay, qf, norm in zip(win_dens, decays, qfs, norms)
        ]
        mixes = [
            (num + decay * far) / den
            for num, decay, far, den in zip(win_nums, decays, fars, dens)
        ]
        for i, mix in zip(tokens, mixes):
            mix_ref[pl.ds(2 * i, 2)] = mix.astype(bf16).reshape(2, length, width)
        @pl.when(turn < pairs - 1)
        def _():
            each(4, lambda u: send_student(pair_block(p, u)))

        mismatches = [mix - teacher for mix, teacher in zip(mixes, teachers)]
        g_nums = [x / den for x, den in zip(mismatches, dens)]
        g_dens = [
            -jnp.sum(x * mix, axis=-1, keepdims=True) / den
            for x, mix, den in zip(mismatches, mixes, dens)
        ]
        lifts = [decay * qf for decay, qf in zip(decays, qfs)]
        pulled_norms = [lift * g_den for lift, g_den in zip(lifts, g_dens)]
        for x, i in enumerate(tokens):
            for h in range(2):
                gstate_ref[2 * i + h] = wide_by_rounded(cut(lifts[x], h), cut(g_nums[x], h), TN)
                gnorm_ref[2 * i + h] = jnp.sum(cut(pulled_norms[x], h), axis=0, keepdims=True)
        pulled = halves_of(lambda x, h: wide_by_rounded(cut(g_nums[x], h), states[x][h], NT))
        g_qfs = [
            decay * (pull + norm * g_den)
            for decay, pull, norm, g_den in zip(decays, pulled, norms, g_dens)
        ]
        d_qs = [qf * (g - half_sum(qf * g, halves)) for qf, g in zip(qfs, g_qfs)]
        gq_ref[...] += wide_by_exact(d_qs[0], qs[0], TN) + wide_by_exact(d_qs[1], qs[1], TN)
        return carry

    lax.fori_loop(0, pairs, forward, 0)
    own_grad[0] = (gq_ref[:features] - gq_ref[features:]).astype(bf16)
    send_grad(0)

    for b in range(blocks - 2, 1, -1):
        gstate_ref[b] = gstate_ref[b] + gstate_ref[b + 1]
        gnorm_ref[b] = gnorm_ref[b] + gnorm_ref[b + 1]

    def backward(group_of):
        ks, vs, kfs = ([f(i) for i in group_of] for f in (lambda i: load(1, i), lambda i: load(2, i), lambda i: kfeat_ref[i]))
        g_kfs = [
            cat(
                [
                    exact_by_wide(v[h * length:(h + 1) * length], gstate_ref[2 * i + h + 2], NT)
                    + gnorm_ref[2 * i + h + 2]
                    for h in range(2)
                ],
                0,
            )
            for i, v in zip(group_of, vs)
        ]
        d_ks = [kf * (g - half_sum(kf * g, halves)) for kf, g in zip(kfs, g_kfs)]
        return [wide_by_exact(d_k, k, TN) for d_k, k in zip(d_ks, ks)]

    gk = sum(backward(range(steps // 2)) + backward(range(steps // 2, steps - 1)))
    own_grad[1] = (gk[:features] - gk[features:]).astype(bf16)
    send_grad(1)
    square = own_grad[...].astype(f32).reshape(2 * features, width)
    sq_own[...] = jnp.sum(square * square, axis=0, keepdims=True)
    each(blocks, lambda n: unless_own((me + n) % blocks, lambda: sq_copy((me + n) % blocks).start()))

    @pl.when(native)
    def _():
        sq_all[mine] = sq_own[...]

    each(4, lambda u: send_student(pair_block((my_pair + pairs - 1) % pairs, u)))
    relay_grad(0)
    relay_grad(1)
    hop_grad(0)
    hop_grad(1)

    either(1, lambda n: bulk(st_all.at[pl.ds(0, blocks - n)], st_sem.at[0], st_sem.at[1]).wait_recv())
    st_turned[...] = jnp.transpose(st_all[...], (1, 0, 2))
    student_out = pltpu.make_async_copy(st_turned, student_hbm, out_sem.at[0])
    student_out.start()

    either(1, lambda n: bulk(sq_all.at[pl.ds(0, blocks - n)], sq_sem.at[0], sq_sem.at[1]).wait_recv())
    sq_ref[0] = jnp.sum(sq_all[...], axis=0)
    swap = remote(
        sq_ref.at[0], sq_ref.at[1], swap_sem.at[0], swap_sem.at[1], ctx=me, head=1 - side
    )
    swap.start()

    either(1, lambda n: bulk(qt_ref.at[pl.ds(0, blocks - n)], q_sem.at[pairs], q_sem.at[0]).wait_send())
    either(1, lambda n: bulk(mix_ref.at[pl.ds(0, blocks - n)], st_sem.at[0], st_sem.at[1]).wait_send())
    either(1, lambda n: bulk(sq_all.at[pl.ds(0, blocks - n)], sq_sem.at[0], sq_sem.at[1]).wait_send())
    either(1, lambda n: bulk(kvt_ref.at[pl.ds(0, planes - n)], kv_send.at[0], kv_recv.at[0]).wait_send())
    bulk(kv_all.at[pl.ds(0, planes)], kv_send.at[1], kv_recv.at[0]).wait_send()
    bulk(kv_all.at[pl.ds(0, 2 * planes)], kv_send.at[2], kv_recv.at[0]).wait_send()
    either(2, lambda n: bulk(gat_ref.at[0, pl.ds(0, 2 * planes - n)], g_send.at[0], g_final.at[0]).wait_send())

    @pl.when(native)
    def _():
        w_copy().wait_send()

    swap.wait()
    entries = 2 * blocks * width * 2 * features
    total = jnp.sum(sq_ref[0] + sq_ref[1], keepdims=True)
    scale_ref[...] = jnp.broadcast_to(1.0 / jnp.sqrt(total / entries + 1e-06), (8, width))
    scale_out = pltpu.make_async_copy(scale_ref, scale_hbm, out_sem.at[2])
    scale_out.start()

    @pl.when(native)
    def _():
        bulk(gat_ref.at[0, pl.ds(0, 2 * planes)], g_send.at[0], g_final.at[0]).wait_recv()

    @pl.when(jnp.logical_not(native))
    def _():
        bulk(gat_ref.at[:, pl.ds(0, 3 * planes)], g_send.at[0], g_final.at[0]).wait_recv()

    grad_out = pltpu.make_async_copy(gat_ref, grad_hbm, out_sem.at[1])
    grad_out.start()

    @pl.when(native)
    def _():
        for d in range(1, group - 1):
            bulk(gat_ref.at[0], g_send.at[d], g_final.at[0]).wait_send()

    bulk(gat_ref.at[0, pl.ds(0, 2 * planes)], g_send.at[3], g_final.at[0]).wait_send()
    student_out.wait()
    scale_out.wait()
    grad_out.wait()


def finish_kernel(
    student_hbm, grad_hbm, scale_hbm, student_out, update_out,
    st_ref, grad_ref, scale_ref, update_ref, in_sem, out_sem,
):
    parts, blocks, features, width = grad_ref.shape
    chunks = in_sem.shape[0] - 2
    each_len = blocks // chunks
    fetches = [
        pltpu.make_async_copy(
            grad_hbm.at[:, pl.ds(n * each_len, each_len)],
            grad_ref.at[:, pl.ds(n * each_len, each_len)], in_sem.at[n],
        )
        for n in range(chunks)
    ]
    scale_in = pltpu.make_async_copy(scale_hbm, scale_ref, in_sem.at[chunks])
    student_in = pltpu.make_async_copy(student_hbm, st_ref, in_sem.at[chunks + 1])
    scale_in.start()
    student_in.start()
    for fetch in fetches:
        fetch.start()
    scale_in.wait()
    scale = scale_ref[:1]
    stores = [pltpu.make_async_copy(st_ref, student_out, out_sem.at[chunks])]
    student_in.wait()
    stores[0].start()
    for n, fetch in enumerate(fetches):
        fetch.wait()
        for j in range(n * each_len, (n + 1) * each_len):
            piece = cat([grad_ref[0, j], grad_ref[1, j]], 0).astype(f32)
            update_ref[j] = piece.T * scale
        stores.append(
            pltpu.make_async_copy(
                update_ref.at[pl.ds(n * each_len, each_len)],
                update_out.at[pl.ds(n * each_len, each_len)], out_sem.at[n],
            )
        )
        stores[-1].start()
    for store in stores:
        store.wait()


def whole_head(queries, keys, values, w):
    length, blocks, width = queries.shape
    planes = keys.shape[1]
    group = blocks // planes
    double = w.shape[2]
    half = double // 2
    rows, steps = 2 * length, blocks // 2
    vmem, dma = pltpu.VMEM, pltpu.SemaphoreType.DMA
    hbm = pl.BlockSpec(memory_space=pltpu.MemorySpace.HBM)
    limit = 67_043_328
    student, grads, scale = pl.pallas_call(
        head_kernel,
        out_shape=(
            jax.ShapeDtypeStruct((length, blocks, width), bf16),
            jax.ShapeDtypeStruct((2, blocks, half, width), bf16),
            jax.ShapeDtypeStruct((8, width), f32),
        ),
        in_specs=[hbm] * 4,
        out_specs=(hbm,) * 3,
        scratch_shapes=[
            vmem((length, blocks, width), bf16),
            vmem((length, planes, width), bf16),
            vmem((length, planes, width), bf16),
            vmem((width, double), f32),
            vmem((blocks, length, width), bf16),
            vmem((planes, 2, length, width), bf16),
            vmem((blocks, length, width), bf16),
            vmem((blocks, 2, length, width), bf16),
            vmem((blocks, length, width), bf16),
            vmem((length, blocks, width), bf16),
            vmem((blocks, length, width), bf16),
            vmem((2, half, width), bf16),
            vmem((2, blocks, half, width), bf16),
            vmem((1, width), f32),
            vmem((blocks, 1, width), f32),
            vmem((2, 1, width), f32),
            vmem((8, width), f32),
            vmem((blocks, double, width), f32),
            vmem((blocks, 1, double), f32),
            vmem((blocks, double, width), f32),
            vmem((blocks, 1, double), f32),
            vmem((blocks // 4 - 1, rows, 2 * rows), f32),
            vmem((3, rows, rows), f32),
            vmem((steps, rows, double), f32),
            vmem((blocks, double, width), f32),
            vmem((blocks, 1, double), f32),
            vmem((3 * width, double), bf16),
            vmem((3 * width, double), bf16),
            vmem((double, width), f32),
            dma((blocks // 4 + 1,)),
            dma((3,)),
            dma((3 * planes,)),
            dma((3,)),
            dma((2,)),
            dma((group,)),
            dma((2, 2 * planes)),
            dma((2, planes)),
            dma((1,)),
            dma((2,)),
            dma((3,)),
            dma((1,)),
            dma((1,)),
            dma((3,)),
            dma((2,)),
        ],
        compiler_params=pltpu.CompilerParams(
            vmem_limit_bytes=limit, collective_id=0, has_side_effects=True
        ),
    )(queries, keys, values, w)
    chunks = 2
    return pl.pallas_call(
        finish_kernel,
        out_shape=(
            jax.ShapeDtypeStruct((length, blocks, width), bf16),
            jax.ShapeDtypeStruct((blocks, width, double), f32),
        ),
        in_specs=[hbm] * 3,
        out_specs=(hbm,) * 2,
        scratch_shapes=[
            vmem((length, blocks, width), bf16),
            vmem((2, blocks, half, width), bf16),
            vmem((8, width), f32),
            vmem((blocks, width, double), f32),
            dma((chunks + 2,)),
            dma((chunks + 1,)),
        ],
        compiler_params=pltpu.CompilerParams(vmem_limit_bytes=limit),
    )(student, grads, scale)


def head_shards(queries, keys, values, feature_weight):
    return whole_head(queries, keys, values, feature_weight)


def shards(queries, keys, values, feature_weight):
    count = lax.axis_size("ctx")
    width = queries.shape[2]
    fits = queries.shape[1] == count and count == 4 * keys.shape[1] and lax.axis_size("head") == 2 and count % 4 == 0 and keys.shape[1] == 4 and count * queries.shape[0] <= 4096
    fits = fits and queries.shape[1] // keys.shape[1] % 4 == 0 and queries.shape[0] == width and feature_weight.shape[2] == width
    body = head_shards if fits else general_shards
    return body(queries, keys, values, feature_weight)


def solution(mesh):
    return jax.shard_map(
        shards,
        mesh=mesh,
        in_specs=(
            P("ctx", "head", None),
            P("ctx", "head", None),
            P("ctx", "head", None),
            P("head", None, None),
        ),
        out_specs=(P("ctx", "head", None), P("head", None, None)),
        check_vma=False,
    )
```

```python
import functools
import math

import jax
import jax.numpy as jnp
from jax import lax
from jax.experimental import pallas as pl
from jax.experimental.pallas import tpu as pltpu
from jax.sharding import PartitionSpec as P

precise = lax.Precision.HIGHEST
big_negative = -1e30


def shifted(shard, axis, by):
    devices = lax.axis_size(axis)
    pairs = [(i, i + by) for i in range(devices) if 0 <= i + by < devices]
    return lax.ppermute(shard, axis, pairs)


def carried_in(part, axis, combine, identity):
    count = lax.axis_size(axis)
    place = lax.axis_index(axis)
    ahead = count - 1 - place
    gathered = jax.tree.map(lambda a: lax.all_gather(a, axis), part)
    state = jax.tree.map(lambda a, e: jnp.zeros_like(a) + jnp.asarray(e, a.dtype), part, identity)

    def one(step, state):
        source = count - 1 - step
        return combine(
            state, jax.tree.map(lambda a: lax.dynamic_index_in_dim(a, source, 0, False), gathered)
        )

    return lax.fori_loop(0, ahead, one, state)


def feature_map(projection):
    return jnp.concatenate(
        [jax.nn.softmax(projection, axis=-1), jax.nn.softmax(-projection, axis=-1)], axis=-1
    )


def feature_pull(projection, upstream):
    half_len = upstream.shape[-1] // 2
    upper = jax.nn.softmax(projection, axis=-1)
    lower = jax.nn.softmax(-projection, axis=-1)
    grad_upper = upstream[..., :half_len]
    grad_lower = upstream[..., half_len:]
    upper_part = upper * (grad_upper - jnp.sum(upper * grad_upper, axis=-1, keepdims=True))
    lower_part = lower * (grad_lower - jnp.sum(lower * grad_lower, axis=-1, keepdims=True))
    return upper_part - lower_part


def add_pair(earlier, later):
    return (earlier[0] + later[0], earlier[1] + later[1])


def skip_block(carry_in):
    return carry_in


def general_shards(queries, keys, values, feature_weight):
    block_len, head_count, head_width = queries.shape
    kv_count = keys.shape[1]
    group_size = head_count // kv_count
    feature_len = feature_weight.shape[2] // 2
    my_block = lax.axis_index("ctx")
    score_scale = 1.0 / math.sqrt(head_width)
    grouped_q = queries.reshape(block_len, kv_count, group_size, head_width)
    maps_weight = feature_weight.reshape(kv_count, group_size, head_width, 2 * feature_len)
    query_map = maps_weight[..., :feature_len]
    key_map = maps_weight[..., feature_len:]
    query_pos = my_block * block_len + jnp.arange(block_len, dtype=jnp.int32)
    prev_start = (my_block - 1) * block_len
    last_row = my_block * block_len + block_len - 1
    initial = [
        jnp.full((kv_count, group_size, block_len), big_negative, jnp.float32),
        jnp.zeros((kv_count, group_size, block_len), jnp.float32),
        jnp.zeros((kv_count, group_size, block_len, head_width), jnp.float32),
    ]
    initial = initial + [
        jnp.zeros((kv_count, group_size, 2 * feature_len, head_width), jnp.float32),
        jnp.zeros((kv_count, group_size, 2 * feature_len), jnp.float32),
    ]
    initial = tuple(initial)
    piece_keys = lax.all_gather(keys, "ctx", axis=0, tiled=True)
    piece_values = lax.all_gather(values, "ctx", axis=0, tiled=True)
    piece_rows = piece_keys.shape[0]
    step_rows = math.gcd(piece_rows, 512)

    def attend(step_index, running):
        first_row = step_index * step_rows
        block_keys = lax.dynamic_slice_in_dim(piece_keys, step_index * step_rows, step_rows, 0)
        block_values = lax.dynamic_slice_in_dim(piece_values, step_index * step_rows, step_rows, 0)
        key_pos = first_row + jnp.arange(step_rows, dtype=jnp.int32)

        def compute(carry_in):
            row_max, running_sum, accumulated = (carry_in[0], carry_in[1], carry_in[2])
            scores = (
                jnp.einsum(
                    "tkgd,skd->kgts", grouped_q, block_keys, preferred_element_type=jnp.float32
                )
                * score_scale
            )
            allowed = key_pos[None, :] <= query_pos[:, None]
            scores = jnp.where(allowed, scores, big_negative)
            new_max = jnp.maximum(row_max, jnp.max(scores, axis=-1))
            attn_weight = jnp.where(allowed, jnp.exp(scores - new_max[..., None]), 0.0)
            factor = jnp.exp(row_max - new_max)
            running_sum = running_sum * factor + jnp.sum(attn_weight, axis=-1)
            accumulated = accumulated * factor[..., None] + jnp.einsum(
                "kgts,skd->kgtd",
                attn_weight.astype(jnp.bfloat16),
                block_values,
                preferred_element_type=jnp.float32,
            )
            result = [new_max, running_sum, accumulated] + list(carry_in[3:])
            in_state = (key_pos < prev_start).astype(jnp.float32)
            features = feature_map(
                jnp.einsum(
                    "skd,kgdf->kgsf", block_keys.astype(jnp.float32), key_map, precision=precise
                )
            )
            features = features * in_state[None, None, :, None]
            result[-2] = carry_in[-2] + jnp.einsum(
                "kgsf,skd->kgfd", features, block_values.astype(jnp.float32), precision=precise
            )
            result[-1] = carry_in[-1] + jnp.sum(features, axis=2)
            return tuple(result)

        return lax.cond(first_row <= last_row, compute, skip_block, running)

    folded = lax.fori_loop(0, piece_rows // step_rows, attend, initial)
    teacher = folded[2] / folded[1][..., None]
    stacked = jnp.stack([keys, values])
    moved = shifted(stacked, "ctx", 1)
    prev_keys, prev_values = (moved[0], moved[1])
    has_prev = (my_block > 0).astype(jnp.float32)
    window_keys = jnp.concatenate([prev_keys, keys], axis=0)
    window_values = jnp.concatenate([prev_values, values], axis=0)
    column = jnp.arange(2 * block_len, dtype=jnp.int32)
    row_index = jnp.arange(block_len, dtype=jnp.int32)
    allowed = (column[None, :] < block_len) & (my_block > 0) | (column[None, :] >= block_len) & (
        column[None, :] - block_len <= row_index[:, None]
    )
    scores = (
        jnp.einsum("tkgd,skd->kgts", grouped_q, window_keys, preferred_element_type=jnp.float32)
        * score_scale
    )
    scores = jnp.where(allowed, scores, big_negative)
    row_max = jnp.max(scores, axis=-1)
    window_weight = jnp.where(allowed, jnp.exp(scores - row_max[..., None]), 0.0)
    window_den = jnp.sum(window_weight, axis=-1)
    window_num = jnp.einsum(
        "kgts,skd->kgtd",
        window_weight.astype(jnp.bfloat16),
        window_values,
        preferred_element_type=jnp.float32,
    )
    key_proj = jnp.einsum(
        "skd,kgdf->kgsf", prev_keys.astype(jnp.float32), key_map, precision=precise
    )
    state, norm = (folded[-2], folded[-1])
    query_proj = jnp.einsum(
        "tkgd,kgdf->kgtf", grouped_q.astype(jnp.float32), query_map, precision=precise
    )
    query_feats = feature_map(query_proj)
    decay = jnp.exp(-row_max)
    far_num = decay[..., None] * jnp.einsum(
        "kgtf,kgfd->kgtd", query_feats, state, precision=precise
    )
    far_den = decay * jnp.einsum("kgtf,kgf->kgt", query_feats, norm, precision=precise)
    denominator = window_den + far_den
    mix = (window_num + far_num) / denominator[..., None]
    student = jnp.transpose(mix.astype(jnp.bfloat16), (2, 0, 1, 3)).reshape(
        block_len, head_count, head_width
    )
    mismatch = mix - teacher
    grad_num = mismatch / denominator[..., None]
    grad_den = -jnp.sum(mismatch * mix, axis=-1) / denominator
    lifted = decay[..., None] * query_feats
    grad_state = jnp.einsum("kgtf,kgtd->kgfd", lifted, grad_num, precision=precise)
    grad_norm = jnp.einsum("kgtf,kgt->kgf", lifted, grad_den, precision=precise)
    grad_qfeat = decay[..., None] * (
        jnp.einsum("kgfd,kgtd->kgtf", state, grad_num, precision=precise)
        + norm[:, :, None, :] * grad_den[..., None]
    )
    later_state, later_norm = carried_in(
        (grad_state, grad_norm),
        "ctx",
        add_pair,
        (jnp.zeros_like(grad_state), jnp.zeros_like(grad_norm)),
    )
    grad_kfeat = (
        jnp.einsum(
            "kgfd,skd->kgsf", later_state, prev_values.astype(jnp.float32), precision=precise
        )
        + later_norm[:, :, None, :]
    ) * has_prev
    grad_query = jnp.einsum(
        "tkgd,kgtf->kgdf",
        grouped_q.astype(jnp.float32),
        feature_pull(query_proj, grad_qfeat),
        precision=precise,
    )
    grad_key = jnp.einsum(
        "skd,kgsf->kgdf",
        prev_keys.astype(jnp.float32),
        feature_pull(key_proj, grad_kfeat),
        precision=precise,
    )
    gradients = jnp.concatenate([grad_query, grad_key], axis=-1).reshape(
        head_count, head_width, 2 * feature_len
    )
    entry_count = gradients.size * lax.axis_size("head")
    summed = lax.psum(gradients, "ctx")
    squares = lax.psum(jnp.sum(summed * summed), "head")
    update = summed / jnp.sqrt(squares / entry_count + 1e-06)
    return (student, update)


f32, bf16 = jnp.float32, jnp.bfloat16
NN = (((1,), (0,)), ((), ()))
NT = (((1,), (1,)), ((), ()))
TN = (((0,), (0,)), ((), ()))


def mxu(a, b, dims):
    return lax.dot_general(a, b, dims, preferred_element_type=f32)


def split(x, pieces):
    out = []
    for _ in range(pieces):
        piece = x.astype(bf16)
        out.append(piece)
        x = x - piece.astype(f32)
    return out


def cat(parts, axis):
    return jnp.concatenate(parts, axis=axis)


def exact_by_wide(a, b, dims):
    return mxu(cat([a, a], dims[0][0][0]), cat(split(b, 2), dims[0][1][0]), dims)


def wide_by_exact(a, b, dims):
    return mxu(cat(split(a, 2), dims[0][0][0]), cat([b, b], dims[0][1][0]), dims)


def wide_by_rounded(a, b, dims):
    return wide_by_exact(a, b.astype(bf16), dims)


def half_sum(x, halves):
    return wide_by_exact(x, halves, NN)


def half_softmax(u, is_upper, halves):
    top = jnp.max(jnp.where(is_upper, u, big_negative), axis=-1, keepdims=True)
    low = jnp.max(jnp.where(is_upper, big_negative, u), axis=-1, keepdims=True)
    e = jnp.exp(u - jnp.where(is_upper, top, low))
    return e / half_sum(e, halves)


def remote(src, dst, send_sem, recv_sem, **where):
    return pltpu.make_async_remote_copy(
        src_ref=src,
        dst_ref=dst,
        send_sem=send_sem,
        recv_sem=recv_sem,
        device_id=where,
        device_id_type=pl.DeviceIdType.MESH,
    )


def each(count, body):
    def step(index, carry):
        body(index)
        return carry

    lax.fori_loop(0, count, step, 0)


def head_kernel(
    q_hbm, k_hbm, v_hbm, w_hbm, student_hbm, grad_hbm, scale_hbm,
    q_raw, k_raw, v_raw, w_ref, qt_ref, kvt_ref, q_all, kv_all, st_all, st_turned, mix_ref,
    own_grad, gat_ref, sq_own, sq_all, sq_ref, scale_ref, own_ref, sum_ref, pre_ref, pre_norm_ref,
    score_ref, near_ref, kfeat_ref, gstate_ref, gnorm_ref, wq_ref, wk_ref, gq_ref,
    q_sem, kv_send, kv_recv, local_sem, st_sem, g_send, g_recv, g_hop, g_final, sq_sem, fetch_sem,
    w_send, w_recv, out_sem, swap_sem,
):
    blocks, length, width = qt_ref.shape
    planes = kvt_ref.shape[0]
    group = blocks // planes
    me, side = lax.axis_index("ctx"), lax.axis_index("head")
    plane, spot = me // group, me % group
    row, column = spot // 2, spot % 2
    native = row == side
    mine = plane * group + 2 * column + side
    features = w_ref.shape[1] // 2
    rows = 2 * length
    steps, pairs = blocks // 2, blocks // 4
    middle = pairs - 1

    def pair_block(p, u):
        return jnp.where(u < 2, 4 * p + u, blocks - 4 - 4 * p + u)

    my_pair = jnp.where(row == 0, plane, planes - 1 - plane)
    barrier = pltpu.get_barrier_semaphore()

    def greet(t, h):
        pl.semaphore_signal(
            barrier, inc=1, device_id={"ctx": t, "head": h}, device_id_type=pl.DeviceIdType.MESH
        )

    def greet_side(d):
        t = (me + d) % blocks

        @pl.when(jnp.logical_not(native & (t == me)))
        def _():
            greet(t, row)

    fetches = [
        pltpu.make_async_copy(src, dst, fetch_sem.at[n])
        for n, (src, dst) in enumerate([(k_hbm, k_raw), (v_hbm, v_raw), (q_hbm, q_raw)])
    ]
    for fetch in fetches:
        fetch.start()
    each(blocks, greet_side)
    each(blocks // 2, lambda n: greet((n // 2) * group + 2 * side + n % 2, 1 - row))
    own_w = pltpu.make_async_copy(w_hbm.at[mine], w_ref, local_sem.at[2])

    @pl.when(native)
    def _():
        own_w.start()

    def flip(index, d):
        bit = 1
        while bit <= d:
            if d & bit:
                index = index + bit - 2 * bit * ((index // bit) % 2)
            bit *= 2
        return index

    def w_copy():
        other = plane * group + 2 * column + 1 - side
        return remote(w_hbm.at[other], w_ref, w_send.at[0], w_recv.at[0], ctx=me, head=1 - side)

    def kv_land(g):
        return remote(
            kvt_ref.at[g], kv_all.at[me], kv_send.at[0], kv_recv.at[plane],
            ctx=g * group + 2 * side + column, head=row,
        )

    def landed_block(z):
        return z * group + 2 * side + column

    def crossed_block(z):
        return z * group + 2 * side + 1 - column

    def kv_across(z):
        block = landed_block(z)
        return remote(
            kv_all.at[block], kv_all.at[block], kv_send.at[1], kv_recv.at[planes + z],
            ctx=plane * group + 2 * row + 1 - column, head=side,
        )

    def kv_share(block, z):
        return remote(
            kv_all.at[block], kv_all.at[block], kv_send.at[2], kv_recv.at[2 * planes + z],
            ctx=me, head=1 - side,
        )

    def q_copy(j):
        return remote(
            qt_ref.at[j], q_all.at[me], q_sem.at[pairs], q_sem.at[my_pair],
            ctx=(j // group) * group + 2 * side + (j % group) // 2, head=j % 2,
        )

    def bulk(ref, send_sem, recv_sem):
        return remote(ref, ref, send_sem, recv_sem, ctx=me, head=1 - side)

    def kv_arrival(first, count, n):
        return bulk(kv_all.at[pl.ds(first, count)], kv_send.at[0], kv_recv.at[n])

    def st_copy(b):
        return remote(mix_ref.at[b], st_all.at[mine], st_sem.at[0], st_sem.at[1], ctx=b, head=row)

    def g_column(part, z):
        return remote(
            own_grad.at[part], gat_ref.at[part, mine], g_send.at[0], g_recv.at[part, 2 * plane + side],
            ctx=z * group + spot, head=row,
        )

    def g_pass(part, z, h, d):
        piece = gat_ref.at[part, z * group + 2 * column + h]
        arrival = g_hop.at[part, z] if (d == 1) == (h == 0) else g_final.at[0]
        return remote(
            piece, piece, g_send.at[d], arrival, ctx=plane * group + flip(spot, d), head=side
        )

    def g_forward(part, z):
        j = z * group + jnp.where(native, 2 - 2 * column, 2 * column + 1)
        piece = gat_ref.at[part, j]
        target = jnp.where(native, flip(spot, 2), flip(spot, 1))
        return remote(
            piece, piece, g_send.at[3], g_final.at[0], ctx=plane * group + target, head=side
        )

    def g_landing(part, j, n):
        return bulk(gat_ref.at[part, j], g_send.at[0], g_recv.at[part, n])

    def sq_copy(t):
        return remote(
            sq_own, sq_all.at[mine], sq_sem.at[0], sq_sem.at[1], ctx=t, head=row
        )

    def unless_own(b, body):
        @pl.when(jnp.logical_not(native & (b == me)))
        def _():
            body()

    rate = math.log2(math.e) / math.sqrt(width)
    lane = lax.broadcasted_iota(jnp.int32, (rows, 2 * features), 1)
    is_upper = lane < features
    row_half = lax.broadcasted_iota(jnp.int32, (2 * features, 2 * features), 0) < features
    col_half = lax.broadcasted_iota(jnp.int32, (2 * features, 2 * features), 1) < features
    halves = jnp.where(row_half == col_half, 1.0, 0.0).astype(bf16)
    square = (rows, rows)
    causal = lax.broadcasted_iota(jnp.int32, square, 1) <= lax.broadcasted_iota(jnp.int32, square, 0)
    for part, (fetch, raw) in enumerate(zip(fetches, (k_raw, v_raw))):
        fetch.wait()
        kvt_ref[:, part] = jnp.transpose(raw[...], (1, 0, 2))
    own_kv = pltpu.make_async_copy(kvt_ref.at[plane], kv_all.at[me], local_sem.at[0])

    @pl.when(native)
    def _():
        own_kv.start()

    pl.semaphore_wait(barrier, jnp.where(native, 3 * blocks // 2 - 1, 3 * blocks // 2))
    for d in range(planes):
        g = flip(plane, d)
        if d == 0:
            @pl.when(jnp.logical_not(native))
            def _():
                kv_land(g).start()
        else:
            kv_land(g).start()

    @pl.when(native)
    def _():
        w_copy().start()

    fetches[2].wait()
    qt_ref[...] = jnp.transpose(q_raw[...], (1, 0, 2))
    own_q = pltpu.make_async_copy(qt_ref.at[mine], q_all.at[me], local_sem.at[1])

    @pl.when(native)
    def _():
        own_q.start()
        own_kv.wait()

    def land(d):
        z = flip(plane, d)
        block = landed_block(z)
        unless_own(block, lambda: kv_arrival(block, 1, z).wait_recv())
        kv_across(z).start()
        kv_share(block, z).start()

    def cross(d):
        z = flip(plane, d)
        block = crossed_block(z)
        kv_arrival(block, 1, planes + z).wait_recv()
        kv_share(block, z).start()

    def load(part, i):
        if part == 0:
            return q_all[pl.ds(2 * i, 2)].reshape(rows, width)
        return kv_all[pl.ds(2 * i, 2), part - 1].reshape(rows, width)

    def either(less, body):
        for flag, count in ((native, less), (jnp.logical_not(native), 0)):
            @pl.when(flag)
            def _():
                body(count)

    def q_arrived(p):
        here = native & (p == my_pair)
        for flag, count in ((here, 3), (jnp.logical_not(here), 4)):
            @pl.when(flag)
            def _():
                bulk(q_all.at[pl.ds(0, count)], q_sem.at[pairs], q_sem.at[p]).wait_recv()

    def send_student(b):
        unless_own(b, lambda: st_copy(b).start())

        @pl.when(native & (b == me))
        def _():
            st_all[mine] = mix_ref[me]

    def send_grad(part):
        for d in range(planes):
            z = flip(plane, d)
            if d == 0:
                @pl.when(native)
                def _():
                    gat_ref[part, mine] = own_grad[part]

                @pl.when(jnp.logical_not(native))
                def _():
                    g_column(part, z).start()
            else:
                g_column(part, z).start()

    def relay_grad(part):
        @pl.when(native)
        def _():
            for z in range(planes):
                for h in range(2):
                    j = flip(plane, z) * group + 2 * column + h

                    @pl.when(j != mine)
                    def _():
                        g_landing(part, j, 2 * flip(plane, z) + h).wait_recv()

                    for d in range(1, group - 1):
                        g_pass(part, flip(plane, z), h, d).start()

    def hop_grad(part):
        for d in range(planes):
            z = flip(plane, d)
            bulk(gat_ref.at[part, z], g_send.at[0], g_hop.at[part, z]).wait_recv()
            g_forward(part, z).start()

    def key_side(pair):
        kv_arrival(group * pair, 2, 2 * planes + pair).wait_recv()
        steps_of = (2 * pair, 2 * pair + 1)
        ks, vs = ([load(part, i) for i in steps_of] for part in (1, 2))
        kfs = [
            half_softmax(mxu(cat([k, k, k], 1), wk_ref[...], NN), is_upper, halves) for k in ks
        ]
        for i, kf, v in zip(steps_of, kfs, vs):
            kfeat_ref[i] = kf
            for h in range(2):
                part = kf[h * length:(h + 1) * length]
                own_ref[2 * i + h] = wide_by_exact(part, v[h * length:(h + 1) * length], TN)
                sum_ref[2 * i + h] = jnp.sum(part, axis=0, keepdims=True)

    def push(n):
        p = (my_pair + pairs - n // group) % pairs
        j = jnp.where(side == 0, p, planes - 1 - p) * group + n % group

        @pl.when(jnp.logical_not(native & (j == mine)))
        def _():
            q_copy(j).start()

    def plane_keys(z):
        each(group // 4, lambda u: key_side(z * (group // 4) + u))

    def push_turns(first, last):
        each((last - first) * group, lambda n: push(first * group + n))

    land(0)
    @pl.when(native)
    def _():
        own_w.wait()

    @pl.when(jnp.logical_not(native))
    def _():
        w_copy().wait_recv()

    w = w_ref[...]
    wq, wk = w[:, :features], w[:, features:]
    wq_ref[...] = cat(split(cat([wq, -wq], 1), 3), 0)
    wk_ref[...] = cat(split(cat([wk, -wk], 1), 3), 0)
    gq_ref[...] = jnp.zeros_like(gq_ref)
    land(1)
    push_turns(0, 1)
    cross(0)
    land(2)
    cross(1)
    land(3)
    push_turns(1, 2)
    plane_keys(flip(plane, 0))
    cross(2)
    plane_keys(flip(plane, 1))
    cross(3)
    push_turns(2, pairs)
    plane_keys(flip(plane, 2))
    plane_keys(flip(plane, 3))

    @pl.when(native)
    def _():
        own_q.wait()

    for b in range(2):
        pre_ref[b] = jnp.zeros_like(pre_ref[b])
        pre_norm_ref[b] = jnp.zeros_like(pre_norm_ref[b])

    def prefix(b):
        pre_ref[b + 2] = pre_ref[b + 1] + own_ref[b]
        pre_norm_ref[b + 2] = pre_norm_ref[b + 1] + sum_ref[b]

    each(blocks - 2, prefix)

    def forward(turn, carry):
        p = (my_pair + turn) % pairs
        a, b = 2 * p, steps - 1 - 2 * p
        q_arrived(p)
        tokens = (a, b)
        qs = [load(0, i) for i in tokens]
        vs = [load(2, i) for i in tokens]
        wide_b = b // 2

        def pair_of(part, j):
            return cat([load(part, 2 * j), load(part, 2 * j + 1)], 0)

        def fold(x, combine):
            while x.shape[1] > length:
                half = x.shape[1] // 2
                x = combine(x[:, :half], x[:, half:])
            return x

        s = mxu(qs[0], load(1, a), NT) * rate
        s_a = jnp.where(causal, s, big_negative)
        near_ref[0] = s_a
        s = mxu(qs[1], pair_of(1, wide_b), NT) * rate
        s_b = [s[:, :rows], jnp.where(causal, s[:, rows:], big_negative)]
        near_ref[1], near_ref[2] = s_b
        peaks = [fold(s_a, jnp.maximum), fold(jnp.maximum(*s_b), jnp.maximum)]

        def far_tile(m):
            first = m < p
            return first, jnp.where(first, a, b), jnp.where(first, m, m - p)

        for m in range(middle):
            first, i, j = far_tile(m)
            s = mxu(load(0, i), pair_of(1, j), NT) * rate
            score_ref[m] = s
            top = fold(s, jnp.maximum)
            peaks = [
                jnp.maximum(peaks[0], jnp.where(first, top, big_negative)),
                jnp.maximum(peaks[1], jnp.where(first, big_negative, top)),
            ]
        tops = [jnp.max(x, axis=-1, keepdims=True) for x in peaks]

        weight = jnp.exp2(near_ref[0] - tops[0])
        sums = [fold(weight, jnp.add)]
        accs = [mxu(weight.astype(bf16), vs[0], NN)]
        weight = jnp.exp2(cat([near_ref[1], near_ref[2]], 1) - tops[1])
        sums.append(fold(weight, jnp.add))
        accs.append(mxu(weight.astype(bf16), pair_of(2, wide_b), NN))
        for m in range(middle):
            first, i, j = far_tile(m)
            weight = jnp.exp2(score_ref[m] - jnp.where(first, tops[0], tops[1]))
            part = fold(weight, jnp.add)
            prod = mxu(weight.astype(bf16), pair_of(2, j), NN)
            sums = [sums[0] + jnp.where(first, part, 0.0), sums[1] + jnp.where(first, 0.0, part)]
            accs = [accs[0] + jnp.where(first, prod, 0.0), accs[1] + jnp.where(first, 0.0, prod)]
        teachers = [
            acc / jnp.sum(total, axis=-1, keepdims=True) for acc, total in zip(accs, sums)
        ]

        def halves_of(f):
            return [cat([f(x, 0), f(x, 1)], 0) for x in range(2)]

        def cut(x, half):
            return x[half * length:(half + 1) * length]

        last_far = score_ref[jnp.maximum(p - 1, 0), :length, 3 * length:]
        prevs = [
            cat([jnp.where(p > 0, last_far, big_negative), near_ref[0, length:, :length]], 0),
            cat([near_ref[1, :length, length:], near_ref[2, length:, :length]], 0),
        ]
        owns = [
            cat([near_ref[k, :length, :length], near_ref[k, length:, length:]], 0) for k in (0, 2)
        ]
        win_maxs = [
            jnp.max(jnp.maximum(prev, own), axis=-1, keepdims=True)
            for prev, own in zip(prevs, owns)
        ]
        p_prevs = [jnp.exp2(x - top) for x, top in zip(prevs, win_maxs)]
        p_owns = [jnp.exp2(x - top) for x, top in zip(owns, win_maxs)]
        win_dens = [jnp.sum(x + y, axis=-1, keepdims=True) for x, y in zip(p_prevs, p_owns)]
        p_wins = [cat([x.astype(bf16), y.astype(bf16)], 1) for x, y in zip(p_prevs, p_owns)]
        v_befores = [kv_all[jnp.maximum(2 * i - 1, 0), 1] for i in tokens]
        v_wins = [
            (cat([before, v[:length]], 0), v) for before, v in zip(v_befores, vs)
        ]
        win_nums = halves_of(lambda x, h: mxu(cut(p_wins[x], h), v_wins[x][h], NN))

        qfs = [
            half_softmax(mxu(cat([q, q, q], 1), wq_ref[...], NN), is_upper, halves) for q in qs
        ]
        states = [[pre_ref[2 * i], pre_ref[2 * i + 1]] for i in tokens]
        norms = [
            cat(
                [
                    jnp.broadcast_to(pre_norm_ref[2 * i + h], (length, 2 * features))
                    for h in range(2)
                ],
                0,
            )
            for i in tokens
        ]
        decays = [jnp.exp2(-top) for top in win_maxs]
        fars = halves_of(lambda x, h: wide_by_rounded(cut(qfs[x], h), states[x][h], NN))
        dens = [
            win_den + decay * jnp.sum(qf * norm, axis=-1, keepdims=True)
            for win_den, decay, qf, norm in zip(win_dens, decays, qfs, norms)
        ]
        mixes = [
            (num + decay * far) / den
            for num, decay, far, den in zip(win_nums, decays, fars, dens)
        ]
        for i, mix in zip(tokens, mixes):
            mix_ref[pl.ds(2 * i, 2)] = mix.astype(bf16).reshape(2, length, width)
        @pl.when(turn < pairs - 1)
        def _():
            each(4, lambda u: send_student(pair_block(p, u)))

        mismatches = [mix - teacher for mix, teacher in zip(mixes, teachers)]
        g_nums = [x / den for x, den in zip(mismatches, dens)]
        g_dens = [
            -jnp.sum(x * mix, axis=-1, keepdims=True) / den
            for x, mix, den in zip(mismatches, mixes, dens)
        ]
        lifts = [decay * qf for decay, qf in zip(decays, qfs)]
        pulled_norms = [lift * g_den for lift, g_den in zip(lifts, g_dens)]
        for x, i in enumerate(tokens):
            for h in range(2):
                gstate_ref[2 * i + h] = wide_by_rounded(cut(lifts[x], h), cut(g_nums[x], h), TN)
                gnorm_ref[2 * i + h] = jnp.sum(cut(pulled_norms[x], h), axis=0, keepdims=True)
        pulled = halves_of(lambda x, h: wide_by_rounded(cut(g_nums[x], h), states[x][h], NT))
        g_qfs = [
            decay * (pull + norm * g_den)
            for decay, pull, norm, g_den in zip(decays, pulled, norms, g_dens)
        ]
        d_qs = [qf * (g - half_sum(qf * g, halves)) for qf, g in zip(qfs, g_qfs)]
        gq_ref[...] += wide_by_exact(d_qs[0], qs[0], TN) + wide_by_exact(d_qs[1], qs[1], TN)
        return carry

    lax.fori_loop(0, pairs, forward, 0)
    own_grad[0] = (gq_ref[:features] - gq_ref[features:]).astype(bf16)
    send_grad(0)

    for b in range(blocks - 2, 1, -1):
        gstate_ref[b] = gstate_ref[b] + gstate_ref[b + 1]
        gnorm_ref[b] = gnorm_ref[b] + gnorm_ref[b + 1]

    def backward(group_of):
        ks, vs, kfs = ([f(i) for i in group_of] for f in (lambda i: load(1, i), lambda i: load(2, i), lambda i: kfeat_ref[i]))
        g_kfs = [
            cat(
                [
                    mxu(v[h * length:(h + 1) * length], gstate_ref[2 * i + h + 2].astype(bf16), NT)
                    + gnorm_ref[2 * i + h + 2]
                    for h in range(2)
                ],
                0,
            )
            for i, v in zip(group_of, vs)
        ]
        d_ks = [kf * (g - half_sum(kf * g, halves)) for kf, g in zip(kfs, g_kfs)]
        return [wide_by_exact(d_k, k, TN) for d_k, k in zip(d_ks, ks)]

    gk = sum(backward(range(steps // 2)) + backward(range(steps // 2, steps - 1)))
    own_grad[1] = (gk[:features] - gk[features:]).astype(bf16)
    send_grad(1)
    square = own_grad[...].astype(f32).reshape(2 * features, width)
    sq_own[...] = jnp.sum(square * square, axis=0, keepdims=True)
    each(blocks, lambda n: unless_own((me + n) % blocks, lambda: sq_copy((me + n) % blocks).start()))

    @pl.when(native)
    def _():
        sq_all[mine] = sq_own[...]

    each(4, lambda u: send_student(pair_block((my_pair + pairs - 1) % pairs, u)))
    relay_grad(0)
    relay_grad(1)
    hop_grad(0)
    hop_grad(1)

    either(1, lambda n: bulk(st_all.at[pl.ds(0, blocks - n)], st_sem.at[0], st_sem.at[1]).wait_recv())
    st_turned[...] = jnp.transpose(st_all[...], (1, 0, 2))
    student_out = pltpu.make_async_copy(st_turned, student_hbm, out_sem.at[0])
    student_out.start()

    either(1, lambda n: bulk(sq_all.at[pl.ds(0, blocks - n)], sq_sem.at[0], sq_sem.at[1]).wait_recv())
    sq_ref[0] = jnp.sum(sq_all[...], axis=0)
    swap = remote(
        sq_ref.at[0], sq_ref.at[1], swap_sem.at[0], swap_sem.at[1], ctx=me, head=1 - side
    )
    swap.start()

    either(1, lambda n: bulk(qt_ref.at[pl.ds(0, blocks - n)], q_sem.at[pairs], q_sem.at[0]).wait_send())
    either(1, lambda n: bulk(mix_ref.at[pl.ds(0, blocks - n)], st_sem.at[0], st_sem.at[1]).wait_send())
    either(1, lambda n: bulk(sq_all.at[pl.ds(0, blocks - n)], sq_sem.at[0], sq_sem.at[1]).wait_send())
    either(1, lambda n: bulk(kvt_ref.at[pl.ds(0, planes - n)], kv_send.at[0], kv_recv.at[0]).wait_send())
    bulk(kv_all.at[pl.ds(0, planes)], kv_send.at[1], kv_recv.at[0]).wait_send()
    bulk(kv_all.at[pl.ds(0, 2 * planes)], kv_send.at[2], kv_recv.at[0]).wait_send()
    either(2, lambda n: bulk(gat_ref.at[0, pl.ds(0, 2 * planes - n)], g_send.at[0], g_final.at[0]).wait_send())

    @pl.when(native)
    def _():
        w_copy().wait_send()

    swap.wait()
    entries = 2 * blocks * width * 2 * features
    total = jnp.sum(sq_ref[0] + sq_ref[1], keepdims=True)
    scale_ref[...] = jnp.broadcast_to(1.0 / jnp.sqrt(total / entries + 1e-06), (8, width))
    scale_out = pltpu.make_async_copy(scale_ref, scale_hbm, out_sem.at[2])
    scale_out.start()

    @pl.when(native)
    def _():
        bulk(gat_ref.at[0, pl.ds(0, 2 * planes)], g_send.at[0], g_final.at[0]).wait_recv()

    @pl.when(jnp.logical_not(native))
    def _():
        bulk(gat_ref.at[:, pl.ds(0, 3 * planes)], g_send.at[0], g_final.at[0]).wait_recv()

    grad_out = pltpu.make_async_copy(gat_ref, grad_hbm, out_sem.at[1])
    grad_out.start()

    @pl.when(native)
    def _():
        for d in range(1, group - 1):
            bulk(gat_ref.at[0], g_send.at[d], g_final.at[0]).wait_send()

    bulk(gat_ref.at[0, pl.ds(0, 2 * planes)], g_send.at[3], g_final.at[0]).wait_send()
    student_out.wait()
    scale_out.wait()
    grad_out.wait()


def finish_kernel(
    student_hbm, grad_hbm, scale_hbm, student_out, update_out,
    st_ref, grad_ref, scale_ref, update_ref, in_sem, out_sem,
):
    parts, blocks, features, width = grad_ref.shape
    chunks = in_sem.shape[0] - 2
    each_len = blocks // chunks
    fetches = [
        pltpu.make_async_copy(
            grad_hbm.at[:, pl.ds(n * each_len, each_len)],
            grad_ref.at[:, pl.ds(n * each_len, each_len)], in_sem.at[n],
        )
        for n in range(chunks)
    ]
    scale_in = pltpu.make_async_copy(scale_hbm, scale_ref, in_sem.at[chunks])
    student_in = pltpu.make_async_copy(student_hbm, st_ref, in_sem.at[chunks + 1])
    scale_in.start()
    student_in.start()
    for fetch in fetches:
        fetch.start()
    scale_in.wait()
    scale = scale_ref[:1]
    stores = [pltpu.make_async_copy(st_ref, student_out, out_sem.at[chunks])]
    student_in.wait()
    stores[0].start()
    for n, fetch in enumerate(fetches):
        fetch.wait()
        for j in range(n * each_len, (n + 1) * each_len):
            piece = cat([grad_ref[0, j], grad_ref[1, j]], 0).astype(f32)
            update_ref[j] = piece.T * scale
        stores.append(
            pltpu.make_async_copy(
                update_ref.at[pl.ds(n * each_len, each_len)],
                update_out.at[pl.ds(n * each_len, each_len)], out_sem.at[n],
            )
        )
        stores[-1].start()
    for store in stores:
        store.wait()


def whole_head(queries, keys, values, w):
    length, blocks, width = queries.shape
    planes = keys.shape[1]
    group = blocks // planes
    double = w.shape[2]
    half = double // 2
    rows, steps = 2 * length, blocks // 2
    vmem, dma = pltpu.VMEM, pltpu.SemaphoreType.DMA
    hbm = pl.BlockSpec(memory_space=pltpu.MemorySpace.HBM)
    limit = 67_043_328
    student, grads, scale = pl.pallas_call(
        head_kernel,
        out_shape=(
            jax.ShapeDtypeStruct((length, blocks, width), bf16),
            jax.ShapeDtypeStruct((2, blocks, half, width), bf16),
            jax.ShapeDtypeStruct((8, width), f32),
        ),
        in_specs=[hbm] * 4,
        out_specs=(hbm,) * 3,
        scratch_shapes=[
            vmem((length, blocks, width), bf16),
            vmem((length, planes, width), bf16),
            vmem((length, planes, width), bf16),
            vmem((width, double), f32),
            vmem((blocks, length, width), bf16),
            vmem((planes, 2, length, width), bf16),
            vmem((blocks, length, width), bf16),
            vmem((blocks, 2, length, width), bf16),
            vmem((blocks, length, width), bf16),
            vmem((length, blocks, width), bf16),
            vmem((blocks, length, width), bf16),
            vmem((2, half, width), bf16),
            vmem((2, blocks, half, width), bf16),
            vmem((1, width), f32),
            vmem((blocks, 1, width), f32),
            vmem((2, 1, width), f32),
            vmem((8, width), f32),
            vmem((blocks, double, width), f32),
            vmem((blocks, 1, double), f32),
            vmem((blocks, double, width), f32),
            vmem((blocks, 1, double), f32),
            vmem((blocks // 4 - 1, rows, 2 * rows), f32),
            vmem((3, rows, rows), f32),
            vmem((steps, rows, double), f32),
            vmem((blocks, double, width), f32),
            vmem((blocks, 1, double), f32),
            vmem((3 * width, double), bf16),
            vmem((3 * width, double), bf16),
            vmem((double, width), f32),
            dma((blocks // 4 + 1,)),
            dma((3,)),
            dma((3 * planes,)),
            dma((3,)),
            dma((2,)),
            dma((group,)),
            dma((2, 2 * planes)),
            dma((2, planes)),
            dma((1,)),
            dma((2,)),
            dma((3,)),
            dma((1,)),
            dma((1,)),
            dma((3,)),
            dma((2,)),
        ],
        compiler_params=pltpu.CompilerParams(
            vmem_limit_bytes=limit, collective_id=0, has_side_effects=True
        ),
    )(queries, keys, values, w)
    chunks = 2
    return pl.pallas_call(
        finish_kernel,
        out_shape=(
            jax.ShapeDtypeStruct((length, blocks, width), bf16),
            jax.ShapeDtypeStruct((blocks, width, double), f32),
        ),
        in_specs=[hbm] * 3,
        out_specs=(hbm,) * 2,
        scratch_shapes=[
            vmem((length, blocks, width), bf16),
            vmem((2, blocks, half, width), bf16),
            vmem((8, width), f32),
            vmem((blocks, width, double), f32),
            dma((chunks + 2,)),
            dma((chunks + 1,)),
        ],
        compiler_params=pltpu.CompilerParams(vmem_limit_bytes=limit),
    )(student, grads, scale)


def head_shards(queries, keys, values, feature_weight):
    return whole_head(queries, keys, values, feature_weight)


def shards(queries, keys, values, feature_weight):
    count = lax.axis_size("ctx")
    width = queries.shape[2]
    fits = queries.shape[1] == count and count == 4 * keys.shape[1] and lax.axis_size("head") == 2 and count % 4 == 0 and keys.shape[1] == 4 and count * queries.shape[0] <= 4096
    fits = fits and queries.shape[1] // keys.shape[1] % 4 == 0 and queries.shape[0] == width and feature_weight.shape[2] == width
    body = head_shards if fits else general_shards
    return body(queries, keys, values, feature_weight)


def solution(mesh):
    return jax.shard_map(
        shards,
        mesh=mesh,
        in_specs=(
            P("ctx", "head", None),
            P("ctx", "head", None),
            P("ctx", "head", None),
            P("head", None, None),
        ),
        out_specs=(P("ctx", "head", None), P("head", None, None)),
        check_vma=False,
    )
```

```python
import functools
import math

import jax
import jax.numpy as jnp
from jax import lax
from jax.experimental import pallas as pl
from jax.experimental.pallas import tpu as pltpu
from jax.sharding import PartitionSpec as P

precise = lax.Precision.HIGHEST
big_negative = -1e30


def shifted(shard, axis, by):
    devices = lax.axis_size(axis)
    pairs = [(i, i + by) for i in range(devices) if 0 <= i + by < devices]
    return lax.ppermute(shard, axis, pairs)


def carried_in(part, axis, combine, identity):
    count = lax.axis_size(axis)
    place = lax.axis_index(axis)
    ahead = count - 1 - place
    gathered = jax.tree.map(lambda a: lax.all_gather(a, axis), part)
    state = jax.tree.map(lambda a, e: jnp.zeros_like(a) + jnp.asarray(e, a.dtype), part, identity)

    def one(step, state):
        source = count - 1 - step
        return combine(
            state, jax.tree.map(lambda a: lax.dynamic_index_in_dim(a, source, 0, False), gathered)
        )

    return lax.fori_loop(0, ahead, one, state)


def feature_map(projection):
    return jnp.concatenate(
        [jax.nn.softmax(projection, axis=-1), jax.nn.softmax(-projection, axis=-1)], axis=-1
    )


def feature_pull(projection, upstream):
    half_len = upstream.shape[-1] // 2
    upper = jax.nn.softmax(projection, axis=-1)
    lower = jax.nn.softmax(-projection, axis=-1)
    grad_upper = upstream[..., :half_len]
    grad_lower = upstream[..., half_len:]
    upper_part = upper * (grad_upper - jnp.sum(upper * grad_upper, axis=-1, keepdims=True))
    lower_part = lower * (grad_lower - jnp.sum(lower * grad_lower, axis=-1, keepdims=True))
    return upper_part - lower_part


def add_pair(earlier, later):
    return (earlier[0] + later[0], earlier[1] + later[1])


def skip_block(carry_in):
    return carry_in


def general_shards(queries, keys, values, feature_weight):
    block_len, head_count, head_width = queries.shape
    kv_count = keys.shape[1]
    group_size = head_count // kv_count
    feature_len = feature_weight.shape[2] // 2
    my_block = lax.axis_index("ctx")
    score_scale = 1.0 / math.sqrt(head_width)
    grouped_q = queries.reshape(block_len, kv_count, group_size, head_width)
    maps_weight = feature_weight.reshape(kv_count, group_size, head_width, 2 * feature_len)
    query_map = maps_weight[..., :feature_len]
    key_map = maps_weight[..., feature_len:]
    query_pos = my_block * block_len + jnp.arange(block_len, dtype=jnp.int32)
    prev_start = (my_block - 1) * block_len
    last_row = my_block * block_len + block_len - 1
    initial = [
        jnp.full((kv_count, group_size, block_len), big_negative, jnp.float32),
        jnp.zeros((kv_count, group_size, block_len), jnp.float32),
        jnp.zeros((kv_count, group_size, block_len, head_width), jnp.float32),
    ]
    initial = initial + [
        jnp.zeros((kv_count, group_size, 2 * feature_len, head_width), jnp.float32),
        jnp.zeros((kv_count, group_size, 2 * feature_len), jnp.float32),
    ]
    initial = tuple(initial)
    piece_keys = lax.all_gather(keys, "ctx", axis=0, tiled=True)
    piece_values = lax.all_gather(values, "ctx", axis=0, tiled=True)
    piece_rows = piece_keys.shape[0]
    step_rows = math.gcd(piece_rows, 512)

    def attend(step_index, running):
        first_row = step_index * step_rows
        block_keys = lax.dynamic_slice_in_dim(piece_keys, step_index * step_rows, step_rows, 0)
        block_values = lax.dynamic_slice_in_dim(piece_values, step_index * step_rows, step_rows, 0)
        key_pos = first_row + jnp.arange(step_rows, dtype=jnp.int32)

        def compute(carry_in):
            row_max, running_sum, accumulated = (carry_in[0], carry_in[1], carry_in[2])
            scores = (
                jnp.einsum(
                    "tkgd,skd->kgts", grouped_q, block_keys, preferred_element_type=jnp.float32
                )
                * score_scale
            )
            allowed = key_pos[None, :] <= query_pos[:, None]
            scores = jnp.where(allowed, scores, big_negative)
            new_max = jnp.maximum(row_max, jnp.max(scores, axis=-1))
            attn_weight = jnp.where(allowed, jnp.exp(scores - new_max[..., None]), 0.0)
            factor = jnp.exp(row_max - new_max)
            running_sum = running_sum * factor + jnp.sum(attn_weight, axis=-1)
            accumulated = accumulated * factor[..., None] + jnp.einsum(
                "kgts,skd->kgtd",
                attn_weight.astype(jnp.bfloat16),
                block_values,
                preferred_element_type=jnp.float32,
            )
            result = [new_max, running_sum, accumulated] + list(carry_in[3:])
            in_state = (key_pos < prev_start).astype(jnp.float32)
            features = feature_map(
                jnp.einsum(
                    "skd,kgdf->kgsf", block_keys.astype(jnp.float32), key_map, precision=precise
                )
            )
            features = features * in_state[None, None, :, None]
            result[-2] = carry_in[-2] + jnp.einsum(
                "kgsf,skd->kgfd", features, block_values.astype(jnp.float32), precision=precise
            )
            result[-1] = carry_in[-1] + jnp.sum(features, axis=2)
            return tuple(result)

        return lax.cond(first_row <= last_row, compute, skip_block, running)

    folded = lax.fori_loop(0, piece_rows // step_rows, attend, initial)
    teacher = folded[2] / folded[1][..., None]
    stacked = jnp.stack([keys, values])
    moved = shifted(stacked, "ctx", 1)
    prev_keys, prev_values = (moved[0], moved[1])
    has_prev = (my_block > 0).astype(jnp.float32)
    window_keys = jnp.concatenate([prev_keys, keys], axis=0)
    window_values = jnp.concatenate([prev_values, values], axis=0)
    column = jnp.arange(2 * block_len, dtype=jnp.int32)
    row_index = jnp.arange(block_len, dtype=jnp.int32)
    allowed = (column[None, :] < block_len) & (my_block > 0) | (column[None, :] >= block_len) & (
        column[None, :] - block_len <= row_index[:, None]
    )
    scores = (
        jnp.einsum("tkgd,skd->kgts", grouped_q, window_keys, preferred_element_type=jnp.float32)
        * score_scale
    )
    scores = jnp.where(allowed, scores, big_negative)
    row_max = jnp.max(scores, axis=-1)
    window_weight = jnp.where(allowed, jnp.exp(scores - row_max[..., None]), 0.0)
    window_den = jnp.sum(window_weight, axis=-1)
    window_num = jnp.einsum(
        "kgts,skd->kgtd",
        window_weight.astype(jnp.bfloat16),
        window_values,
        preferred_element_type=jnp.float32,
    )
    key_proj = jnp.einsum(
        "skd,kgdf->kgsf", prev_keys.astype(jnp.float32), key_map, precision=precise
    )
    state, norm = (folded[-2], folded[-1])
    query_proj = jnp.einsum(
        "tkgd,kgdf->kgtf", grouped_q.astype(jnp.float32), query_map, precision=precise
    )
    query_feats = feature_map(query_proj)
    decay = jnp.exp(-row_max)
    far_num = decay[..., None] * jnp.einsum(
        "kgtf,kgfd->kgtd", query_feats, state, precision=precise
    )
    far_den = decay * jnp.einsum("kgtf,kgf->kgt", query_feats, norm, precision=precise)
    denominator = window_den + far_den
    mix = (window_num + far_num) / denominator[..., None]
    student = jnp.transpose(mix.astype(jnp.bfloat16), (2, 0, 1, 3)).reshape(
        block_len, head_count, head_width
    )
    mismatch = mix - teacher
    grad_num = mismatch / denominator[..., None]
    grad_den = -jnp.sum(mismatch * mix, axis=-1) / denominator
    lifted = decay[..., None] * query_feats
    grad_state = jnp.einsum("kgtf,kgtd->kgfd", lifted, grad_num, precision=precise)
    grad_norm = jnp.einsum("kgtf,kgt->kgf", lifted, grad_den, precision=precise)
    grad_qfeat = decay[..., None] * (
        jnp.einsum("kgfd,kgtd->kgtf", state, grad_num, precision=precise)
        + norm[:, :, None, :] * grad_den[..., None]
    )
    later_state, later_norm = carried_in(
        (grad_state, grad_norm),
        "ctx",
        add_pair,
        (jnp.zeros_like(grad_state), jnp.zeros_like(grad_norm)),
    )
    grad_kfeat = (
        jnp.einsum(
            "kgfd,skd->kgsf", later_state, prev_values.astype(jnp.float32), precision=precise
        )
        + later_norm[:, :, None, :]
    ) * has_prev
    grad_query = jnp.einsum(
        "tkgd,kgtf->kgdf",
        grouped_q.astype(jnp.float32),
        feature_pull(query_proj, grad_qfeat),
        precision=precise,
    )
    grad_key = jnp.einsum(
        "skd,kgsf->kgdf",
        prev_keys.astype(jnp.float32),
        feature_pull(key_proj, grad_kfeat),
        precision=precise,
    )
    gradients = jnp.concatenate([grad_query, grad_key], axis=-1).reshape(
        head_count, head_width, 2 * feature_len
    )
    entry_count = gradients.size * lax.axis_size("head")
    summed = lax.psum(gradients, "ctx")
    squares = lax.psum(jnp.sum(summed * summed), "head")
    update = summed / jnp.sqrt(squares / entry_count + 1e-06)
    return (student, update)


f32, bf16 = jnp.float32, jnp.bfloat16
NN = (((1,), (0,)), ((), ()))
NT = (((1,), (1,)), ((), ()))
TN = (((0,), (0,)), ((), ()))


def mxu(a, b, dims):
    return lax.dot_general(a, b, dims, preferred_element_type=f32)


def split(x, pieces):
    out = []
    for _ in range(pieces):
        piece = x.astype(bf16)
        out.append(piece)
        x = x - piece.astype(f32)
    return out


def cat(parts, axis):
    return jnp.concatenate(parts, axis=axis)


def exact_by_wide(a, b, dims):
    return mxu(cat([a, a], dims[0][0][0]), cat(split(b, 2), dims[0][1][0]), dims)


def wide_by_exact(a, b, dims):
    return mxu(cat(split(a, 2), dims[0][0][0]), cat([b, b], dims[0][1][0]), dims)


def wide_by_rounded(a, b, dims):
    return wide_by_exact(a, b.astype(bf16), dims)


def half_sum(x, halves):
    return wide_by_exact(x, halves, NN)


def half_softmax(u, is_upper, halves):
    top = jnp.max(jnp.where(is_upper, u, big_negative), axis=-1, keepdims=True)
    low = jnp.max(jnp.where(is_upper, big_negative, u), axis=-1, keepdims=True)
    e = jnp.exp(u - jnp.where(is_upper, top, low))
    return e / half_sum(e, halves)


def remote(src, dst, send_sem, recv_sem, **where):
    return pltpu.make_async_remote_copy(
        src_ref=src,
        dst_ref=dst,
        send_sem=send_sem,
        recv_sem=recv_sem,
        device_id=where,
        device_id_type=pl.DeviceIdType.MESH,
    )


def each(count, body):
    def step(index, carry):
        body(index)
        return carry

    lax.fori_loop(0, count, step, 0)


def head_kernel(
    q_hbm, k_hbm, v_hbm, w_hbm, student_hbm, grad_hbm, scale_hbm,
    q_raw, k_raw, v_raw, w_ref, qt_ref, kvt_ref, q_all, kv_all, st_all, st_turned, mix_ref,
    own_grad, gat_ref, sq_own, sq_all, sq_ref, scale_ref, own_ref, sum_ref, pre_ref, pre_norm_ref,
    score_ref, near_ref, kfeat_ref, gstate_ref, gnorm_ref, wq_ref, wk_ref, gq_ref,
    q_sem, kv_send, kv_recv, local_sem, st_sem, g_send, g_recv, g_hop, g_final, sq_sem, fetch_sem,
    w_send, w_recv, out_sem, swap_sem,
):
    blocks, length, width = qt_ref.shape
    planes = kvt_ref.shape[0]
    group = blocks // planes
    me, side = lax.axis_index("ctx"), lax.axis_index("head")
    plane, spot = me // group, me % group
    row, column = spot // 2, spot % 2
    native = row == side
    mine = plane * group + 2 * column + side
    features = w_ref.shape[1] // 2
    rows = 2 * length
    steps, pairs = blocks // 2, blocks // 4
    middle = pairs - 1

    def pair_block(p, u):
        return jnp.where(u < 2, 4 * p + u, blocks - 4 - 4 * p + u)

    my_pair = jnp.where(row == 0, plane, planes - 1 - plane)
    barrier = pltpu.get_barrier_semaphore()

    def greet(t, h):
        pl.semaphore_signal(
            barrier, inc=1, device_id={"ctx": t, "head": h}, device_id_type=pl.DeviceIdType.MESH
        )

    def greet_side(d):
        t = (me + d) % blocks

        @pl.when(jnp.logical_not(native & (t == me)))
        def _():
            greet(t, row)

    fetches = [
        pltpu.make_async_copy(src, dst, fetch_sem.at[n])
        for n, (src, dst) in enumerate([(k_hbm, k_raw), (v_hbm, v_raw), (q_hbm, q_raw)])
    ]
    for fetch in fetches:
        fetch.start()
    each(blocks, greet_side)
    each(blocks // 2, lambda n: greet((n // 2) * group + 2 * side + n % 2, 1 - row))
    own_w = pltpu.make_async_copy(w_hbm.at[mine], w_ref, local_sem.at[2])

    @pl.when(native)
    def _():
        own_w.start()

    def flip(index, d):
        bit = 1
        while bit <= d:
            if d & bit:
                index = index + bit - 2 * bit * ((index // bit) % 2)
            bit *= 2
        return index

    def w_copy():
        other = plane * group + 2 * column + 1 - side
        return remote(w_hbm.at[other], w_ref, w_send.at[0], w_recv.at[0], ctx=me, head=1 - side)

    def kv_land(g):
        return remote(
            kvt_ref.at[g], kv_all.at[me], kv_send.at[0], kv_recv.at[plane],
            ctx=g * group + 2 * side + column, head=row,
        )

    def landed_block(z):
        return z * group + 2 * side + column

    def crossed_block(z):
        return z * group + 2 * side + 1 - column

    def kv_across(z):
        block = landed_block(z)
        return remote(
            kv_all.at[block], kv_all.at[block], kv_send.at[1], kv_recv.at[planes + z],
            ctx=plane * group + 2 * row + 1 - column, head=side,
        )

    def kv_share(block, z):
        return remote(
            kv_all.at[block], kv_all.at[block], kv_send.at[2], kv_recv.at[2 * planes + z],
            ctx=me, head=1 - side,
        )

    def q_copy(j):
        return remote(
            qt_ref.at[j], q_all.at[me], q_sem.at[pairs], q_sem.at[my_pair],
            ctx=(j // group) * group + 2 * side + (j % group) // 2, head=j % 2,
        )

    def bulk(ref, send_sem, recv_sem):
        return remote(ref, ref, send_sem, recv_sem, ctx=me, head=1 - side)

    def kv_arrival(first, count, n):
        return bulk(kv_all.at[pl.ds(first, count)], kv_send.at[0], kv_recv.at[n])

    def st_copy(b):
        return remote(mix_ref.at[b], st_all.at[mine], st_sem.at[0], st_sem.at[1], ctx=b, head=row)

    def g_column(part, z):
        return remote(
            own_grad.at[part], gat_ref.at[part, mine], g_send.at[0], g_recv.at[part, 2 * plane + side],
            ctx=z * group + spot, head=row,
        )

    def g_pass(part, z, h, d):
        piece = gat_ref.at[part, z * group + 2 * column + h]
        arrival = g_hop.at[part, z] if (d == 1) == (h == 0) else g_final.at[0]
        return remote(
            piece, piece, g_send.at[d], arrival, ctx=plane * group + flip(spot, d), head=side
        )

    def g_forward(part, z):
        j = z * group + jnp.where(native, 2 - 2 * column, 2 * column + 1)
        piece = gat_ref.at[part, j]
        target = jnp.where(native, flip(spot, 2), flip(spot, 1))
        return remote(
            piece, piece, g_send.at[3], g_final.at[0], ctx=plane * group + target, head=side
        )

    def g_landing(part, j, n):
        return bulk(gat_ref.at[part, j], g_send.at[0], g_recv.at[part, n])

    def sq_copy(t):
        return remote(
            sq_own, sq_all.at[mine], sq_sem.at[0], sq_sem.at[1], ctx=t, head=row
        )

    def unless_own(b, body):
        @pl.when(jnp.logical_not(native & (b == me)))
        def _():
            body()

    rate = math.log2(math.e) / math.sqrt(width)
    lane = lax.broadcasted_iota(jnp.int32, (rows, 2 * features), 1)
    is_upper = lane < features
    row_half = lax.broadcasted_iota(jnp.int32, (2 * features, 2 * features), 0) < features
    col_half = lax.broadcasted_iota(jnp.int32, (2 * features, 2 * features), 1) < features
    halves = jnp.where(row_half == col_half, 1.0, 0.0).astype(bf16)
    square = (rows, rows)
    causal = lax.broadcasted_iota(jnp.int32, square, 1) <= lax.broadcasted_iota(jnp.int32, square, 0)
    for part, (fetch, raw) in enumerate(zip(fetches, (k_raw, v_raw))):
        fetch.wait()
        kvt_ref[:, part] = jnp.transpose(raw[...], (1, 0, 2))
    own_kv = pltpu.make_async_copy(kvt_ref.at[plane], kv_all.at[me], local_sem.at[0])

    @pl.when(native)
    def _():
        own_kv.start()

    pl.semaphore_wait(barrier, jnp.where(native, 3 * blocks // 2 - 1, 3 * blocks // 2))
    for d in range(planes):
        g = flip(plane, d)
        if d == 0:
            @pl.when(jnp.logical_not(native))
            def _():
                kv_land(g).start()
        else:
            kv_land(g).start()

    @pl.when(native)
    def _():
        w_copy().start()

    fetches[2].wait()
    qt_ref[...] = jnp.transpose(q_raw[...], (1, 0, 2))
    own_q = pltpu.make_async_copy(qt_ref.at[mine], q_all.at[me], local_sem.at[1])

    @pl.when(native)
    def _():
        own_q.start()
        own_kv.wait()

    def land(d):
        z = flip(plane, d)
        block = landed_block(z)
        unless_own(block, lambda: kv_arrival(block, 1, z).wait_recv())
        kv_across(z).start()
        kv_share(block, z).start()

    def cross(d):
        z = flip(plane, d)
        block = crossed_block(z)
        kv_arrival(block, 1, planes + z).wait_recv()
        kv_share(block, z).start()

    def load(part, i):
        if part == 0:
            return q_all[pl.ds(2 * i, 2)].reshape(rows, width)
        return kv_all[pl.ds(2 * i, 2), part - 1].reshape(rows, width)

    def either(less, body):
        for flag, count in ((native, less), (jnp.logical_not(native), 0)):
            @pl.when(flag)
            def _():
                body(count)

    def q_arrived(p):
        here = native & (p == my_pair)
        for flag, count in ((here, 3), (jnp.logical_not(here), 4)):
            @pl.when(flag)
            def _():
                bulk(q_all.at[pl.ds(0, count)], q_sem.at[pairs], q_sem.at[p]).wait_recv()

    def send_student(b):
        unless_own(b, lambda: st_copy(b).start())

        @pl.when(native & (b == me))
        def _():
            st_all[mine] = mix_ref[me]

    def send_grad(part):
        for d in range(planes):
            z = flip(plane, d)
            if d == 0:
                @pl.when(native)
                def _():
                    gat_ref[part, mine] = own_grad[part]

                @pl.when(jnp.logical_not(native))
                def _():
                    g_column(part, z).start()
            else:
                g_column(part, z).start()

    def relay_grad(part):
        @pl.when(native)
        def _():
            for z in range(planes):
                for h in range(2):
                    j = flip(plane, z) * group + 2 * column + h

                    @pl.when(j != mine)
                    def _():
                        g_landing(part, j, 2 * flip(plane, z) + h).wait_recv()

                    for d in range(1, group - 1):
                        g_pass(part, flip(plane, z), h, d).start()

    def hop_grad(part):
        for d in range(planes):
            z = flip(plane, d)
            bulk(gat_ref.at[part, z], g_send.at[0], g_hop.at[part, z]).wait_recv()
            g_forward(part, z).start()

    def key_side(pair):
        kv_arrival(group * pair, 2, 2 * planes + pair).wait_recv()
        steps_of = (2 * pair, 2 * pair + 1)
        ks, vs = ([load(part, i) for i in steps_of] for part in (1, 2))
        kfs = [
            half_softmax(mxu(cat([k, k, k], 1), wk_ref[...], NN), is_upper, halves) for k in ks
        ]
        for i, kf, v in zip(steps_of, kfs, vs):
            kfeat_ref[i] = kf
            for h in range(2):
                part = kf[h * length:(h + 1) * length]
                own_ref[2 * i + h] = wide_by_exact(part, v[h * length:(h + 1) * length], TN)
                sum_ref[2 * i + h] = jnp.sum(part, axis=0, keepdims=True)

    def push(n):
        p = (my_pair + pairs - n // group) % pairs
        j = jnp.where(side == 0, p, planes - 1 - p) * group + n % group

        @pl.when(jnp.logical_not(native & (j == mine)))
        def _():
            q_copy(j).start()

    def plane_keys(z):
        each(group // 4, lambda u: key_side(z * (group // 4) + u))

    def push_turns(first, last):
        each((last - first) * group, lambda n: push(first * group + n))

    land(0)
    push_turns(0, 1)
    @pl.when(native)
    def _():
        own_w.wait()

    @pl.when(jnp.logical_not(native))
    def _():
        w_copy().wait_recv()

    w = w_ref[...]
    wq, wk = w[:, :features], w[:, features:]
    wq_ref[...] = cat(split(cat([wq, -wq], 1), 3), 0)
    wk_ref[...] = cat(split(cat([wk, -wk], 1), 3), 0)
    gq_ref[...] = jnp.zeros_like(gq_ref)
    land(1)
    cross(0)
    land(2)
    cross(1)
    land(3)
    push_turns(1, 2)
    plane_keys(flip(plane, 0))
    cross(2)
    plane_keys(flip(plane, 1))
    cross(3)
    push_turns(2, pairs)
    plane_keys(flip(plane, 2))
    plane_keys(flip(plane, 3))

    @pl.when(native)
    def _():
        own_q.wait()

    for b in range(2):
        pre_ref[b] = jnp.zeros_like(pre_ref[b])
        pre_norm_ref[b] = jnp.zeros_like(pre_norm_ref[b])

    def prefix(b):
        pre_ref[b + 2] = pre_ref[b + 1] + own_ref[b]
        pre_norm_ref[b + 2] = pre_norm_ref[b + 1] + sum_ref[b]

    each(blocks - 2, prefix)

    def forward(turn, carry):
        p = (my_pair + turn) % pairs
        a, b = 2 * p, steps - 1 - 2 * p
        q_arrived(p)
        tokens = (a, b)
        qs = [load(0, i) for i in tokens]
        vs = [load(2, i) for i in tokens]
        wide_b = b // 2

        def pair_of(part, j):
            return cat([load(part, 2 * j), load(part, 2 * j + 1)], 0)

        def fold(x, combine):
            while x.shape[1] > length:
                half = x.shape[1] // 2
                x = combine(x[:, :half], x[:, half:])
            return x

        s = mxu(qs[0], load(1, a), NT) * rate
        s_a = jnp.where(causal, s, big_negative)
        near_ref[0] = s_a
        s = mxu(qs[1], pair_of(1, wide_b), NT) * rate
        s_b = [s[:, :rows], jnp.where(causal, s[:, rows:], big_negative)]
        near_ref[1], near_ref[2] = s_b
        peaks = [fold(s_a, jnp.maximum), fold(jnp.maximum(*s_b), jnp.maximum)]

        def far_tile(m):
            first = m < p
            return first, jnp.where(first, a, b), jnp.where(first, m, m - p)

        for m in range(middle):
            first, i, j = far_tile(m)
            s = mxu(load(0, i), pair_of(1, j), NT) * rate
            score_ref[m] = s
            top = fold(s, jnp.maximum)
            peaks = [
                jnp.maximum(peaks[0], jnp.where(first, top, big_negative)),
                jnp.maximum(peaks[1], jnp.where(first, big_negative, top)),
            ]
        tops = [jnp.max(x, axis=-1, keepdims=True) for x in peaks]

        weight = jnp.exp2(near_ref[0] - tops[0])
        sums = [fold(weight, jnp.add)]
        accs = [mxu(weight.astype(bf16), vs[0], NN)]
        weight = jnp.exp2(cat([near_ref[1], near_ref[2]], 1) - tops[1])
        sums.append(fold(weight, jnp.add))
        accs.append(mxu(weight.astype(bf16), pair_of(2, wide_b), NN))
        for m in range(middle):
            first, i, j = far_tile(m)
            weight = jnp.exp2(score_ref[m] - jnp.where(first, tops[0], tops[1]))
            part = fold(weight, jnp.add)
            prod = mxu(weight.astype(bf16), pair_of(2, j), NN)
            sums = [sums[0] + jnp.where(first, part, 0.0), sums[1] + jnp.where(first, 0.0, part)]
            accs = [accs[0] + jnp.where(first, prod, 0.0), accs[1] + jnp.where(first, 0.0, prod)]
        teachers = [
            acc / jnp.sum(total, axis=-1, keepdims=True) for acc, total in zip(accs, sums)
        ]

        def halves_of(f):
            return [cat([f(x, 0), f(x, 1)], 0) for x in range(2)]

        def cut(x, half):
            return x[half * length:(half + 1) * length]

        last_far = score_ref[jnp.maximum(p - 1, 0), :length, 3 * length:]
        prevs = [
            cat([jnp.where(p > 0, last_far, big_negative), near_ref[0, length:, :length]], 0),
            cat([near_ref[1, :length, length:], near_ref[2, length:, :length]], 0),
        ]
        owns = [
            cat([near_ref[k, :length, :length], near_ref[k, length:, length:]], 0) for k in (0, 2)
        ]
        win_maxs = [
            jnp.max(jnp.maximum(prev, own), axis=-1, keepdims=True)
            for prev, own in zip(prevs, owns)
        ]
        p_prevs = [jnp.exp2(x - top) for x, top in zip(prevs, win_maxs)]
        p_owns = [jnp.exp2(x - top) for x, top in zip(owns, win_maxs)]
        win_dens = [jnp.sum(x + y, axis=-1, keepdims=True) for x, y in zip(p_prevs, p_owns)]
        p_wins = [cat([x.astype(bf16), y.astype(bf16)], 1) for x, y in zip(p_prevs, p_owns)]
        v_befores = [kv_all[jnp.maximum(2 * i - 1, 0), 1] for i in tokens]
        v_wins = [
            (cat([before, v[:length]], 0), v) for before, v in zip(v_befores, vs)
        ]
        win_nums = halves_of(lambda x, h: mxu(cut(p_wins[x], h), v_wins[x][h], NN))

        qfs = [
            half_softmax(mxu(cat([q, q, q], 1), wq_ref[...], NN), is_upper, halves) for q in qs
        ]
        states = [[pre_ref[2 * i], pre_ref[2 * i + 1]] for i in tokens]
        norms = [
            cat(
                [
                    jnp.broadcast_to(pre_norm_ref[2 * i + h], (length, 2 * features))
                    for h in range(2)
                ],
                0,
            )
            for i in tokens
        ]
        decays = [jnp.exp2(-top) for top in win_maxs]
        fars = halves_of(lambda x, h: wide_by_rounded(cut(qfs[x], h), states[x][h], NN))
        dens = [
            win_den + decay * jnp.sum(qf * norm, axis=-1, keepdims=True)
            for win_den, decay, qf, norm in zip(win_dens, decays, qfs, norms)
        ]
        mixes = [
            (num + decay * far) / den
            for num, decay, far, den in zip(win_nums, decays, fars, dens)
        ]
        for i, mix in zip(tokens, mixes):
            mix_ref[pl.ds(2 * i, 2)] = mix.astype(bf16).reshape(2, length, width)
        @pl.when(turn < pairs - 1)
        def _():
            each(4, lambda u: send_student(pair_block(p, u)))

        mismatches = [mix - teacher for mix, teacher in zip(mixes, teachers)]
        g_nums = [x / den for x, den in zip(mismatches, dens)]
        g_dens = [
            -jnp.sum(x * mix, axis=-1, keepdims=True) / den
            for x, mix, den in zip(mismatches, mixes, dens)
        ]
        lifts = [decay * qf for decay, qf in zip(decays, qfs)]
        pulled_norms = [lift * g_den for lift, g_den in zip(lifts, g_dens)]
        for x, i in enumerate(tokens):
            for h in range(2):
                gstate_ref[2 * i + h] = wide_by_rounded(cut(lifts[x], h), cut(g_nums[x], h), TN)
                gnorm_ref[2 * i + h] = jnp.sum(cut(pulled_norms[x], h), axis=0, keepdims=True)
        pulled = halves_of(lambda x, h: wide_by_rounded(cut(g_nums[x], h), states[x][h], NT))
        g_qfs = [
            decay * (pull + norm * g_den)
            for decay, pull, norm, g_den in zip(decays, pulled, norms, g_dens)
        ]
        d_qs = [qf * (g - half_sum(qf * g, halves)) for qf, g in zip(qfs, g_qfs)]
        gq_ref[...] += wide_by_exact(d_qs[0], qs[0], TN) + wide_by_exact(d_qs[1], qs[1], TN)
        return carry

    lax.fori_loop(0, pairs, forward, 0)
    own_grad[0] = (gq_ref[:features] - gq_ref[features:]).astype(bf16)
    send_grad(0)

    for b in range(blocks - 2, 1, -1):
        gstate_ref[b] = gstate_ref[b] + gstate_ref[b + 1]
        gnorm_ref[b] = gnorm_ref[b] + gnorm_ref[b + 1]

    def backward(group_of):
        ks, vs, kfs = ([f(i) for i in group_of] for f in (lambda i: load(1, i), lambda i: load(2, i), lambda i: kfeat_ref[i]))
        g_kfs = [
            cat(
                [
                    mxu(v[h * length:(h + 1) * length], gstate_ref[2 * i + h + 2].astype(bf16), NT)
                    + gnorm_ref[2 * i + h + 2]
                    for h in range(2)
                ],
                0,
            )
            for i, v in zip(group_of, vs)
        ]
        d_ks = [kf * (g - half_sum(kf * g, halves)) for kf, g in zip(kfs, g_kfs)]
        return [wide_by_exact(d_k, k, TN) for d_k, k in zip(d_ks, ks)]

    gk = sum(backward(range(steps // 2)) + backward(range(steps // 2, steps - 1)))
    own_grad[1] = (gk[:features] - gk[features:]).astype(bf16)
    send_grad(1)
    square = own_grad[...].astype(f32).reshape(2 * features, width)
    sq_own[...] = jnp.sum(square * square, axis=0, keepdims=True)
    each(blocks, lambda n: unless_own((me + n) % blocks, lambda: sq_copy((me + n) % blocks).start()))

    @pl.when(native)
    def _():
        sq_all[mine] = sq_own[...]

    each(4, lambda u: send_student(pair_block((my_pair + pairs - 1) % pairs, u)))
    relay_grad(0)
    relay_grad(1)
    hop_grad(0)
    hop_grad(1)

    either(1, lambda n: bulk(st_all.at[pl.ds(0, blocks - n)], st_sem.at[0], st_sem.at[1]).wait_recv())
    st_turned[...] = jnp.transpose(st_all[...], (1, 0, 2))
    student_out = pltpu.make_async_copy(st_turned, student_hbm, out_sem.at[0])
    student_out.start()

    either(1, lambda n: bulk(sq_all.at[pl.ds(0, blocks - n)], sq_sem.at[0], sq_sem.at[1]).wait_recv())
    sq_ref[0] = jnp.sum(sq_all[...], axis=0)
    swap = remote(
        sq_ref.at[0], sq_ref.at[1], swap_sem.at[0], swap_sem.at[1], ctx=me, head=1 - side
    )
    swap.start()

    either(1, lambda n: bulk(qt_ref.at[pl.ds(0, blocks - n)], q_sem.at[pairs], q_sem.at[0]).wait_send())
    either(1, lambda n: bulk(mix_ref.at[pl.ds(0, blocks - n)], st_sem.at[0], st_sem.at[1]).wait_send())
    either(1, lambda n: bulk(sq_all.at[pl.ds(0, blocks - n)], sq_sem.at[0], sq_sem.at[1]).wait_send())
    either(1, lambda n: bulk(kvt_ref.at[pl.ds(0, planes - n)], kv_send.at[0], kv_recv.at[0]).wait_send())
    bulk(kv_all.at[pl.ds(0, planes)], kv_send.at[1], kv_recv.at[0]).wait_send()
    bulk(kv_all.at[pl.ds(0, 2 * planes)], kv_send.at[2], kv_recv.at[0]).wait_send()
    either(2, lambda n: bulk(gat_ref.at[0, pl.ds(0, 2 * planes - n)], g_send.at[0], g_final.at[0]).wait_send())

    @pl.when(native)
    def _():
        w_copy().wait_send()

    swap.wait()
    entries = 2 * blocks * width * 2 * features
    total = jnp.sum(sq_ref[0] + sq_ref[1], keepdims=True)
    scale_ref[...] = jnp.broadcast_to(1.0 / jnp.sqrt(total / entries + 1e-06), (8, width))
    scale_out = pltpu.make_async_copy(scale_ref, scale_hbm, out_sem.at[2])
    scale_out.start()

    @pl.when(native)
    def _():
        bulk(gat_ref.at[0, pl.ds(0, 2 * planes)], g_send.at[0], g_final.at[0]).wait_recv()

    @pl.when(jnp.logical_not(native))
    def _():
        bulk(gat_ref.at[:, pl.ds(0, 3 * planes)], g_send.at[0], g_final.at[0]).wait_recv()

    grad_out = pltpu.make_async_copy(gat_ref, grad_hbm, out_sem.at[1])
    grad_out.start()

    @pl.when(native)
    def _():
        for d in range(1, group - 1):
            bulk(gat_ref.at[0], g_send.at[d], g_final.at[0]).wait_send()

    bulk(gat_ref.at[0, pl.ds(0, 2 * planes)], g_send.at[3], g_final.at[0]).wait_send()
    student_out.wait()
    scale_out.wait()
    grad_out.wait()


def finish_kernel(
    student_hbm, grad_hbm, scale_hbm, student_out, update_out,
    st_ref, grad_ref, scale_ref, update_ref, in_sem, out_sem,
):
    parts, blocks, features, width = grad_ref.shape
    chunks = in_sem.shape[0] - 2
    each_len = blocks // chunks
    fetches = [
        pltpu.make_async_copy(
            grad_hbm.at[:, pl.ds(n * each_len, each_len)],
            grad_ref.at[:, pl.ds(n * each_len, each_len)], in_sem.at[n],
        )
        for n in range(chunks)
    ]
    scale_in = pltpu.make_async_copy(scale_hbm, scale_ref, in_sem.at[chunks])
    student_in = pltpu.make_async_copy(student_hbm, st_ref, in_sem.at[chunks + 1])
    scale_in.start()
    student_in.start()
    for fetch in fetches:
        fetch.start()
    scale_in.wait()
    scale = scale_ref[:1]
    stores = [pltpu.make_async_copy(st_ref, student_out, out_sem.at[chunks])]
    student_in.wait()
    stores[0].start()
    for n, fetch in enumerate(fetches):
        fetch.wait()
        for j in range(n * each_len, (n + 1) * each_len):
            piece = cat([grad_ref[0, j], grad_ref[1, j]], 0).astype(f32)
            update_ref[j] = piece.T * scale
        stores.append(
            pltpu.make_async_copy(
                update_ref.at[pl.ds(n * each_len, each_len)],
                update_out.at[pl.ds(n * each_len, each_len)], out_sem.at[n],
            )
        )
        stores[-1].start()
    for store in stores:
        store.wait()


def whole_head(queries, keys, values, w):
    length, blocks, width = queries.shape
    planes = keys.shape[1]
    group = blocks // planes
    double = w.shape[2]
    half = double // 2
    rows, steps = 2 * length, blocks // 2
    vmem, dma = pltpu.VMEM, pltpu.SemaphoreType.DMA
    hbm = pl.BlockSpec(memory_space=pltpu.MemorySpace.HBM)
    limit = 67_043_328
    student, grads, scale = pl.pallas_call(
        head_kernel,
        out_shape=(
            jax.ShapeDtypeStruct((length, blocks, width), bf16),
            jax.ShapeDtypeStruct((2, blocks, half, width), bf16),
            jax.ShapeDtypeStruct((8, width), f32),
        ),
        in_specs=[hbm] * 4,
        out_specs=(hbm,) * 3,
        scratch_shapes=[
            vmem((length, blocks, width), bf16),
            vmem((length, planes, width), bf16),
            vmem((length, planes, width), bf16),
            vmem((width, double), f32),
            vmem((blocks, length, width), bf16),
            vmem((planes, 2, length, width), bf16),
            vmem((blocks, length, width), bf16),
            vmem((blocks, 2, length, width), bf16),
            vmem((blocks, length, width), bf16),
            vmem((length, blocks, width), bf16),
            vmem((blocks, length, width), bf16),
            vmem((2, half, width), bf16),
            vmem((2, blocks, half, width), bf16),
            vmem((1, width), f32),
            vmem((blocks, 1, width), f32),
            vmem((2, 1, width), f32),
            vmem((8, width), f32),
            vmem((blocks, double, width), f32),
            vmem((blocks, 1, double), f32),
            vmem((blocks, double, width), f32),
            vmem((blocks, 1, double), f32),
            vmem((blocks // 4 - 1, rows, 2 * rows), f32),
            vmem((3, rows, rows), f32),
            vmem((steps, rows, double), f32),
            vmem((blocks, double, width), f32),
            vmem((blocks, 1, double), f32),
            vmem((3 * width, double), bf16),
            vmem((3 * width, double), bf16),
            vmem((double, width), f32),
            dma((blocks // 4 + 1,)),
            dma((3,)),
            dma((3 * planes,)),
            dma((3,)),
            dma((2,)),
            dma((group,)),
            dma((2, 2 * planes)),
            dma((2, planes)),
            dma((1,)),
            dma((2,)),
            dma((3,)),
            dma((1,)),
            dma((1,)),
            dma((3,)),
            dma((2,)),
        ],
        compiler_params=pltpu.CompilerParams(
            vmem_limit_bytes=limit, collective_id=0, has_side_effects=True
        ),
    )(queries, keys, values, w)
    chunks = 2
    return pl.pallas_call(
        finish_kernel,
        out_shape=(
            jax.ShapeDtypeStruct((length, blocks, width), bf16),
            jax.ShapeDtypeStruct((blocks, width, double), f32),
        ),
        in_specs=[hbm] * 3,
        out_specs=(hbm,) * 2,
        scratch_shapes=[
            vmem((length, blocks, width), bf16),
            vmem((2, blocks, half, width), bf16),
            vmem((8, width), f32),
            vmem((blocks, width, double), f32),
            dma((chunks + 2,)),
            dma((chunks + 1,)),
        ],
        compiler_params=pltpu.CompilerParams(vmem_limit_bytes=limit),
    )(student, grads, scale)


def head_shards(queries, keys, values, feature_weight):
    return whole_head(queries, keys, values, feature_weight)


def shards(queries, keys, values, feature_weight):
    count = lax.axis_size("ctx")
    width = queries.shape[2]
    fits = queries.shape[1] == count and count == 4 * keys.shape[1] and lax.axis_size("head") == 2 and count % 4 == 0 and keys.shape[1] == 4 and count * queries.shape[0] <= 4096
    fits = fits and queries.shape[1] // keys.shape[1] % 4 == 0 and queries.shape[0] == width and feature_weight.shape[2] == width
    body = head_shards if fits else general_shards
    return body(queries, keys, values, feature_weight)


def solution(mesh):
    return jax.shard_map(
        shards,
        mesh=mesh,
        in_specs=(
            P("ctx", "head", None),
            P("ctx", "head", None),
            P("ctx", "head", None),
            P("head", None, None),
        ),
        out_specs=(P("ctx", "head", None), P("head", None, None)),
        check_vma=False,
    )
```
